512 devices in a mesh: rows: 64 (over x_lo, z, core), blk: 8 (over x_hi, y).
Axes of the slice: x: 4 (x_hi: 2, x_lo: 2; x = x_hi * 2 + x_lo), y: 4, z: 16, core: 2. Of those that a mesh axis runs over, the one named last changes fastest.
Arguments:
- cov_blocks: bfloat16 [1024, 40, 128, 128], P(('rows', 'blk')), may hold values from -24 to 24
- col_index: int32 [1024, 40], P(('rows', 'blk')), may hold values from 0 to 1023, as said below
- block_count: int32 [1024], P(('rows', 'blk')), may hold values from 2 to 40, as said below
- probes: bfloat16 [131072, 512], P(('rows', 'blk')), may hold values from -60 to 60
Outputs:
- basis: float32 [131072, 512], P(('rows', 'blk'))
The draws below stay inside these ranges and needn't reach their ends.
Inputs may be any that keep to these rules, and one draw needn't show every extreme that they name: `col_index`: the live slots of block row i name distinct column blocks of zone i // 16 or of an adjacent zone; rows of the first and last zone have at most 32 live slots; every entry of a row is distinct. `block_count`: some block row uses all 40 slots in every draw.
All inputs are finite; a program needn't handle non-finite values.
Results may differ from the reference program's by a relative error of at most 0.0003.
Values may be sent and summed in bfloat16 or wider, within the bound.
A program may use at most 64 MiB of HBM per device.

```python
import math
import jax
import jax.numpy as jnp
from jax import lax

BLOCK = 128
K = 512
NNZ = 40
ZONE_BLK = 16
ZONES = 64
NB = 1024
NPTS = 131072


def draw_cov_blocks(key, part):
    value_key, rough_key = jax.random.split(jax.random.fold_in(key, 11))
    shape = (NB, NNZ, BLOCK, BLOCK)
    row_rough = jnp.exp(jax.random.uniform(rough_key, (NB, 1, BLOCK, 1)) * math.log(10.0))
    position = (jnp.arange(NB)[:, None] * BLOCK + jnp.arange(BLOCK)[None, :]).astype(jnp.float32) / (NB * BLOCK - 1)
    position = position.reshape(NB, 1, BLOCK, 1)
    trend_up = 1.0 + 2.0 * position
    values = jnp.clip(jax.random.normal(value_key, shape), -6.0, 6.0)
    scaled = values * trend_up * row_rough / math.sqrt(BLOCK * NNZ)
    return jnp.clip(scaled, -24.0, 24.0).astype(jnp.bfloat16)


def draw_probes(key, part):
    value_key, column_key = jax.random.split(jax.random.fold_in(key, 23))
    column_scale = jnp.exp(jax.random.uniform(column_key, (1, K)) * math.log(10.0))
    values = jnp.clip(jax.random.normal(value_key, (NPTS, K)), -6.0, 6.0)
    return (values * column_scale).astype(jnp.bfloat16)


def draw_col_index(key, part):
    spread = 3 * ZONE_BLK
    zone_of = jnp.arange(NB, dtype=jnp.int32) // ZONE_BLK
    window_base = (zone_of - 1) * ZONE_BLK
    offsets = jnp.arange(spread, dtype=jnp.int32)
    row_keys = jax.random.split(jax.random.fold_in(key, 37), NB)
    orders = jax.vmap(lambda row_key: jax.random.permutation(row_key, spread))(row_keys).astype(jnp.int32)
    target = window_base[:, None] + offsets[None, :]
    outside = ((target < 0) | (target >= NB)).astype(jnp.int32)
    region = jnp.broadcast_to(offsets[None, :] // ZONE_BLK, target.shape)
    keyed = jnp.where(outside == 1, spread + orders, orders)
    upper_least = jnp.min(jnp.where(region == 2, keyed, 4 * spread), axis=1, keepdims=True)
    lower_least = jnp.min(jnp.where(region == 0, keyed, 4 * spread), axis=1, keepdims=True)
    is_upper = ((region == 2) & (keyed == upper_least) & (outside == 0)).astype(jnp.int32)
    is_lower = ((region == 0) & (keyed == lower_least) & (outside == 0)).astype(jnp.int32)
    ranking = keyed + outside * 3 * spread - is_upper * 3 * spread - is_lower * 2 * spread
    picked = jnp.argsort(ranking, axis=1, stable=True)[:, :NNZ]
    chosen = jnp.take_along_axis(target, picked, axis=1)
    return (chosen % NB).astype(jnp.int32)


def draw_block_count(key, part):
    level_key, count_key, zone_key, row_key = jax.random.split(jax.random.fold_in(key, 41), 4)
    least = max(2, NNZ // 5)
    spread = NNZ - least
    zone_of = jnp.arange(NB, dtype=jnp.int32) // ZONE_BLK
    density = jax.random.randint(level_key, (ZONES,), 0, 4)
    row_density = density[zone_of]
    ceiling = spread * (row_density + 1) // 4
    counts = least + jax.random.randint(count_key, (NB,), 0, 1 << 20) % (ceiling + 1)
    at_edge = (zone_of == 0) | (zone_of == ZONES - 1)
    counts = jnp.where(at_edge, jnp.minimum(counts, 2 * ZONE_BLK), counts)
    picked_zone = jax.random.randint(zone_key, (), 1, ZONES - 1)
    picked_row = picked_zone * ZONE_BLK + jax.random.randint(row_key, (), 0, ZONE_BLK)
    counts = jnp.where(jnp.arange(NB, dtype=jnp.int32) == picked_row, NNZ, counts)
    return counts.astype(jnp.int32)


def setup_inputs(seed: int = 0) -> dict:
    seeds = jax.random.split(jax.random.key(seed), 5)
    return {
        "cov_blocks": draw_cov_blocks(jax.random.fold_in(seeds[4], 71), 0),
        "col_index": draw_col_index(jax.random.fold_in(seeds[4], 71), 0),
        "block_count": draw_block_count(jax.random.fold_in(seeds[4], 71), 0),
        "probes": draw_probes(jax.random.fold_in(seeds[4], 71), 0),
    }


def reference(cov_blocks, col_index, block_count, probes):
    probe_tiles = probes.reshape(NB, BLOCK, K)
    slot_ids = jnp.arange(NNZ, dtype=jnp.int32)

    def one_row(packed):
        blocks, columns, live_count = packed
        live_mask = (slot_ids < live_count).astype(jnp.float32)
        gathered = probe_tiles[columns].astype(jnp.float32)
        weighted = blocks.astype(jnp.float32) * live_mask[:, None, None]
        return jnp.einsum('sac,sck->ak', weighted, gathered, precision=lax.Precision.HIGHEST)
    images = lax.map(one_row, (cov_blocks, col_index, block_count)).reshape(NPTS, K)
    gram_matrix = lax.dot_general(images.astype(jnp.float32), images.astype(jnp.float32), (((0,), (0,)), ((), ())), precision=lax.Precision.HIGHEST, preferred_element_type=jnp.float32) / NPTS
    factor = jnp.linalg.cholesky(gram_matrix)
    return lax.linalg.triangular_solve(factor, images, left_side=False, lower=True, transpose_a=True)
```

```python
import functools
import jax
import jax.numpy as jnp
from jax import lax
from jax.experimental import pallas as pl
from jax.experimental.pallas import tpu as pltpu
from jax.sharding import PartitionSpec as P

MESH_ID = pl.DeviceIdType.MESH


def _ar_kernel(dims, g_ref, out_ref, rc, ry, rx, rzl, rzh, a1, a2, a3, a4, full, ssem, rsem):
    XL, Z, C, XH, Y = dims
    X = XL * XH
    ZH = Z // 2
    N = g_ref.shape[0]
    S1 = N // C
    S2 = S1 // Y
    S3 = S2 // X
    S4 = S3 // 2
    r = lax.axis_index("rows")
    b = lax.axis_index("blk")
    c = r % C
    z = (r // C) % Z
    xl = r // (C * Z)
    xh = b // Y
    y = b % Y
    x = xh * XL + xl
    zl = z % 2
    zh = z // 2

    def dev(c_, y_, x_, z_):
        return ((x_ % XL) * (Z * C) + z_ * C + c_, (x_ // XL) * Y + y_)

    core_peer = dev(1 - c, y, x, z)
    y_peers = [(y + k) % Y for k in range(1, Y)]
    x_peers = [(x + k) % X for k in range(1, X)]
    zl_peer = dev(c, y, x, zh * 2 + 1 - zl)
    zh_peers = [(zh + k) % ZH for k in range(1, ZH)]
    peers = [core_peer, zl_peer]
    peers += [dev(c, p, x, z) for p in y_peers]
    peers += [dev(c, y, p, z) for p in x_peers]
    peers += [dev(c, y, x, p * 2 + zl) for p in zh_peers]

    barrier = pltpu.get_barrier_semaphore()
    for p in peers:
        pl.semaphore_signal(barrier, inc=1, device_id=p, device_id_type=MESH_ID)
    pl.semaphore_wait(barrier, len(peers))

    o_core, o_y, o_x, o_zl, o_zh = 0, 1, 1 + Y, 1 + Y + X, 2 + Y + X
    o_agzl, o_agx, o_agy, o_agc = 2 + Y + X + ZH, 3 + Y + X + ZH, 3 + Y + 2 * X + ZH, 3 + 2 * Y + 2 * X + ZH

    def send(src, dst, sidx, ridx, peer):
        d = pltpu.make_async_remote_copy(
            src_ref=src, dst_ref=dst, send_sem=ssem.at[sidx], recv_sem=rsem.at[ridx],
            device_id=peer, device_id_type=MESH_ID)
        d.start()
        return d

    def wait_recv(src, dst, ridx, peer):
        pltpu.make_async_remote_copy(
            src_ref=src, dst_ref=dst, send_sem=ssem.at[0], recv_sem=rsem.at[ridx],
            device_id=peer, device_id_type=MESH_ID).wait_recv()

    def rows(start, size):
        return pl.ds(pl.multiple_of(start, 8), size)

    d = send(g_ref.at[rows((1 - c) * S1, S1)], rc, o_core, o_core, core_peer)
    wait_recv(g_ref.at[rows(c * S1, S1)], rc, o_core, core_peer)
    d.wait_send()
    a1[...] = g_ref[rows(c * S1, S1), :] + rc[...]

    ds = [send(a1.at[rows(p * S2, S2)], ry.at[y], o_y + k, o_y + y, dev(c, p, x, z))
          for k, p in enumerate(y_peers)]
    for k in range(1, Y):
        s = (y - k + Y) % Y
        wait_recv(a1.at[rows(0, S2)], ry.at[s], o_y + s, dev(c, s, x, z))
    for d in ds:
        d.wait_send()
    acc = a1[rows(y * S2, S2), :]
    for k in range(1, Y):
        acc = acc + ry[(y - k + Y) % Y]
    a2[...] = acc

    ds = [send(a2.at[rows(p * S3, S3)], rx.at[x], o_x + k, o_x + x, dev(c, y, p, z))
          for k, p in enumerate(x_peers)]
    for k in range(1, X):
        s = (x - k + X) % X
        wait_recv(a2.at[rows(0, S3)], rx.at[s], o_x + s, dev(c, y, s, z))
    for d in ds:
        d.wait_send()
    acc = a2[rows(x * S3, S3), :]
    for k in range(1, X):
        acc = acc + rx[(x - k + X) % X]
    a3[...] = acc

    d = send(a3.at[rows((1 - zl) * S4, S4)], rzl, o_zl, o_zl, zl_peer)
    wait_recv(a3.at[rows(zl * S4, S4)], rzl, o_zl, zl_peer)
    d.wait_send()
    a4[...] = a3[rows(zl * S4, S4), :] + rzl[...]

    ds = [send(a4, rzh.at[zh], o_zh + k, o_zh + zh, dev(c, y, x, p * 2 + zl))
          for k, p in enumerate(zh_peers)]
    rzh[zh] = a4[...]
    for k in range(1, ZH):
        s = (zh - k + ZH) % ZH
        wait_recv(a4, rzh.at[s], o_zh + s, dev(c, y, x, s * 2 + zl))
    for d in ds:
        d.wait_send()
    acc = rzh[0]
    for j in range(1, ZH):
        acc = acc + rzh[j]
    base = c * S1 + y * S2 + x * S3
    full[rows(base + zl * S4, S4), :] = acc

    mine = rows(base + zl * S4, S4)
    d = send(full.at[mine], full.at[mine], o_agzl, o_agzl, zl_peer)
    wait_recv(full.at[mine], full.at[rows(base + (1 - zl) * S4, S4)], o_agzl, zl_peer)
    d.wait_send()

    mine = rows(c * S1 + y * S2 + x * S3, S3)
    ds = [send(full.at[mine], full.at[mine], o_agx + k, o_agx + x, dev(c, y, p, z))
          for k, p in enumerate(x_peers)]
    for k in range(1, X):
        s = (x - k + X) % X
        wait_recv(full.at[mine], full.at[rows(c * S1 + y * S2 + s * S3, S3)], o_agx + s, dev(c, y, s, z))
    for d in ds:
        d.wait_send()

    mine = rows(c * S1 + y * S2, S2)
    ds = [send(full.at[mine], full.at[mine], o_agy + k, o_agy + y, dev(c, p, x, z))
          for k, p in enumerate(y_peers)]
    for k in range(1, Y):
        s = (y - k + Y) % Y
        wait_recv(full.at[mine], full.at[rows(c * S1 + s * S2, S2)], o_agy + s, dev(c, s, x, z))
    for d in ds:
        d.wait_send()

    mine = rows(c * S1, S1)
    d = send(full.at[mine], full.at[mine], o_agc, o_agc, core_peer)
    wait_recv(full.at[mine], full.at[rows((1 - c) * S1, S1)], o_agc, core_peer)
    d.wait_send()

    out_ref[...] = full[...]


def gram_allreduce(g, dims):
    XL, Z, C, XH, Y = dims
    X = XL * XH
    ZH = Z // 2
    N, M = g.shape
    S1 = N // C
    S2 = S1 // Y
    S3 = S2 // X
    S4 = S3 // 2
    nsem = 4 + 2 * Y + 2 * X + ZH
    vmem = pltpu.VMEM
    return pl.pallas_call(
        functools.partial(_ar_kernel, dims),
        out_shape=jax.ShapeDtypeStruct((N, M), jnp.float32),
        in_specs=[pl.BlockSpec(memory_space=vmem)],
        out_specs=pl.BlockSpec(memory_space=vmem),
        scratch_shapes=[
            vmem((S1, M), jnp.float32),
            vmem((Y, S2, M), jnp.float32),
            vmem((X, S3, M), jnp.float32),
            vmem((S4, M), jnp.float32),
            vmem((ZH, S4, M), jnp.float32),
            vmem((S1, M), jnp.float32),
            vmem((S2, M), jnp.float32),
            vmem((S3, M), jnp.float32),
            vmem((S4, M), jnp.float32),
            vmem((N, M), jnp.float32),
            pltpu.SemaphoreType.DMA((nsem,)),
            pltpu.SemaphoreType.DMA((nsem,)),
        ],
        compiler_params=pltpu.CompilerParams(collective_id=0, has_side_effects=True),
    )(g)


def extended(x, sides, width):
    for axis, dim in sides:
        devices, length = (lax.axis_size(axis), x.shape[dim])
        up = [(i, (i + 1) % devices) for i in range(devices - 1)]
        down = [(j, i) for i, j in up]
        last = lax.slice_in_dim(x, length - width, length, axis=dim)
        first = lax.slice_in_dim(x, 0, width, axis=dim)
        before = lax.ppermute(last, axis, up)
        after = lax.ppermute(first, axis, down)
        x = jnp.concatenate([before, x, after], axis=dim)
    return x


def _dims():
    rows, blk = lax.axis_size("rows"), lax.axis_size("blk")
    return (2, rows // 4, 2, 2, blk // 2)


def local(cov_blocks, col_index, block_count, probes):
    rows_here, slots, block, _ = cov_blocks.shape
    tile_rows = probes.shape[0]
    probe_cols = probes.shape[1]
    zone_blocks = rows_here * lax.axis_size("blk")
    zone_number = lax.axis_index("rows")
    relative = col_index - (zone_number - 1) * zone_blocks
    window_blocks = 3 * zone_blocks
    inside = (relative >= 0) & (relative < window_blocks)
    slot_ids = lax.broadcasted_iota(jnp.int32, (rows_here, slots), 1)
    live_mask = inside & (slot_ids < block_count[:, None])
    column_ids = jnp.arange(window_blocks, dtype=jnp.int32)
    hits = (relative[:, :, None] == column_ids[None, None, :]) & live_mask[:, :, None]
    selector = hits.astype(jnp.bfloat16)
    window_matrix = jnp.einsum(
        "lsp,lsac->lapc", selector, cov_blocks, preferred_element_type=jnp.float32
    )
    window_matrix = window_matrix.astype(jnp.bfloat16).reshape(
        rows_here * block, window_blocks * block
    )

    def add_columns(running, shard_rows, first_row):
        length = shard_rows.shape[0]
        columns = lax.dynamic_slice_in_dim(window_matrix, first_row, length, 1)
        return running + jnp.dot(columns, shard_rows, preferred_element_type=jnp.float32)

    zeros_out = jnp.zeros((tile_rows, probe_cols), jnp.float32)
    own_zone = lax.all_gather(probes, "blk", axis=0, tiled=True)
    zone_length = own_zone.shape[0]
    images = add_columns(zeros_out, own_zone, zone_length)
    near_zones = extended(own_zone, (("rows", 0),), zone_length)
    images = add_columns(images, lax.slice_in_dim(near_zones, 0, zone_length, axis=0), 0)
    images = add_columns(
        images,
        lax.slice_in_dim(near_zones, 2 * zone_length, 3 * zone_length, axis=0),
        2 * zone_length,
    )
    gram_local = lax.dot_general(
        images,
        images,
        (((0,), (0,)), ((), ())),
        precision=lax.Precision.HIGHEST,
        preferred_element_type=jnp.float32,
    )
    gram_total = gram_allreduce(gram_local, _dims())
    point_count = tile_rows * lax.axis_size("rows") * lax.axis_size("blk")
    gram_matrix = gram_total / point_count
    factor = jnp.linalg.cholesky(gram_matrix)
    return lax.linalg.triangular_solve(
        factor, images, left_side=False, lower=True, transpose_a=True
    )


def solution(mesh):
    return jax.shard_map(
        local,
        mesh=mesh,
        in_specs=(
            P(("rows", "blk"), None, None, None),
            P(("rows", "blk"), None),
            P(("rows", "blk")),
            P(("rows", "blk"), None),
        ),
        out_specs=P(("rows", "blk"), None),
        check_vma=False,
    )
```

```python
import functools
import jax
import jax.numpy as jnp
from jax import lax
from jax.experimental import pallas as pl
from jax.experimental.pallas import tpu as pltpu
from jax.sharding import PartitionSpec as P

MESH_ID = pl.DeviceIdType.MESH


def _ar_kernel(dims, g_ref, out_ref, rc, ry, rx, rzl, rzh, a1, a2, a3, a4, full, ssem, rsem):
    XL, Z, C, XH, Y = dims
    X = XL * XH
    ZH = Z // 2
    N = g_ref.shape[0]
    S1 = N // C
    S2 = S1 // Y
    S3 = S2 // X
    S4 = S3 // 2
    r = lax.axis_index("rows")
    b = lax.axis_index("blk")
    c = r % C
    z = (r // C) % Z
    xl = r // (C * Z)
    xh = b // Y
    y = b % Y
    x = xh * XL + xl
    zl = z % 2
    zh = z // 2

    def dev(c_, y_, x_, z_):
        return ((x_ % XL) * (Z * C) + z_ * C + c_, (x_ // XL) * Y + y_)

    core_peer = dev(1 - c, y, x, z)
    y_peers = [(y + k) % Y for k in range(1, Y)]
    x_peers = [(x + k) % X for k in range(1, X)]
    zl_peer = dev(c, y, x, zh * 2 + 1 - zl)
    zh_peers = [(zh + k) % ZH for k in range(1, ZH)]
    peers = [core_peer, zl_peer]
    peers += [dev(c, p, x, z) for p in y_peers]
    peers += [dev(c, y, p, z) for p in x_peers]
    peers += [dev(c, y, x, p * 2 + zl) for p in zh_peers]

    barrier = pltpu.get_barrier_semaphore()
    for p in peers:
        pl.semaphore_signal(barrier, inc=1, device_id=p, device_id_type=MESH_ID)
    pl.semaphore_wait(barrier, len(peers))

    o_core, o_y, o_x, o_zl, o_zh = 0, 1, 1 + Y, 1 + Y + X, 2 + Y + X
    o_agzl, o_agx, o_agy, o_agc = 2 + Y + X + ZH, 3 + Y + X + ZH, 3 + Y + 2 * X + ZH, 3 + 2 * Y + 2 * X + ZH

    def send(src, dst, sidx, ridx, peer):
        d = pltpu.make_async_remote_copy(
            src_ref=src, dst_ref=dst, send_sem=ssem.at[sidx], recv_sem=rsem.at[ridx],
            device_id=peer, device_id_type=MESH_ID)
        d.start()
        return d

    def wait_recv(src, dst, ridx, peer):
        pltpu.make_async_remote_copy(
            src_ref=src, dst_ref=dst, send_sem=ssem.at[0], recv_sem=rsem.at[ridx],
            device_id=peer, device_id_type=MESH_ID).wait_recv()

    def rows(start, size):
        return pl.ds(pl.multiple_of(start, 8), size)

    d = send(g_ref.at[rows((1 - c) * S1, S1)], rc, o_core, o_core, core_peer)
    wait_recv(g_ref.at[rows(c * S1, S1)], rc, o_core, core_peer)
    d.wait_send()
    a1[...] = g_ref[rows(c * S1, S1), :] + rc[...]

    ds = [send(a1.at[rows(p * S2, S2)], ry.at[y], o_y + k, o_y + y, dev(c, p, x, z))
          for k, p in enumerate(y_peers)]
    for k in range(1, Y):
        s = (y - k + Y) % Y
        wait_recv(a1.at[rows(0, S2)], ry.at[s], o_y + s, dev(c, s, x, z))
    for d in ds:
        d.wait_send()
    acc = a1[rows(y * S2, S2), :]
    for k in range(1, Y):
        acc = acc + ry[(y - k + Y) % Y]
    a2[...] = acc

    ds = [send(a2.at[rows(p * S3, S3)], rx.at[x], o_x + k, o_x + x, dev(c, y, p, z))
          for k, p in enumerate(x_peers)]
    for k in range(1, X):
        s = (x - k + X) % X
        wait_recv(a2.at[rows(0, S3)], rx.at[s], o_x + s, dev(c, y, s, z))
    for d in ds:
        d.wait_send()
    acc = a2[rows(x * S3, S3), :]
    for k in range(1, X):
        acc = acc + rx[(x - k + X) % X]
    a3[...] = acc

    d = send(a3.at[rows((1 - zl) * S4, S4)], rzl, o_zl, o_zl, zl_peer)
    wait_recv(a3.at[rows(zl * S4, S4)], rzl, o_zl, zl_peer)
    d.wait_send()
    a4[...] = a3[rows(zl * S4, S4), :] + rzl[...]

    ds = [send(a4, rzh.at[zh], o_zh + k, o_zh + zh, dev(c, y, x, p * 2 + zl))
          for k, p in enumerate(zh_peers)]
    rzh[zh] = a4[...]
    for k in range(1, ZH):
        s = (zh - k + ZH) % ZH
        wait_recv(a4, rzh.at[s], o_zh + s, dev(c, y, x, s * 2 + zl))
    for d in ds:
        d.wait_send()
    acc = rzh[0]
    for j in range(1, ZH):
        acc = acc + rzh[j]
    base = c * S1 + y * S2 + x * S3
    full[rows(base + zl * S4, S4), :] = acc

    mine = rows(base + zl * S4, S4)
    d = send(full.at[mine], full.at[mine], o_agzl, o_agzl, zl_peer)
    wait_recv(full.at[mine], full.at[rows(base + (1 - zl) * S4, S4)], o_agzl, zl_peer)
    d.wait_send()

    mine = rows(c * S1 + y * S2 + x * S3, S3)
    ds = [send(full.at[mine], full.at[mine], o_agx + k, o_agx + x, dev(c, y, p, z))
          for k, p in enumerate(x_peers)]
    for k in range(1, X):
        s = (x - k + X) % X
        wait_recv(full.at[mine], full.at[rows(c * S1 + y * S2 + s * S3, S3)], o_agx + s, dev(c, y, s, z))
    for d in ds:
        d.wait_send()

    mine = rows(c * S1 + y * S2, S2)
    ds = [send(full.at[mine], full.at[mine], o_agy + k, o_agy + y, dev(c, p, x, z))
          for k, p in enumerate(y_peers)]
    for k in range(1, Y):
        s = (y - k + Y) % Y
        wait_recv(full.at[mine], full.at[rows(c * S1 + s * S2, S2)], o_agy + s, dev(c, s, x, z))
    for d in ds:
        d.wait_send()

    mine = rows(c * S1, S1)
    d = send(full.at[mine], full.at[mine], o_agc, o_agc, core_peer)
    wait_recv(full.at[mine], full.at[rows((1 - c) * S1, S1)], o_agc, core_peer)
    d.wait_send()

    out_ref[...] = full[...]


def _zone_gather_kernel(nb, p_ref, out_ref, ssem, rsem, lsem):
    T = p_ref.shape[0]
    r = lax.axis_index("rows")
    b = lax.axis_index("blk")
    barrier = pltpu.get_barrier_semaphore()
    for k in range(1, nb):
        pl.semaphore_signal(barrier, inc=1, device_id=(r, (b + k) % nb), device_id_type=MESH_ID)
    pl.semaphore_wait(barrier, nb - 1)
    here = pl.ds(pl.multiple_of(b * T, 8), T)
    ds = []
    for k in range(1, nb):
        d = pltpu.make_async_remote_copy(
            src_ref=p_ref, dst_ref=out_ref.at[here], send_sem=ssem.at[k - 1], recv_sem=rsem.at[b],
            device_id=(r, (b + k) % nb), device_id_type=MESH_ID)
        d.start()
        ds.append(d)
    own = pltpu.make_async_copy(p_ref, out_ref.at[here], lsem.at[0])
    own.start()
    for k in range(1, nb):
        s = (b - k + nb) % nb
        pltpu.make_async_remote_copy(
            src_ref=p_ref, dst_ref=out_ref.at[pl.ds(pl.multiple_of(s * T, 8), T)], send_sem=ssem.at[0],
            recv_sem=rsem.at[s], device_id=(r, s), device_id_type=MESH_ID).wait_recv()
    for d in ds:
        d.wait_send()
    own.wait()


def zone_gather(p, nb):
    T, K = p.shape
    return pl.pallas_call(
        functools.partial(_zone_gather_kernel, nb),
        out_shape=jax.ShapeDtypeStruct((nb * T, K), p.dtype),
        in_specs=[pl.BlockSpec(memory_space=pl.ANY)],
        out_specs=pl.BlockSpec(memory_space=pl.ANY),
        scratch_shapes=[
            pltpu.SemaphoreType.DMA((nb - 1,)),
            pltpu.SemaphoreType.DMA((nb,)),
            pltpu.SemaphoreType.DMA((1,)),
        ],
        compiler_params=pltpu.CompilerParams(collective_id=1, has_side_effects=True),
    )(p)


def gram_allreduce(g, dims):
    XL, Z, C, XH, Y = dims
    X = XL * XH
    ZH = Z // 2
    N, M = g.shape
    S1 = N // C
    S2 = S1 // Y
    S3 = S2 // X
    S4 = S3 // 2
    nsem = 4 + 2 * Y + 2 * X + ZH
    vmem = pltpu.VMEM
    return pl.pallas_call(
        functools.partial(_ar_kernel, dims),
        out_shape=jax.ShapeDtypeStruct((N, M), jnp.float32),
        in_specs=[pl.BlockSpec(memory_space=vmem)],
        out_specs=pl.BlockSpec(memory_space=vmem),
        scratch_shapes=[
            vmem((S1, M), jnp.float32),
            vmem((Y, S2, M), jnp.float32),
            vmem((X, S3, M), jnp.float32),
            vmem((S4, M), jnp.float32),
            vmem((ZH, S4, M), jnp.float32),
            vmem((S1, M), jnp.float32),
            vmem((S2, M), jnp.float32),
            vmem((S3, M), jnp.float32),
            vmem((S4, M), jnp.float32),
            vmem((N, M), jnp.float32),
            pltpu.SemaphoreType.DMA((nsem,)),
            pltpu.SemaphoreType.DMA((nsem,)),
        ],
        compiler_params=pltpu.CompilerParams(collective_id=0, has_side_effects=True),
    )(g)


def extended(x, sides, width):
    for axis, dim in sides:
        devices, length = (lax.axis_size(axis), x.shape[dim])
        up = [(i, (i + 1) % devices) for i in range(devices - 1)]
        down = [(j, i) for i, j in up]
        last = lax.slice_in_dim(x, length - width, length, axis=dim)
        first = lax.slice_in_dim(x, 0, width, axis=dim)
        before = lax.ppermute(last, axis, up)
        after = lax.ppermute(first, axis, down)
        x = jnp.concatenate([before, x, after], axis=dim)
    return x


def _dims():
    rows, blk = lax.axis_size("rows"), lax.axis_size("blk")
    return (2, rows // 4, 2, 2, blk // 2)


def local(cov_blocks, col_index, block_count, probes):
    rows_here, slots, block, _ = cov_blocks.shape
    tile_rows = probes.shape[0]
    probe_cols = probes.shape[1]
    zone_blocks = rows_here * lax.axis_size("blk")
    zone_number = lax.axis_index("rows")
    relative = col_index - (zone_number - 1) * zone_blocks
    window_blocks = 3 * zone_blocks
    inside = (relative >= 0) & (relative < window_blocks)
    slot_ids = lax.broadcasted_iota(jnp.int32, (rows_here, slots), 1)
    live_mask = inside & (slot_ids < block_count[:, None])
    column_ids = jnp.arange(window_blocks, dtype=jnp.int32)
    hits = (relative[:, :, None] == column_ids[None, None, :]) & live_mask[:, :, None]
    selector = hits.astype(jnp.bfloat16)
    window_matrix = jnp.einsum(
        "lsp,lsac->lapc", selector, cov_blocks, preferred_element_type=jnp.float32
    )
    window_matrix = window_matrix.astype(jnp.bfloat16).reshape(
        rows_here * block, window_blocks * block
    )

    def add_columns(running, shard_rows, first_row):
        length = shard_rows.shape[0]
        columns = lax.dynamic_slice_in_dim(window_matrix, first_row, length, 1)
        return running + jnp.dot(columns, shard_rows, preferred_element_type=jnp.float32)

    zeros_out = jnp.zeros((tile_rows, probe_cols), jnp.float32)
    own_zone = zone_gather(probes, lax.axis_size("blk"))
    zone_length = own_zone.shape[0]
    images = add_columns(zeros_out, own_zone, zone_length)
    near_zones = extended(own_zone, (("rows", 0),), zone_length)
    images = add_columns(images, lax.slice_in_dim(near_zones, 0, zone_length, axis=0), 0)
    images = add_columns(
        images,
        lax.slice_in_dim(near_zones, 2 * zone_length, 3 * zone_length, axis=0),
        2 * zone_length,
    )
    gram_local = lax.dot_general(
        images,
        images,
        (((0,), (0,)), ((), ())),
        precision=lax.Precision.HIGHEST,
        preferred_element_type=jnp.float32,
    )
    gram_total = gram_allreduce(gram_local, _dims())
    point_count = tile_rows * lax.axis_size("rows") * lax.axis_size("blk")
    gram_matrix = gram_total / point_count
    factor = jnp.linalg.cholesky(gram_matrix)
    return lax.linalg.triangular_solve(
        factor, images, left_side=False, lower=True, transpose_a=True
    )


def solution(mesh):
    return jax.shard_map(
        local,
        mesh=mesh,
        in_specs=(
            P(("rows", "blk"), None, None, None),
            P(("rows", "blk"), None),
            P(("rows", "blk")),
            P(("rows", "blk"), None),
        ),
        out_specs=P(("rows", "blk"), None),
        check_vma=False,
    )
```

```python
import functools
import jax
import jax.numpy as jnp
from jax import lax
from jax.experimental import pallas as pl
from jax.experimental.pallas import tpu as pltpu
from jax.sharding import PartitionSpec as P

MESH_ID = pl.DeviceIdType.MESH


def _ar_kernel(dims, g_ref, out_ref, rc, ry, rx, rzl, rzh, a1, a2, a3, a4, full, ssem, rsem):
    XL, Z, C, XH, Y = dims
    X = XL * XH
    ZH = Z // 2
    N = g_ref.shape[0]
    S1 = N // C
    S2 = S1 // Y
    S3 = S2 // X
    S4 = S3 // 2
    r = lax.axis_index("rows")
    b = lax.axis_index("blk")
    c = r % C
    z = (r // C) % Z
    xl = r // (C * Z)
    xh = b // Y
    y = b % Y
    x = xh * XL + xl
    zl = z % 2
    zh = z // 2

    def dev(c_, y_, x_, z_):
        return ((x_ % XL) * (Z * C) + z_ * C + c_, (x_ // XL) * Y + y_)

    core_peer = dev(1 - c, y, x, z)
    y_peers = [(y + k) % Y for k in range(1, Y)]
    x_peers = [(x + k) % X for k in range(1, X)]
    zl_peer = dev(c, y, x, zh * 2 + 1 - zl)
    zh_peers = [(zh + k) % ZH for k in range(1, ZH)]
    peers = [core_peer, zl_peer]
    peers += [dev(c, p, x, z) for p in y_peers]
    peers += [dev(c, y, p, z) for p in x_peers]
    peers += [dev(c, y, x, p * 2 + zl) for p in zh_peers]

    barrier = pltpu.get_barrier_semaphore()
    for p in peers:
        pl.semaphore_signal(barrier, inc=1, device_id=p, device_id_type=MESH_ID)
    pl.semaphore_wait(barrier, len(peers))

    o_core, o_y, o_x, o_zl, o_zh = 0, 1, 1 + Y, 1 + Y + X, 2 + Y + X
    o_agzl, o_agx, o_agy, o_agc = 2 + Y + X + ZH, 3 + Y + X + ZH, 3 + Y + 2 * X + ZH, 3 + 2 * Y + 2 * X + ZH

    def send(src, dst, sidx, ridx, peer):
        d = pltpu.make_async_remote_copy(
            src_ref=src, dst_ref=dst, send_sem=ssem.at[sidx], recv_sem=rsem.at[ridx],
            device_id=peer, device_id_type=MESH_ID)
        d.start()
        return d

    def wait_recv(src, dst, ridx, peer):
        pltpu.make_async_remote_copy(
            src_ref=src, dst_ref=dst, send_sem=ssem.at[0], recv_sem=rsem.at[ridx],
            device_id=peer, device_id_type=MESH_ID).wait_recv()

    def rows(start, size):
        return pl.ds(pl.multiple_of(start, 8), size)

    d = send(g_ref.at[rows((1 - c) * S1, S1)], rc, o_core, o_core, core_peer)
    wait_recv(g_ref.at[rows(c * S1, S1)], rc, o_core, core_peer)
    d.wait_send()
    a1[...] = g_ref[rows(c * S1, S1), :] + rc[...]

    ds = [send(a1.at[rows(p * S2, S2)], ry.at[y], o_y + k, o_y + y, dev(c, p, x, z))
          for k, p in enumerate(y_peers)]
    for k in range(1, Y):
        s = (y - k + Y) % Y
        wait_recv(a1.at[rows(0, S2)], ry.at[s], o_y + s, dev(c, s, x, z))
    for d in ds:
        d.wait_send()
    acc = a1[rows(y * S2, S2), :]
    for k in range(1, Y):
        acc = acc + ry[(y - k + Y) % Y]
    a2[...] = acc

    ds = [send(a2.at[rows(p * S3, S3)], rx.at[x], o_x + k, o_x + x, dev(c, y, p, z))
          for k, p in enumerate(x_peers)]
    for k in range(1, X):
        s = (x - k + X) % X
        wait_recv(a2.at[rows(0, S3)], rx.at[s], o_x + s, dev(c, y, s, z))
    for d in ds:
        d.wait_send()
    acc = a2[rows(x * S3, S3), :]
    for k in range(1, X):
        acc = acc + rx[(x - k + X) % X]
    a3[...] = acc

    d = send(a3.at[rows((1 - zl) * S4, S4)], rzl, o_zl, o_zl, zl_peer)
    wait_recv(a3.at[rows(zl * S4, S4)], rzl, o_zl, zl_peer)
    d.wait_send()
    a4[...] = a3[rows(zl * S4, S4), :] + rzl[...]

    ds = [send(a4, rzh.at[zh], o_zh + k, o_zh + zh, dev(c, y, x, p * 2 + zl))
          for k, p in enumerate(zh_peers)]
    rzh[zh] = a4[...]
    for k in range(1, ZH):
        s = (zh - k + ZH) % ZH
        wait_recv(a4, rzh.at[s], o_zh + s, dev(c, y, x, s * 2 + zl))
    for d in ds:
        d.wait_send()
    acc = rzh[0]
    for j in range(1, ZH):
        acc = acc + rzh[j]
    base = c * S1 + y * S2 + x * S3
    full[rows(base + zl * S4, S4), :] = acc

    mine = rows(base + zl * S4, S4)
    d = send(full.at[mine], full.at[mine], o_agzl, o_agzl, zl_peer)
    wait_recv(full.at[mine], full.at[rows(base + (1 - zl) * S4, S4)], o_agzl, zl_peer)
    d.wait_send()

    mine = rows(c * S1 + y * S2 + x * S3, S3)
    ds = [send(full.at[mine], full.at[mine], o_agx + k, o_agx + x, dev(c, y, p, z))
          for k, p in enumerate(x_peers)]
    for k in range(1, X):
        s = (x - k + X) % X
        wait_recv(full.at[mine], full.at[rows(c * S1 + y * S2 + s * S3, S3)], o_agx + s, dev(c, y, s, z))
    for d in ds:
        d.wait_send()

    mine = rows(c * S1 + y * S2, S2)
    ds = [send(full.at[mine], full.at[mine], o_agy + k, o_agy + y, dev(c, p, x, z))
          for k, p in enumerate(y_peers)]
    for k in range(1, Y):
        s = (y - k + Y) % Y
        wait_recv(full.at[mine], full.at[rows(c * S1 + s * S2, S2)], o_agy + s, dev(c, s, x, z))
    for d in ds:
        d.wait_send()

    mine = rows(c * S1, S1)
    d = send(full.at[mine], full.at[mine], o_agc, o_agc, core_peer)
    wait_recv(full.at[mine], full.at[rows((1 - c) * S1, S1)], o_agc, core_peer)
    d.wait_send()

    out_ref[...] = full[...]


def _zone_gather_kernel(nb, p_ref, out_ref, ssem, rsem, lsem):
    T = p_ref.shape[0]
    r = lax.axis_index("rows")
    b = lax.axis_index("blk")
    barrier = pltpu.get_barrier_semaphore()
    for k in range(1, nb):
        pl.semaphore_signal(barrier, inc=1, device_id=(r, (b + k) % nb), device_id_type=MESH_ID)
    pl.semaphore_wait(barrier, nb - 1)
    here = pl.ds(pl.multiple_of(b * T, 8), T)
    ds = []
    for k in range(1, nb):
        d = pltpu.make_async_remote_copy(
            src_ref=p_ref, dst_ref=out_ref.at[here], send_sem=ssem.at[k - 1], recv_sem=rsem.at[b],
            device_id=(r, (b + k) % nb), device_id_type=MESH_ID)
        d.start()
        ds.append(d)
    own = pltpu.make_async_copy(p_ref, out_ref.at[here], lsem.at[0])
    own.start()
    for k in range(1, nb):
        s = (b - k + nb) % nb
        pltpu.make_async_remote_copy(
            src_ref=p_ref, dst_ref=out_ref.at[pl.ds(pl.multiple_of(s * T, 8), T)], send_sem=ssem.at[0],
            recv_sem=rsem.at[s], device_id=(r, s), device_id_type=MESH_ID).wait_recv()
    for d in ds:
        d.wait_send()
    own.wait()


def zone_gather(p, nb):
    T, K = p.shape
    return pl.pallas_call(
        functools.partial(_zone_gather_kernel, nb),
        out_shape=jax.ShapeDtypeStruct((nb * T, K), p.dtype),
        in_specs=[pl.BlockSpec(memory_space=pl.ANY)],
        out_specs=pl.BlockSpec(memory_space=pl.ANY),
        scratch_shapes=[
            pltpu.SemaphoreType.DMA((nb - 1,)),
            pltpu.SemaphoreType.DMA((nb,)),
            pltpu.SemaphoreType.DMA((1,)),
        ],
        compiler_params=pltpu.CompilerParams(collective_id=1, has_side_effects=True),
    )(p)


HI = lax.Precision.HIGHEST


def _mm(a, b):
    return jnp.dot(a, b, precision=HI, preferred_element_type=jnp.float32)


def _mm_t(a, b):
    return lax.dot_general(a, b, (((1,), (1,)), ((), ())), precision=HI, preferred_element_type=jnp.float32)


def _chol_inv_kernel(g_ref, m_ref, a_ref, d_ref, b_ref, l_ref):
    n = g_ref.shape[0]
    t = d_ref.shape[0]
    nb = n // t
    a_ref[...] = g_ref[...]
    m_ref[...] = jnp.zeros_like(m_ref)
    lane = lax.broadcasted_iota(jnp.int32, (1, t), 1)
    lane2 = lax.broadcasted_iota(jnp.int32, (t, t), 1)
    sub = lax.broadcasted_iota(jnp.int32, (t, 1), 0)
    eye = (lax.broadcasted_iota(jnp.int32, (t, t), 0) == lane2).astype(jnp.float32)

    def step(j, carry):
        row = d_ref[pl.ds(j, 1), :]
        piv2 = jnp.sum(jnp.where(lane == j, row, 0.0), axis=1, keepdims=True)
        inv = 1.0 / jnp.sqrt(piv2)
        dmat = d_ref[...]
        colfull = jnp.sum(jnp.where(lane2 == j, dmat, 0.0), axis=1, keepdims=True)
        col = jnp.where(sub >= j, colfull * inv, 0.0)
        lrow = jnp.where(lane >= j, row * inv, 0.0)
        d_ref[...] = dmat - col * lrow
        brow = b_ref[pl.ds(j, 1), :] * inv
        bmat = b_ref[...]
        b_ref[...] = bmat - jnp.where(sub > j, col, 0.0) * brow
        b_ref[pl.ds(j, 1), :] = brow
        return carry

    for k in range(nb):
        lo = k * t
        d_ref[...] = a_ref[lo:lo + t, lo:lo + t]
        b_ref[...] = eye
        lax.fori_loop(0, t, step, 0)
        m_ref[lo:lo + t, lo:lo + t] = b_ref[...]
        if k < nb - 1:
            hi = lo + t
            panel = _mm_t(a_ref[hi:, lo:lo + t], b_ref[...])
            l_ref[hi:, lo:lo + t] = panel
            a_ref[hi:, hi:] = a_ref[hi:, hi:] - _mm_t(panel, panel)
    for dist in range(1, nb):
        for i in range(dist, nb):
            j = i - dist
            acc = None
            for k in range(j, i):
                term = _mm(l_ref[i * t:(i + 1) * t, k * t:(k + 1) * t], m_ref[k * t:(k + 1) * t, j * t:(j + 1) * t])
                acc = term if acc is None else acc + term
            m_ref[i * t:(i + 1) * t, j * t:(j + 1) * t] = -_mm(m_ref[i * t:(i + 1) * t, i * t:(i + 1) * t], acc)


def chol_inverse(g, t=128):
    n = g.shape[0]
    vmem = pltpu.VMEM
    return pl.pallas_call(
        _chol_inv_kernel,
        out_shape=jax.ShapeDtypeStruct((n, n), jnp.float32),
        in_specs=[pl.BlockSpec(memory_space=vmem)],
        out_specs=pl.BlockSpec(memory_space=vmem),
        scratch_shapes=[
            vmem((n, n), jnp.float32),
            vmem((t, t), jnp.float32),
            vmem((t, t), jnp.float32),
            vmem((n, n), jnp.float32),
        ],
    )(g)


def gram_allreduce(g, dims):
    XL, Z, C, XH, Y = dims
    X = XL * XH
    ZH = Z // 2
    N, M = g.shape
    S1 = N // C
    S2 = S1 // Y
    S3 = S2 // X
    S4 = S3 // 2
    nsem = 4 + 2 * Y + 2 * X + ZH
    vmem = pltpu.VMEM
    return pl.pallas_call(
        functools.partial(_ar_kernel, dims),
        out_shape=jax.ShapeDtypeStruct((N, M), jnp.float32),
        in_specs=[pl.BlockSpec(memory_space=vmem)],
        out_specs=pl.BlockSpec(memory_space=vmem),
        scratch_shapes=[
            vmem((S1, M), jnp.float32),
            vmem((Y, S2, M), jnp.float32),
            vmem((X, S3, M), jnp.float32),
            vmem((S4, M), jnp.float32),
            vmem((ZH, S4, M), jnp.float32),
            vmem((S1, M), jnp.float32),
            vmem((S2, M), jnp.float32),
            vmem((S3, M), jnp.float32),
            vmem((S4, M), jnp.float32),
            vmem((N, M), jnp.float32),
            pltpu.SemaphoreType.DMA((nsem,)),
            pltpu.SemaphoreType.DMA((nsem,)),
        ],
        compiler_params=pltpu.CompilerParams(collective_id=0, has_side_effects=True),
    )(g)


def extended(x, sides, width):
    for axis, dim in sides:
        devices, length = (lax.axis_size(axis), x.shape[dim])
        up = [(i, (i + 1) % devices) for i in range(devices - 1)]
        down = [(j, i) for i, j in up]
        last = lax.slice_in_dim(x, length - width, length, axis=dim)
        first = lax.slice_in_dim(x, 0, width, axis=dim)
        before = lax.ppermute(last, axis, up)
        after = lax.ppermute(first, axis, down)
        x = jnp.concatenate([before, x, after], axis=dim)
    return x


def _dims():
    rows, blk = lax.axis_size("rows"), lax.axis_size("blk")
    return (2, rows // 4, 2, 2, blk // 2)


def local(cov_blocks, col_index, block_count, probes):
    rows_here, slots, block, _ = cov_blocks.shape
    tile_rows = probes.shape[0]
    probe_cols = probes.shape[1]
    zone_blocks = rows_here * lax.axis_size("blk")
    zone_number = lax.axis_index("rows")
    relative = col_index - (zone_number - 1) * zone_blocks
    window_blocks = 3 * zone_blocks
    inside = (relative >= 0) & (relative < window_blocks)
    slot_ids = lax.broadcasted_iota(jnp.int32, (rows_here, slots), 1)
    live_mask = inside & (slot_ids < block_count[:, None])
    column_ids = jnp.arange(window_blocks, dtype=jnp.int32)
    hits = (relative[:, :, None] == column_ids[None, None, :]) & live_mask[:, :, None]
    selector = hits.astype(jnp.bfloat16)
    window_matrix = jnp.einsum(
        "lsp,lsac->lapc", selector, cov_blocks, preferred_element_type=jnp.float32
    )
    window_matrix = window_matrix.astype(jnp.bfloat16).reshape(
        rows_here * block, window_blocks * block
    )

    def add_columns(running, shard_rows, first_row):
        length = shard_rows.shape[0]
        columns = lax.dynamic_slice_in_dim(window_matrix, first_row, length, 1)
        return running + jnp.dot(columns, shard_rows, preferred_element_type=jnp.float32)

    zeros_out = jnp.zeros((tile_rows, probe_cols), jnp.float32)
    own_zone = zone_gather(probes, lax.axis_size("blk"))
    zone_length = own_zone.shape[0]
    images = add_columns(zeros_out, own_zone, zone_length)
    near_zones = extended(own_zone, (("rows", 0),), zone_length)
    images = add_columns(images, lax.slice_in_dim(near_zones, 0, zone_length, axis=0), 0)
    images = add_columns(
        images,
        lax.slice_in_dim(near_zones, 2 * zone_length, 3 * zone_length, axis=0),
        2 * zone_length,
    )
    gram_local = lax.dot_general(
        images,
        images,
        (((0,), (0,)), ((), ())),
        precision=lax.Precision.HIGHEST,
        preferred_element_type=jnp.float32,
    )
    gram_total = gram_allreduce(gram_local, _dims())
    point_count = tile_rows * lax.axis_size("rows") * lax.axis_size("blk")
    gram_matrix = gram_total / point_count
    symmetric = (gram_matrix + gram_matrix.T) / 2
    factor_inverse = chol_inverse(symmetric)
    return _mm_t(images, factor_inverse)


def solution(mesh):
    return jax.shard_map(
        local,
        mesh=mesh,
        in_specs=(
            P(("rows", "blk"), None, None, None),
            P(("rows", "blk"), None),
            P(("rows", "blk")),
            P(("rows", "blk"), None),
        ),
        out_specs=P(("rows", "blk"), None),
        check_vma=False,
    )
```

```python
import functools
import jax
import jax.numpy as jnp
from jax import lax
from jax.experimental import pallas as pl
from jax.experimental.pallas import tpu as pltpu
from jax.sharding import PartitionSpec as P

MESH_ID = pl.DeviceIdType.MESH


def _ar_kernel(dims, g_ref, out_ref, rc, ry, rx, rzl, rzh, a1, a2, a3, a4, full, ssem, rsem):
    XL, Z, C, XH, Y = dims
    X = XL * XH
    ZH = Z // 2
    N = g_ref.shape[0]
    S1 = N // C
    S2 = S1 // Y
    S3 = S2 // X
    S4 = S3 // 2
    r = lax.axis_index("rows")
    b = lax.axis_index("blk")
    c = r % C
    z = (r // C) % Z
    xl = r // (C * Z)
    xh = b // Y
    y = b % Y
    x = xh * XL + xl
    zl = z % 2
    zh = z // 2

    def dev(c_, y_, x_, z_):
        return ((x_ % XL) * (Z * C) + z_ * C + c_, (x_ // XL) * Y + y_)

    core_peer = dev(1 - c, y, x, z)
    y_peers = [(y + k) % Y for k in range(1, Y)]
    x_peers = [(x + k) % X for k in range(1, X)]
    zl_peer = dev(c, y, x, zh * 2 + 1 - zl)
    zh_peers = [(zh + k) % ZH for k in range(1, ZH)]
    peers = [core_peer, zl_peer]
    peers += [dev(c, p, x, z) for p in y_peers]
    peers += [dev(c, y, p, z) for p in x_peers]
    peers += [dev(c, y, x, p * 2 + zl) for p in zh_peers]

    barrier = pltpu.get_barrier_semaphore()
    for p in peers:
        pl.semaphore_signal(barrier, inc=1, device_id=p, device_id_type=MESH_ID)
    pl.semaphore_wait(barrier, len(peers))

    o_core, o_y, o_x, o_zl, o_zh = 0, 1, 1 + Y, 1 + Y + X, 2 + Y + X
    o_agzl, o_agx, o_agy, o_agc = 2 + Y + X + ZH, 3 + Y + X + ZH, 3 + Y + 2 * X + ZH, 3 + 2 * Y + 2 * X + ZH

    def send(src, dst, sidx, ridx, peer):
        d = pltpu.make_async_remote_copy(
            src_ref=src, dst_ref=dst, send_sem=ssem.at[sidx], recv_sem=rsem.at[ridx],
            device_id=peer, device_id_type=MESH_ID)
        d.start()
        return d

    def wait_recv(src, dst, ridx, peer):
        pltpu.make_async_remote_copy(
            src_ref=src, dst_ref=dst, send_sem=ssem.at[0], recv_sem=rsem.at[ridx],
            device_id=peer, device_id_type=MESH_ID).wait_recv()

    def rows(start, size):
        return pl.ds(pl.multiple_of(start, 8), size)

    d = send(g_ref.at[rows((1 - c) * S1, S1)], rc, o_core, o_core, core_peer)
    wait_recv(g_ref.at[rows(c * S1, S1)], rc, o_core, core_peer)
    d.wait_send()
    a1[...] = g_ref[rows(c * S1, S1), :] + rc[...]

    ds = [send(a1.at[rows(p * S2, S2)], ry.at[y], o_y + k, o_y + y, dev(c, p, x, z))
          for k, p in enumerate(y_peers)]
    for k in range(1, Y):
        s = (y - k + Y) % Y
        wait_recv(a1.at[rows(0, S2)], ry.at[s], o_y + s, dev(c, s, x, z))
    for d in ds:
        d.wait_send()
    acc = a1[rows(y * S2, S2), :]
    for k in range(1, Y):
        acc = acc + ry[(y - k + Y) % Y]
    a2[...] = acc

    ds = [send(a2.at[rows(p * S3, S3)], rx.at[x], o_x + k, o_x + x, dev(c, y, p, z))
          for k, p in enumerate(x_peers)]
    for k in range(1, X):
        s = (x - k + X) % X
        wait_recv(a2.at[rows(0, S3)], rx.at[s], o_x + s, dev(c, y, s, z))
    for d in ds:
        d.wait_send()
    acc = a2[rows(x * S3, S3), :]
    for k in range(1, X):
        acc = acc + rx[(x - k + X) % X]
    a3[...] = acc

    d = send(a3.at[rows((1 - zl) * S4, S4)], rzl, o_zl, o_zl, zl_peer)
    wait_recv(a3.at[rows(zl * S4, S4)], rzl, o_zl, zl_peer)
    d.wait_send()
    a4[...] = a3[rows(zl * S4, S4), :] + rzl[...]

    ds = [send(a4, rzh.at[zh], o_zh + k, o_zh + zh, dev(c, y, x, p * 2 + zl))
          for k, p in enumerate(zh_peers)]
    rzh[zh] = a4[...]
    for k in range(1, ZH):
        s = (zh - k + ZH) % ZH
        wait_recv(a4, rzh.at[s], o_zh + s, dev(c, y, x, s * 2 + zl))
    for d in ds:
        d.wait_send()
    acc = rzh[0]
    for j in range(1, ZH):
        acc = acc + rzh[j]
    base = c * S1 + y * S2 + x * S3
    full[rows(base + zl * S4, S4), :] = acc

    mine = rows(base + zl * S4, S4)
    d = send(full.at[mine], full.at[mine], o_agzl, o_agzl, zl_peer)
    wait_recv(full.at[mine], full.at[rows(base + (1 - zl) * S4, S4)], o_agzl, zl_peer)
    d.wait_send()

    mine = rows(c * S1 + y * S2 + x * S3, S3)
    ds = [send(full.at[mine], full.at[mine], o_agx + k, o_agx + x, dev(c, y, p, z))
          for k, p in enumerate(x_peers)]
    for k in range(1, X):
        s = (x - k + X) % X
        wait_recv(full.at[mine], full.at[rows(c * S1 + y * S2 + s * S3, S3)], o_agx + s, dev(c, y, s, z))
    for d in ds:
        d.wait_send()

    mine = rows(c * S1 + y * S2, S2)
    ds = [send(full.at[mine], full.at[mine], o_agy + k, o_agy + y, dev(c, p, x, z))
          for k, p in enumerate(y_peers)]
    for k in range(1, Y):
        s = (y - k + Y) % Y
        wait_recv(full.at[mine], full.at[rows(c * S1 + s * S2, S2)], o_agy + s, dev(c, s, x, z))
    for d in ds:
        d.wait_send()

    mine = rows(c * S1, S1)
    d = send(full.at[mine], full.at[mine], o_agc, o_agc, core_peer)
    wait_recv(full.at[mine], full.at[rows((1 - c) * S1, S1)], o_agc, core_peer)
    d.wait_send()

    out_ref[...] = full[...]


def _zone_gather_kernel(nb, p_ref, out_ref, ssem, rsem, lsem):
    T = p_ref.shape[0]
    r = lax.axis_index("rows")
    b = lax.axis_index("blk")
    barrier = pltpu.get_barrier_semaphore()
    for k in range(1, nb):
        pl.semaphore_signal(barrier, inc=1, device_id=(r, (b + k) % nb), device_id_type=MESH_ID)
    pl.semaphore_wait(barrier, nb - 1)
    here = pl.ds(pl.multiple_of(b * T, 8), T)
    ds = []
    for k in range(1, nb):
        d = pltpu.make_async_remote_copy(
            src_ref=p_ref, dst_ref=out_ref.at[here], send_sem=ssem.at[k - 1], recv_sem=rsem.at[b],
            device_id=(r, (b + k) % nb), device_id_type=MESH_ID)
        d.start()
        ds.append(d)
    own = pltpu.make_async_copy(p_ref, out_ref.at[here], lsem.at[0])
    own.start()
    for k in range(1, nb):
        s = (b - k + nb) % nb
        pltpu.make_async_remote_copy(
            src_ref=p_ref, dst_ref=out_ref.at[pl.ds(pl.multiple_of(s * T, 8), T)], send_sem=ssem.at[0],
            recv_sem=rsem.at[s], device_id=(r, s), device_id_type=MESH_ID).wait_recv()
    for d in ds:
        d.wait_send()
    own.wait()


def zone_gather(p, nb):
    T, K = p.shape
    return pl.pallas_call(
        functools.partial(_zone_gather_kernel, nb),
        out_shape=jax.ShapeDtypeStruct((nb * T, K), p.dtype),
        in_specs=[pl.BlockSpec(memory_space=pl.ANY)],
        out_specs=pl.BlockSpec(memory_space=pl.ANY),
        scratch_shapes=[
            pltpu.SemaphoreType.DMA((nb - 1,)),
            pltpu.SemaphoreType.DMA((nb,)),
            pltpu.SemaphoreType.DMA((1,)),
        ],
        compiler_params=pltpu.CompilerParams(collective_id=1, has_side_effects=True),
    )(p)


HI = lax.Precision.HIGHEST


def _mm(a, b):
    return jnp.dot(a, b, precision=HI, preferred_element_type=jnp.float32)


def _mm_t(a, b):
    return lax.dot_general(a, b, (((1,), (1,)), ((), ())), precision=HI, preferred_element_type=jnp.float32)


def _chol_inv_kernel(count, g_ref, m_ref, a_ref, d_ref, b_ref, l_ref):
    n = g_ref.shape[0]
    t = d_ref.shape[0]
    nb = n // t
    gram = g_ref[...] / count
    a_ref[...] = (gram + gram.T) / 2
    m_ref[...] = jnp.zeros_like(m_ref)
    lane = lax.broadcasted_iota(jnp.int32, (1, t), 1)
    lane2 = lax.broadcasted_iota(jnp.int32, (t, t), 1)
    sub = lax.broadcasted_iota(jnp.int32, (t, 1), 0)
    eye = (lax.broadcasted_iota(jnp.int32, (t, t), 0) == lane2).astype(jnp.float32)

    def step(j, carry):
        row = d_ref[pl.ds(j, 1), :]
        piv2 = jnp.sum(jnp.where(lane == j, row, 0.0), axis=1, keepdims=True)
        inv = 1.0 / jnp.sqrt(piv2)
        dmat = d_ref[...]
        colfull = jnp.sum(jnp.where(lane2 == j, dmat, 0.0), axis=1, keepdims=True)
        col = jnp.where(sub >= j, colfull * inv, 0.0)
        lrow = jnp.where(lane >= j, row * inv, 0.0)
        d_ref[...] = dmat - col * lrow
        brow = b_ref[pl.ds(j, 1), :] * inv
        bmat = b_ref[...]
        b_ref[...] = bmat - jnp.where(sub > j, col, 0.0) * brow
        b_ref[pl.ds(j, 1), :] = brow
        return carry

    for k in range(nb):
        lo = k * t
        d_ref[...] = a_ref[lo:lo + t, lo:lo + t]
        b_ref[...] = eye
        lax.fori_loop(0, t, step, 0, unroll=4)
        m_ref[lo:lo + t, lo:lo + t] = b_ref[...]
        if k < nb - 1:
            hi = lo + t
            panel = _mm_t(a_ref[hi:, lo:lo + t], b_ref[...])
            l_ref[hi:, lo:lo + t] = panel
            a_ref[hi:, hi:] = a_ref[hi:, hi:] - _mm_t(panel, panel)
    for dist in range(1, nb):
        for i in range(dist, nb):
            j = i - dist
            acc = None
            for k in range(j, i):
                term = _mm(l_ref[i * t:(i + 1) * t, k * t:(k + 1) * t], m_ref[k * t:(k + 1) * t, j * t:(j + 1) * t])
                acc = term if acc is None else acc + term
            m_ref[i * t:(i + 1) * t, j * t:(j + 1) * t] = -_mm(m_ref[i * t:(i + 1) * t, i * t:(i + 1) * t], acc)


def chol_inverse(g, count, t=128):
    n = g.shape[0]
    vmem = pltpu.VMEM
    return pl.pallas_call(
        functools.partial(_chol_inv_kernel, count),
        out_shape=jax.ShapeDtypeStruct((n, n), jnp.float32),
        in_specs=[pl.BlockSpec(memory_space=vmem)],
        out_specs=pl.BlockSpec(memory_space=vmem),
        scratch_shapes=[
            vmem((n, n), jnp.float32),
            vmem((t, t), jnp.float32),
            vmem((t, t), jnp.float32),
            vmem((n, n), jnp.float32),
        ],
    )(g)


def gram_allreduce(g, dims):
    XL, Z, C, XH, Y = dims
    X = XL * XH
    ZH = Z // 2
    N, M = g.shape
    S1 = N // C
    S2 = S1 // Y
    S3 = S2 // X
    S4 = S3 // 2
    nsem = 4 + 2 * Y + 2 * X + ZH
    vmem = pltpu.VMEM
    return pl.pallas_call(
        functools.partial(_ar_kernel, dims),
        out_shape=jax.ShapeDtypeStruct((N, M), jnp.float32),
        in_specs=[pl.BlockSpec(memory_space=vmem)],
        out_specs=pl.BlockSpec(memory_space=vmem),
        scratch_shapes=[
            vmem((S1, M), jnp.float32),
            vmem((Y, S2, M), jnp.float32),
            vmem((X, S3, M), jnp.float32),
            vmem((S4, M), jnp.float32),
            vmem((ZH, S4, M), jnp.float32),
            vmem((S1, M), jnp.float32),
            vmem((S2, M), jnp.float32),
            vmem((S3, M), jnp.float32),
            vmem((S4, M), jnp.float32),
            vmem((N, M), jnp.float32),
            pltpu.SemaphoreType.DMA((nsem,)),
            pltpu.SemaphoreType.DMA((nsem,)),
        ],
        compiler_params=pltpu.CompilerParams(collective_id=0, has_side_effects=True),
    )(g)


def extended(x, sides, width):
    for axis, dim in sides:
        devices, length = (lax.axis_size(axis), x.shape[dim])
        up = [(i, (i + 1) % devices) for i in range(devices - 1)]
        down = [(j, i) for i, j in up]
        last = lax.slice_in_dim(x, length - width, length, axis=dim)
        first = lax.slice_in_dim(x, 0, width, axis=dim)
        before = lax.ppermute(last, axis, up)
        after = lax.ppermute(first, axis, down)
        x = jnp.concatenate([before, x, after], axis=dim)
    return x


def _dims():
    rows, blk = lax.axis_size("rows"), lax.axis_size("blk")
    return (2, rows // 4, 2, 2, blk // 2)


def local(cov_blocks, col_index, block_count, probes):
    rows_here, slots, block, _ = cov_blocks.shape
    tile_rows = probes.shape[0]
    probe_cols = probes.shape[1]
    zone_blocks = rows_here * lax.axis_size("blk")
    zone_number = lax.axis_index("rows")
    relative = col_index - (zone_number - 1) * zone_blocks
    window_blocks = 3 * zone_blocks
    inside = (relative >= 0) & (relative < window_blocks)
    slot_ids = lax.broadcasted_iota(jnp.int32, (rows_here, slots), 1)
    live_mask = inside & (slot_ids < block_count[:, None])
    column_ids = jnp.arange(window_blocks, dtype=jnp.int32)
    hits = (relative[:, :, None] == column_ids[None, None, :]) & live_mask[:, :, None]
    selector = hits.astype(jnp.bfloat16)
    window_matrix = jnp.einsum(
        "lsp,lsac->lapc", selector, cov_blocks, preferred_element_type=jnp.float32
    )
    window_matrix = window_matrix.astype(jnp.bfloat16).reshape(
        rows_here * block, window_blocks * block
    )

    def add_columns(running, shard_rows, first_row):
        length = shard_rows.shape[0]
        columns = lax.dynamic_slice_in_dim(window_matrix, first_row, length, 1)
        return running + jnp.dot(columns, shard_rows, preferred_element_type=jnp.float32)

    zeros_out = jnp.zeros((tile_rows, probe_cols), jnp.float32)
    own_zone = zone_gather(probes, lax.axis_size("blk"))
    zone_length = own_zone.shape[0]
    images = add_columns(zeros_out, own_zone, zone_length)
    near_zones = extended(own_zone, (("rows", 0),), zone_length)
    images = add_columns(images, lax.slice_in_dim(near_zones, 0, zone_length, axis=0), 0)
    images = add_columns(
        images,
        lax.slice_in_dim(near_zones, 2 * zone_length, 3 * zone_length, axis=0),
        2 * zone_length,
    )
    gram_local = lax.dot_general(
        images,
        images,
        (((0,), (0,)), ((), ())),
        precision=lax.Precision.HIGHEST,
        preferred_element_type=jnp.float32,
    )
    gram_total = gram_allreduce(gram_local, _dims())
    point_count = tile_rows * lax.axis_size("rows") * lax.axis_size("blk")
    factor_inverse = chol_inverse(gram_total, float(point_count))
    return _mm_t(images, factor_inverse)


def solution(mesh):
    return jax.shard_map(
        local,
        mesh=mesh,
        in_specs=(
            P(("rows", "blk"), None, None, None),
            P(("rows", "blk"), None),
            P(("rows", "blk")),
            P(("rows", "blk"), None),
        ),
        out_specs=P(("rows", "blk"), None),
        check_vma=False,
    )
```

```python
import functools
import jax
import jax.numpy as jnp
from jax import lax
from jax.experimental import pallas as pl
from jax.experimental.pallas import tpu as pltpu
from jax.sharding import PartitionSpec as P

MESH_ID = pl.DeviceIdType.MESH


def _ar_kernel(dims, g_ref, out_ref, rc, ry, rx, rzl, rzh, a1, a2, a3, a4, full, ssem, rsem):
    XL, Z, C, XH, Y = dims
    X = XL * XH
    ZH = Z // 2
    N = g_ref.shape[0]
    S1 = N // C
    S2 = S1 // Y
    S3 = S2 // X
    S4 = S3 // 2
    r = lax.axis_index("rows")
    b = lax.axis_index("blk")
    c = r % C
    z = (r // C) % Z
    xl = r // (C * Z)
    xh = b // Y
    y = b % Y
    x = xh * XL + xl
    zl = z % 2
    zh = z // 2

    def dev(c_, y_, x_, z_):
        return ((x_ % XL) * (Z * C) + z_ * C + c_, (x_ // XL) * Y + y_)

    core_peer = dev(1 - c, y, x, z)
    y_peers = [(y + k) % Y for k in range(1, Y)]
    x_peers = [(x + k) % X for k in range(1, X)]
    zl_peer = dev(c, y, x, zh * 2 + 1 - zl)
    zh_peers = [(zh + k) % ZH for k in range(1, ZH)]
    peers = [core_peer, zl_peer]
    peers += [dev(c, p, x, z) for p in y_peers]
    peers += [dev(c, y, p, z) for p in x_peers]
    peers += [dev(c, y, x, p * 2 + zl) for p in zh_peers]

    barrier = pltpu.get_barrier_semaphore()
    for p in peers:
        pl.semaphore_signal(barrier, inc=1, device_id=p, device_id_type=MESH_ID)
    pl.semaphore_wait(barrier, len(peers))

    o_core, o_y, o_x, o_zl, o_zh = 0, 1, 1 + Y, 1 + Y + X, 2 + Y + X
    o_agzl, o_agx, o_agy, o_agc = 2 + Y + X + ZH, 3 + Y + X + ZH, 3 + Y + 2 * X + ZH, 3 + 2 * Y + 2 * X + ZH

    def send(src, dst, sidx, ridx, peer):
        d = pltpu.make_async_remote_copy(
            src_ref=src, dst_ref=dst, send_sem=ssem.at[sidx], recv_sem=rsem.at[ridx],
            device_id=peer, device_id_type=MESH_ID)
        d.start()
        return d

    def wait_recv(src, dst, ridx, peer):
        pltpu.make_async_remote_copy(
            src_ref=src, dst_ref=dst, send_sem=ssem.at[0], recv_sem=rsem.at[ridx],
            device_id=peer, device_id_type=MESH_ID).wait_recv()

    def rows(start, size):
        return pl.ds(pl.multiple_of(start, 8), size)

    d = send(g_ref.at[rows((1 - c) * S1, S1)], rc, o_core, o_core, core_peer)
    wait_recv(g_ref.at[rows(c * S1, S1)], rc, o_core, core_peer)
    d.wait_send()
    a1[...] = g_ref[rows(c * S1, S1), :] + rc[...]

    ds = [send(a1.at[rows(p * S2, S2)], ry.at[y], o_y + k, o_y + y, dev(c, p, x, z))
          for k, p in enumerate(y_peers)]
    for k in range(1, Y):
        s = (y - k + Y) % Y
        wait_recv(a1.at[rows(0, S2)], ry.at[s], o_y + s, dev(c, s, x, z))
    for d in ds:
        d.wait_send()
    acc = a1[rows(y * S2, S2), :]
    for k in range(1, Y):
        acc = acc + ry[(y - k + Y) % Y]
    a2[...] = acc

    ds = [send(a2.at[rows(p * S3, S3)], rx.at[x], o_x + k, o_x + x, dev(c, y, p, z))
          for k, p in enumerate(x_peers)]
    for k in range(1, X):
        s = (x - k + X) % X
        wait_recv(a2.at[rows(0, S3)], rx.at[s], o_x + s, dev(c, y, s, z))
    for d in ds:
        d.wait_send()
    acc = a2[rows(x * S3, S3), :]
    for k in range(1, X):
        acc = acc + rx[(x - k + X) % X]
    a3[...] = acc

    d = send(a3.at[rows((1 - zl) * S4, S4)], rzl, o_zl, o_zl, zl_peer)
    wait_recv(a3.at[rows(zl * S4, S4)], rzl, o_zl, zl_peer)
    d.wait_send()
    a4[...] = a3[rows(zl * S4, S4), :] + rzl[...]

    ds = [send(a4, rzh.at[zh], o_zh + k, o_zh + zh, dev(c, y, x, p * 2 + zl))
          for k, p in enumerate(zh_peers)]
    rzh[zh] = a4[...]
    for k in range(1, ZH):
        s = (zh - k + ZH) % ZH
        wait_recv(a4, rzh.at[s], o_zh + s, dev(c, y, x, s * 2 + zl))
    for d in ds:
        d.wait_send()
    acc = rzh[0]
    for j in range(1, ZH):
        acc = acc + rzh[j]
    base = c * S1 + y * S2 + x * S3
    full[rows(base + zl * S4, S4), :] = acc

    mine = rows(base + zl * S4, S4)
    d = send(full.at[mine], full.at[mine], o_agzl, o_agzl, zl_peer)
    wait_recv(full.at[mine], full.at[rows(base + (1 - zl) * S4, S4)], o_agzl, zl_peer)
    d.wait_send()

    mine = rows(c * S1 + y * S2 + x * S3, S3)
    ds = [send(full.at[mine], full.at[mine], o_agx + k, o_agx + x, dev(c, y, p, z))
          for k, p in enumerate(x_peers)]
    for k in range(1, X):
        s = (x - k + X) % X
        wait_recv(full.at[mine], full.at[rows(c * S1 + y * S2 + s * S3, S3)], o_agx + s, dev(c, y, s, z))
    for d in ds:
        d.wait_send()

    mine = rows(c * S1 + y * S2, S2)
    ds = [send(full.at[mine], full.at[mine], o_agy + k, o_agy + y, dev(c, p, x, z))
          for k, p in enumerate(y_peers)]
    for k in range(1, Y):
        s = (y - k + Y) % Y
        wait_recv(full.at[mine], full.at[rows(c * S1 + s * S2, S2)], o_agy + s, dev(c, s, x, z))
    for d in ds:
        d.wait_send()

    mine = rows(c * S1, S1)
    d = send(full.at[mine], full.at[mine], o_agc, o_agc, core_peer)
    wait_recv(full.at[mine], full.at[rows((1 - c) * S1, S1)], o_agc, core_peer)
    d.wait_send()

    out_ref[...] = full[...]


def _zone_gather_kernel(nb, p_ref, out_ref, ssem, rsem, lsem):
    T = p_ref.shape[0]
    r = lax.axis_index("rows")
    b = lax.axis_index("blk")
    barrier = pltpu.get_barrier_semaphore()
    for k in range(1, nb):
        pl.semaphore_signal(barrier, inc=1, device_id=(r, (b + k) % nb), device_id_type=MESH_ID)
    pl.semaphore_wait(barrier, nb - 1)
    here = pl.ds(pl.multiple_of(b * T, 8), T)
    ds = []
    for k in range(1, nb):
        d = pltpu.make_async_remote_copy(
            src_ref=p_ref, dst_ref=out_ref.at[here], send_sem=ssem.at[k - 1], recv_sem=rsem.at[b],
            device_id=(r, (b + k) % nb), device_id_type=MESH_ID)
        d.start()
        ds.append(d)
    own = pltpu.make_async_copy(p_ref, out_ref.at[here], lsem.at[0])
    own.start()
    for k in range(1, nb):
        s = (b - k + nb) % nb
        pltpu.make_async_remote_copy(
            src_ref=p_ref, dst_ref=out_ref.at[pl.ds(pl.multiple_of(s * T, 8), T)], send_sem=ssem.at[0],
            recv_sem=rsem.at[s], device_id=(r, s), device_id_type=MESH_ID).wait_recv()
    for d in ds:
        d.wait_send()
    own.wait()


def zone_gather(p, nb):
    T, K = p.shape
    return pl.pallas_call(
        functools.partial(_zone_gather_kernel, nb),
        out_shape=jax.ShapeDtypeStruct((nb * T, K), p.dtype),
        in_specs=[pl.BlockSpec(memory_space=pl.ANY)],
        out_specs=pl.BlockSpec(memory_space=pl.ANY),
        scratch_shapes=[
            pltpu.SemaphoreType.DMA((nb - 1,)),
            pltpu.SemaphoreType.DMA((nb,)),
            pltpu.SemaphoreType.DMA((1,)),
        ],
        compiler_params=pltpu.CompilerParams(collective_id=1, has_side_effects=True),
    )(p)


HI = lax.Precision.HIGHEST


def _mm(a, b):
    return jnp.dot(a, b, precision=HI, preferred_element_type=jnp.float32)


def _mm_t(a, b):
    return lax.dot_general(a, b, (((1,), (1,)), ((), ())), precision=HI, preferred_element_type=jnp.float32)


def _chol_inv_kernel(count, g_ref, m_ref, a_ref, d_ref, b_ref, l_ref):
    n = g_ref.shape[0]
    t = d_ref.shape[0]
    nb = n // t
    gram = g_ref[...] / count
    a_ref[...] = (gram + gram.T) / 2
    m_ref[...] = jnp.zeros_like(m_ref)
    lane = lax.broadcasted_iota(jnp.int32, (1, t), 1)
    eye = (lax.broadcasted_iota(jnp.int32, (t, t), 0) == lax.broadcasted_iota(jnp.int32, (t, t), 1)).astype(jnp.float32)

    def step(r0, j, carry):
        lane2 = lax.broadcasted_iota(jnp.int32, (t - r0, t), 1)
        sub = lax.broadcasted_iota(jnp.int32, (t - r0, 1), 0) + r0
        row = d_ref[pl.ds(j, 1), :]
        piv2 = jnp.sum(jnp.where(lane == j, row, 0.0), axis=1, keepdims=True)
        inv = 1.0 / jnp.sqrt(piv2)
        dmat = d_ref[r0:, :]
        colfull = jnp.sum(jnp.where(lane2 == j, dmat, 0.0), axis=1, keepdims=True)
        col = jnp.where(sub >= j, colfull * inv, 0.0)
        lrow = jnp.where(lane >= j, row * inv, 0.0)
        d_ref[r0:, :] = dmat - col * lrow
        brow = b_ref[pl.ds(j, 1), :] * inv
        bmat = b_ref[r0:, :]
        b_ref[r0:, :] = bmat - jnp.where(sub > j, col, 0.0) * brow
        b_ref[pl.ds(j, 1), :] = brow
        return carry

    for k in range(nb):
        lo = k * t
        d_ref[...] = a_ref[lo:lo + t, lo:lo + t]
        b_ref[...] = eye
        for r0 in range(0, t, 8):
            lax.fori_loop(r0, r0 + 8, functools.partial(step, r0), 0)
        m_ref[lo:lo + t, lo:lo + t] = b_ref[...]
        if k < nb - 1:
            hi = lo + t
            panel = _mm_t(a_ref[hi:, lo:lo + t], b_ref[...])
            l_ref[hi:, lo:lo + t] = panel
            a_ref[hi:, hi:] = a_ref[hi:, hi:] - _mm_t(panel, panel)
    for dist in range(1, nb):
        for i in range(dist, nb):
            j = i - dist
            acc = None
            for k in range(j, i):
                term = _mm(l_ref[i * t:(i + 1) * t, k * t:(k + 1) * t], m_ref[k * t:(k + 1) * t, j * t:(j + 1) * t])
                acc = term if acc is None else acc + term
            m_ref[i * t:(i + 1) * t, j * t:(j + 1) * t] = -_mm(m_ref[i * t:(i + 1) * t, i * t:(i + 1) * t], acc)


def chol_inverse(g, count, t=128):
    n = g.shape[0]
    vmem = pltpu.VMEM
    return pl.pallas_call(
        functools.partial(_chol_inv_kernel, count),
        out_shape=jax.ShapeDtypeStruct((n, n), jnp.float32),
        in_specs=[pl.BlockSpec(memory_space=vmem)],
        out_specs=pl.BlockSpec(memory_space=vmem),
        scratch_shapes=[
            vmem((n, n), jnp.float32),
            vmem((t, t), jnp.float32),
            vmem((t, t), jnp.float32),
            vmem((n, n), jnp.float32),
        ],
    )(g)


def gram_allreduce(g, dims):
    XL, Z, C, XH, Y = dims
    X = XL * XH
    ZH = Z // 2
    N, M = g.shape
    S1 = N // C
    S2 = S1 // Y
    S3 = S2 // X
    S4 = S3 // 2
    nsem = 4 + 2 * Y + 2 * X + ZH
    vmem = pltpu.VMEM
    return pl.pallas_call(
        functools.partial(_ar_kernel, dims),
        out_shape=jax.ShapeDtypeStruct((N, M), jnp.float32),
        in_specs=[pl.BlockSpec(memory_space=vmem)],
        out_specs=pl.BlockSpec(memory_space=vmem),
        scratch_shapes=[
            vmem((S1, M), jnp.float32),
            vmem((Y, S2, M), jnp.float32),
            vmem((X, S3, M), jnp.float32),
            vmem((S4, M), jnp.float32),
            vmem((ZH, S4, M), jnp.float32),
            vmem((S1, M), jnp.float32),
            vmem((S2, M), jnp.float32),
            vmem((S3, M), jnp.float32),
            vmem((S4, M), jnp.float32),
            vmem((N, M), jnp.float32),
            pltpu.SemaphoreType.DMA((nsem,)),
            pltpu.SemaphoreType.DMA((nsem,)),
        ],
        compiler_params=pltpu.CompilerParams(collective_id=0, has_side_effects=True),
    )(g)


def extended(x, sides, width):
    for axis, dim in sides:
        devices, length = (lax.axis_size(axis), x.shape[dim])
        up = [(i, (i + 1) % devices) for i in range(devices - 1)]
        down = [(j, i) for i, j in up]
        last = lax.slice_in_dim(x, length - width, length, axis=dim)
        first = lax.slice_in_dim(x, 0, width, axis=dim)
        before = lax.ppermute(last, axis, up)
        after = lax.ppermute(first, axis, down)
        x = jnp.concatenate([before, x, after], axis=dim)
    return x


def _dims():
    rows, blk = lax.axis_size("rows"), lax.axis_size("blk")
    return (2, rows // 4, 2, 2, blk // 2)


def local(cov_blocks, col_index, block_count, probes):
    rows_here, slots, block, _ = cov_blocks.shape
    tile_rows = probes.shape[0]
    probe_cols = probes.shape[1]
    zone_blocks = rows_here * lax.axis_size("blk")
    zone_number = lax.axis_index("rows")
    relative = col_index - (zone_number - 1) * zone_blocks
    window_blocks = 3 * zone_blocks
    inside = (relative >= 0) & (relative < window_blocks)
    slot_ids = lax.broadcasted_iota(jnp.int32, (rows_here, slots), 1)
    live_mask = inside & (slot_ids < block_count[:, None])
    column_ids = jnp.arange(window_blocks, dtype=jnp.int32)
    hits = (relative[:, :, None] == column_ids[None, None, :]) & live_mask[:, :, None]
    selector = hits.astype(jnp.bfloat16)
    window_matrix = jnp.einsum(
        "lsp,lsac->lapc", selector, cov_blocks, preferred_element_type=jnp.float32
    )
    window_matrix = window_matrix.astype(jnp.bfloat16).reshape(
        rows_here * block, window_blocks * block
    )

    def add_columns(running, shard_rows, first_row):
        length = shard_rows.shape[0]
        columns = lax.dynamic_slice_in_dim(window_matrix, first_row, length, 1)
        return running + jnp.dot(columns, shard_rows, preferred_element_type=jnp.float32)

    zeros_out = jnp.zeros((tile_rows, probe_cols), jnp.float32)
    own_zone = zone_gather(probes, lax.axis_size("blk"))
    zone_length = own_zone.shape[0]
    images = add_columns(zeros_out, own_zone, zone_length)
    near_zones = extended(own_zone, (("rows", 0),), zone_length)
    images = add_columns(images, lax.slice_in_dim(near_zones, 0, zone_length, axis=0), 0)
    images = add_columns(
        images,
        lax.slice_in_dim(near_zones, 2 * zone_length, 3 * zone_length, axis=0),
        2 * zone_length,
    )
    gram_local = lax.dot_general(
        images,
        images,
        (((0,), (0,)), ((), ())),
        precision=lax.Precision.HIGHEST,
        preferred_element_type=jnp.float32,
    )
    gram_total = gram_allreduce(gram_local, _dims())
    point_count = tile_rows * lax.axis_size("rows") * lax.axis_size("blk")
    factor_inverse = chol_inverse(gram_total, float(point_count))
    return _mm_t(images, factor_inverse)


def solution(mesh):
    return jax.shard_map(
        local,
        mesh=mesh,
        in_specs=(
            P(("rows", "blk"), None, None, None),
            P(("rows", "blk"), None),
            P(("rows", "blk")),
            P(("rows", "blk"), None),
        ),
        out_specs=P(("rows", "blk"), None),
        check_vma=False,
    )
```

```python
import functools
import jax
import jax.numpy as jnp
from jax import lax
from jax.experimental import pallas as pl
from jax.experimental.pallas import tpu as pltpu
from jax.sharding import PartitionSpec as P

MESH_ID = pl.DeviceIdType.MESH


def _ar_kernel(dims, g_ref, out_ref, rc, ry, rx, rzl, rzh, a1, a2, a3, a4, full, ssem, rsem):
    XL, Z, C, XH, Y = dims
    X = XL * XH
    ZH = Z // 2
    N = g_ref.shape[0]
    S1 = N // C
    S2 = S1 // Y
    S3 = S2 // X
    S4 = S3 // 2
    r = lax.axis_index("rows")
    b = lax.axis_index("blk")
    c = r % C
    z = (r // C) % Z
    xl = r // (C * Z)
    xh = b // Y
    y = b % Y
    x = xh * XL + xl
    zl = z % 2
    zh = z // 2

    def dev(c_, y_, x_, z_):
        return ((x_ % XL) * (Z * C) + z_ * C + c_, (x_ // XL) * Y + y_)

    core_peer = dev(1 - c, y, x, z)
    y_peers = [(y + k) % Y for k in range(1, Y)]
    x_peers = [(x + k) % X for k in range(1, X)]
    zl_peer = dev(c, y, x, zh * 2 + 1 - zl)
    zh_peers = [(zh + k) % ZH for k in range(1, ZH)]
    peers = [core_peer, zl_peer]
    peers += [dev(c, p, x, z) for p in y_peers]
    peers += [dev(c, y, p, z) for p in x_peers]
    peers += [dev(c, y, x, p * 2 + zl) for p in zh_peers]

    barrier = pltpu.get_barrier_semaphore()
    for p in peers:
        pl.semaphore_signal(barrier, inc=1, device_id=p, device_id_type=MESH_ID)
    pl.semaphore_wait(barrier, len(peers))

    o_core, o_y, o_x, o_zl, o_zh = 0, 1, 1 + Y, 1 + Y + X, 2 + Y + X
    o_agzl, o_agx, o_agy, o_agc = 2 + Y + X + ZH, 3 + Y + X + ZH, 3 + Y + 2 * X + ZH, 3 + 2 * Y + 2 * X + ZH

    def send(src, dst, sidx, ridx, peer):
        d = pltpu.make_async_remote_copy(
            src_ref=src, dst_ref=dst, send_sem=ssem.at[sidx], recv_sem=rsem.at[ridx],
            device_id=peer, device_id_type=MESH_ID)
        d.start()
        return d

    def wait_recv(src, dst, ridx, peer):
        pltpu.make_async_remote_copy(
            src_ref=src, dst_ref=dst, send_sem=ssem.at[0], recv_sem=rsem.at[ridx],
            device_id=peer, device_id_type=MESH_ID).wait_recv()

    def rows(start, size):
        return pl.ds(pl.multiple_of(start, 8), size)

    d = send(g_ref.at[rows((1 - c) * S1, S1)], rc, o_core, o_core, core_peer)
    wait_recv(g_ref.at[rows(c * S1, S1)], rc, o_core, core_peer)
    d.wait_send()
    a1[...] = g_ref[rows(c * S1, S1), :] + rc[...]

    ds = [send(a1.at[rows(p * S2, S2)], ry.at[y], o_y + k, o_y + y, dev(c, p, x, z))
          for k, p in enumerate(y_peers)]
    for k in range(1, Y):
        s = (y - k + Y) % Y
        wait_recv(a1.at[rows(0, S2)], ry.at[s], o_y + s, dev(c, s, x, z))
    for d in ds:
        d.wait_send()
    acc = a1[rows(y * S2, S2), :]
    for k in range(1, Y):
        acc = acc + ry[(y - k + Y) % Y]
    a2[...] = acc

    ds = [send(a2.at[rows(p * S3, S3)], rx.at[x], o_x + k, o_x + x, dev(c, y, p, z))
          for k, p in enumerate(x_peers)]
    for k in range(1, X):
        s = (x - k + X) % X
        wait_recv(a2.at[rows(0, S3)], rx.at[s], o_x + s, dev(c, y, s, z))
    for d in ds:
        d.wait_send()
    acc = a2[rows(x * S3, S3), :]
    for k in range(1, X):
        acc = acc + rx[(x - k + X) % X]
    a3[...] = acc

    d = send(a3.at[rows((1 - zl) * S4, S4)], rzl, o_zl, o_zl, zl_peer)
    wait_recv(a3.at[rows(zl * S4, S4)], rzl, o_zl, zl_peer)
    d.wait_send()
    a4[...] = a3[rows(zl * S4, S4), :] + rzl[...]

    ds = [send(a4, rzh.at[zh], o_zh + k, o_zh + zh, dev(c, y, x, p * 2 + zl))
          for k, p in enumerate(zh_peers)]
    rzh[zh] = a4[...]
    for k in range(1, ZH):
        s = (zh - k + ZH) % ZH
        wait_recv(a4, rzh.at[s], o_zh + s, dev(c, y, x, s * 2 + zl))
    for d in ds:
        d.wait_send()
    acc = rzh[0]
    for j in range(1, ZH):
        acc = acc + rzh[j]
    base = c * S1 + y * S2 + x * S3
    full[rows(base + zl * S4, S4), :] = acc

    mine = rows(base + zl * S4, S4)
    d = send(full.at[mine], full.at[mine], o_agzl, o_agzl, zl_peer)
    wait_recv(full.at[mine], full.at[rows(base + (1 - zl) * S4, S4)], o_agzl, zl_peer)
    d.wait_send()

    mine = rows(c * S1 + y * S2 + x * S3, S3)
    ds = [send(full.at[mine], full.at[mine], o_agx + k, o_agx + x, dev(c, y, p, z))
          for k, p in enumerate(x_peers)]
    for k in range(1, X):
        s = (x - k + X) % X
        wait_recv(full.at[mine], full.at[rows(c * S1 + y * S2 + s * S3, S3)], o_agx + s, dev(c, y, s, z))
    for d in ds:
        d.wait_send()

    mine = rows(c * S1 + y * S2, S2)
    ds = [send(full.at[mine], full.at[mine], o_agy + k, o_agy + y, dev(c, p, x, z))
          for k, p in enumerate(y_peers)]
    for k in range(1, Y):
        s = (y - k + Y) % Y
        wait_recv(full.at[mine], full.at[rows(c * S1 + s * S2, S2)], o_agy + s, dev(c, s, x, z))
    for d in ds:
        d.wait_send()

    mine = rows(c * S1, S1)
    d = send(full.at[mine], full.at[mine], o_agc, o_agc, core_peer)
    wait_recv(full.at[mine], full.at[rows((1 - c) * S1, S1)], o_agc, core_peer)
    d.wait_send()

    out_ref[...] = full[...]


def _window_gather_kernel(nr, nb, p_ref, out_ref, zbuf, ssem, rsem, lsem):
    T = p_ref.shape[0]
    r = lax.axis_index("rows")
    b = lax.axis_index("blk")
    has_up = r > 0
    has_dn = r < nr - 1
    barrier = pltpu.get_barrier_semaphore()
    for k in range(1, nb):
        pl.semaphore_signal(barrier, inc=1, device_id=(r, (b + k) % nb), device_id_type=MESH_ID)

    @pl.when(has_up)
    def _():
        pl.semaphore_signal(barrier, inc=1, device_id=(r - 1, b), device_id_type=MESH_ID)

    @pl.when(has_dn)
    def _():
        pl.semaphore_signal(barrier, inc=1, device_id=(r + 1, b), device_id_type=MESH_ID)

    pl.semaphore_wait(barrier, nb - 1 + has_up.astype(jnp.int32) + has_dn.astype(jnp.int32))

    def block(j):
        return pl.ds(pl.multiple_of(j * T, 8), T)

    def copy(src, slot, j, sidx, peer):
        return pltpu.make_async_remote_copy(
            src_ref=src, dst_ref=out_ref.at[slot, block(j)], send_sem=ssem.at[sidx],
            recv_sem=rsem.at[slot * nb + j], device_id=peer, device_id_type=MESH_ID)

    zone_peers = [(k, (b + k) % nb) for k in range(1, nb)]
    for k, p in zone_peers:
        copy(p_ref, 1, b, k - 1, (r, p)).start()
    own = pltpu.make_async_copy(p_ref, out_ref.at[1, block(b)], lsem.at[0])
    own.start()

    @pl.when(has_dn)
    def _():
        copy(p_ref, 0, b, nb - 1, (r + 1, b)).start()

    @pl.when(has_up)
    def _():
        copy(p_ref, 2, b, nb, (r - 1, b)).start()

    for slot, cond, src_row, base in ((0, has_up, r - 1, nb + 1), (2, has_dn, r + 1, 2 * nb)):
        @pl.when(cond)
        def _():
            copy(out_ref.at[slot, block(b)], slot, b, 0, (src_row, b)).wait_recv()
            for k, p in zone_peers:
                copy(out_ref.at[slot, block(b)], slot, b, base + k - 1, (r, p)).start()

        @pl.when(jnp.logical_not(cond))
        def _():
            zbuf[...] = jnp.zeros_like(zbuf)
            fill = pltpu.make_async_copy(zbuf, out_ref.at[slot], lsem.at[1])
            fill.start()
            fill.wait()

    for k in range(1, nb):
        s = (b - k + nb) % nb
        copy(p_ref, 1, s, 0, (r, s)).wait_recv()
    for slot, cond, base in ((0, has_up, nb + 1), (2, has_dn, 2 * nb)):
        @pl.when(cond)
        def _():
            for k in range(1, nb):
                s = (b - k + nb) % nb
                copy(p_ref, slot, s, 0, (r, s)).wait_recv()
            for k, p in zone_peers:
                copy(out_ref.at[slot, block(b)], slot, b, base + k - 1, (r, p)).wait_send()

    for k, p in zone_peers:
        copy(p_ref, 1, b, k - 1, (r, p)).wait_send()
    own.wait()

    @pl.when(has_dn)
    def _():
        copy(p_ref, 0, b, nb - 1, (r + 1, b)).wait_send()

    @pl.when(has_up)
    def _():
        copy(p_ref, 2, b, nb, (r - 1, b)).wait_send()


def window_gather(p, nr, nb):
    T, K = p.shape
    return pl.pallas_call(
        functools.partial(_window_gather_kernel, nr, nb),
        out_shape=jax.ShapeDtypeStruct((3, nb * T, K), p.dtype),
        in_specs=[pl.BlockSpec(memory_space=pl.ANY)],
        out_specs=pl.BlockSpec(memory_space=pl.ANY),
        scratch_shapes=[
            pltpu.VMEM((nb * T, K), p.dtype),
            pltpu.SemaphoreType.DMA((3 * nb,)),
            pltpu.SemaphoreType.DMA((3 * nb,)),
            pltpu.SemaphoreType.DMA((2,)),
        ],
        compiler_params=pltpu.CompilerParams(collective_id=1, has_side_effects=True),
    )(p)


HI = lax.Precision.HIGHEST


def _mm(a, b):
    return jnp.dot(a, b, precision=HI, preferred_element_type=jnp.float32)


def _mm_t(a, b):
    return lax.dot_general(a, b, (((1,), (1,)), ((), ())), precision=HI, preferred_element_type=jnp.float32)


def _chol_inv_kernel(count, g_ref, m_ref, a_ref, d_ref, b_ref, l_ref):
    n = g_ref.shape[0]
    t = d_ref.shape[0]
    nb = n // t
    gram = g_ref[...] / count
    a_ref[...] = (gram + gram.T) / 2
    m_ref[...] = jnp.zeros_like(m_ref)
    lane = lax.broadcasted_iota(jnp.int32, (1, t), 1)
    eye = (lax.broadcasted_iota(jnp.int32, (t, t), 0) == lax.broadcasted_iota(jnp.int32, (t, t), 1)).astype(jnp.float32)

    def step(r0, j, carry):
        lane2 = lax.broadcasted_iota(jnp.int32, (t - r0, t), 1)
        sub = lax.broadcasted_iota(jnp.int32, (t - r0, 1), 0) + r0
        row = d_ref[pl.ds(j, 1), :]
        piv2 = jnp.sum(jnp.where(lane == j, row, 0.0), axis=1, keepdims=True)
        inv = 1.0 / jnp.sqrt(piv2)
        dmat = d_ref[r0:, :]
        colfull = jnp.sum(jnp.where(lane2 == j, dmat, 0.0), axis=1, keepdims=True)
        col = jnp.where(sub >= j, colfull * inv, 0.0)
        lrow = jnp.where(lane >= j, row * inv, 0.0)
        d_ref[r0:, :] = dmat - col * lrow
        brow = b_ref[pl.ds(j, 1), :] * inv
        bmat = b_ref[r0:, :]
        b_ref[r0:, :] = bmat - jnp.where(sub > j, col, 0.0) * brow
        b_ref[pl.ds(j, 1), :] = brow
        return carry

    for k in range(nb):
        lo = k * t
        d_ref[...] = a_ref[lo:lo + t, lo:lo + t]
        b_ref[...] = eye
        for r0 in range(0, t, 8):
            lax.fori_loop(r0, r0 + 8, functools.partial(step, r0), 0)
        m_ref[lo:lo + t, lo:lo + t] = b_ref[...]
        if k < nb - 1:
            hi = lo + t
            panel = _mm_t(a_ref[hi:, lo:lo + t], b_ref[...])
            l_ref[hi:, lo:lo + t] = panel
            a_ref[hi:, hi:] = a_ref[hi:, hi:] - _mm_t(panel, panel)
    for dist in range(1, nb):
        for i in range(dist, nb):
            j = i - dist
            acc = None
            for k in range(j, i):
                term = _mm(l_ref[i * t:(i + 1) * t, k * t:(k + 1) * t], m_ref[k * t:(k + 1) * t, j * t:(j + 1) * t])
                acc = term if acc is None else acc + term
            m_ref[i * t:(i + 1) * t, j * t:(j + 1) * t] = -_mm(m_ref[i * t:(i + 1) * t, i * t:(i + 1) * t], acc)


def chol_inverse(g, count, t=128):
    n = g.shape[0]
    vmem = pltpu.VMEM
    return pl.pallas_call(
        functools.partial(_chol_inv_kernel, count),
        out_shape=jax.ShapeDtypeStruct((n, n), jnp.float32),
        in_specs=[pl.BlockSpec(memory_space=vmem)],
        out_specs=pl.BlockSpec(memory_space=vmem),
        scratch_shapes=[
            vmem((n, n), jnp.float32),
            vmem((t, t), jnp.float32),
            vmem((t, t), jnp.float32),
            vmem((n, n), jnp.float32),
        ],
    )(g)


def gram_allreduce(g, dims):
    XL, Z, C, XH, Y = dims
    X = XL * XH
    ZH = Z // 2
    N, M = g.shape
    S1 = N // C
    S2 = S1 // Y
    S3 = S2 // X
    S4 = S3 // 2
    nsem = 4 + 2 * Y + 2 * X + ZH
    vmem = pltpu.VMEM
    return pl.pallas_call(
        functools.partial(_ar_kernel, dims),
        out_shape=jax.ShapeDtypeStruct((N, M), jnp.float32),
        in_specs=[pl.BlockSpec(memory_space=vmem)],
        out_specs=pl.BlockSpec(memory_space=vmem),
        scratch_shapes=[
            vmem((S1, M), jnp.float32),
            vmem((Y, S2, M), jnp.float32),
            vmem((X, S3, M), jnp.float32),
            vmem((S4, M), jnp.float32),
            vmem((ZH, S4, M), jnp.float32),
            vmem((S1, M), jnp.float32),
            vmem((S2, M), jnp.float32),
            vmem((S3, M), jnp.float32),
            vmem((S4, M), jnp.float32),
            vmem((N, M), jnp.float32),
            pltpu.SemaphoreType.DMA((nsem,)),
            pltpu.SemaphoreType.DMA((nsem,)),
        ],
        compiler_params=pltpu.CompilerParams(collective_id=0, has_side_effects=True),
    )(g)


def _dims():
    rows, blk = lax.axis_size("rows"), lax.axis_size("blk")
    return (2, rows // 4, 2, 2, blk // 2)


def local(cov_blocks, col_index, block_count, probes):
    rows_here, slots, block, _ = cov_blocks.shape
    tile_rows = probes.shape[0]
    probe_cols = probes.shape[1]
    zone_blocks = rows_here * lax.axis_size("blk")
    zone_number = lax.axis_index("rows")
    relative = col_index - (zone_number - 1) * zone_blocks
    window_blocks = 3 * zone_blocks
    inside = (relative >= 0) & (relative < window_blocks)
    slot_ids = lax.broadcasted_iota(jnp.int32, (rows_here, slots), 1)
    live_mask = inside & (slot_ids < block_count[:, None])
    column_ids = jnp.arange(window_blocks, dtype=jnp.int32)
    hits = (relative[:, :, None] == column_ids[None, None, :]) & live_mask[:, :, None]
    selector = hits.astype(jnp.bfloat16)
    window_matrix = jnp.einsum(
        "lsp,lsac->lapc", selector, cov_blocks, preferred_element_type=jnp.float32
    )
    window_matrix = window_matrix.astype(jnp.bfloat16).reshape(
        rows_here * block, window_blocks * block
    )

    window = window_gather(probes, lax.axis_size("rows"), lax.axis_size("blk"))
    images = jnp.dot(
        window_matrix, window.reshape(window_blocks * block, probe_cols), preferred_element_type=jnp.float32
    )
    gram_local = lax.dot_general(
        images,
        images,
        (((0,), (0,)), ((), ())),
        precision=lax.Precision.HIGHEST,
        preferred_element_type=jnp.float32,
    )
    gram_total = gram_allreduce(gram_local, _dims())
    point_count = tile_rows * lax.axis_size("rows") * lax.axis_size("blk")
    factor_inverse = chol_inverse(gram_total, float(point_count))
    return _mm_t(images, factor_inverse)


def solution(mesh):
    return jax.shard_map(
        local,
        mesh=mesh,
        in_specs=(
            P(("rows", "blk"), None, None, None),
            P(("rows", "blk"), None),
            P(("rows", "blk")),
            P(("rows", "blk"), None),
        ),
        out_specs=P(("rows", "blk"), None),
        check_vma=False,
    )
```

```python
import functools
import jax
import jax.numpy as jnp
from jax import lax
from jax.experimental import pallas as pl
from jax.experimental.pallas import tpu as pltpu
from jax.sharding import PartitionSpec as P

MESH_ID = pl.DeviceIdType.MESH


def _ar_kernel(dims, g_ref, out_ref, rc, ry, rx, rzl, rzh, a1, a2, a3, a4, full, ssem, rsem):
    XL, Z, C, XH, Y = dims
    X = XL * XH
    ZH = Z // 2
    N = g_ref.shape[0]
    S1 = N // C
    S2 = S1 // Y
    S3 = S2 // X
    S4 = S3 // 2
    r = lax.axis_index("rows")
    b = lax.axis_index("blk")
    c = r % C
    z = (r // C) % Z
    xl = r // (C * Z)
    xh = b // Y
    y = b % Y
    x = xh * XL + xl
    zl = z % 2
    zh = z // 2

    def dev(c_, y_, x_, z_):
        return ((x_ % XL) * (Z * C) + z_ * C + c_, (x_ // XL) * Y + y_)

    core_peer = dev(1 - c, y, x, z)
    y_peers = [(y + k) % Y for k in range(1, Y)]
    x_peers = [(x + k) % X for k in range(1, X)]
    zl_peer = dev(c, y, x, zh * 2 + 1 - zl)
    zh_peers = [(zh + k) % ZH for k in range(1, ZH)]
    peers = [core_peer, zl_peer]
    peers += [dev(c, p, x, z) for p in y_peers]
    peers += [dev(c, y, p, z) for p in x_peers]
    peers += [dev(c, y, x, p * 2 + zl) for p in zh_peers]

    barrier = pltpu.get_barrier_semaphore()
    for p in peers:
        pl.semaphore_signal(barrier, inc=1, device_id=p, device_id_type=MESH_ID)
    pl.semaphore_wait(barrier, len(peers))

    o_core, o_y, o_x, o_zl, o_zh = 0, 1, 1 + Y, 1 + Y + X, 2 + Y + X
    o_agzl, o_agx, o_agy, o_agc = 2 + Y + X + ZH, 3 + Y + X + ZH, 3 + Y + 2 * X + ZH, 3 + 2 * Y + 2 * X + ZH

    def send(src, dst, sidx, ridx, peer):
        d = pltpu.make_async_remote_copy(
            src_ref=src, dst_ref=dst, send_sem=ssem.at[sidx], recv_sem=rsem.at[ridx],
            device_id=peer, device_id_type=MESH_ID)
        d.start()
        return d

    def wait_recv(src, dst, ridx, peer):
        pltpu.make_async_remote_copy(
            src_ref=src, dst_ref=dst, send_sem=ssem.at[0], recv_sem=rsem.at[ridx],
            device_id=peer, device_id_type=MESH_ID).wait_recv()

    def rows(start, size):
        return pl.ds(pl.multiple_of(start, 8), size)

    d = send(g_ref.at[rows((1 - c) * S1, S1)], rc, o_core, o_core, core_peer)
    wait_recv(g_ref.at[rows(c * S1, S1)], rc, o_core, core_peer)
    d.wait_send()
    a1[...] = g_ref[rows(c * S1, S1), :] + rc[...]

    ds = [send(a1.at[rows(p * S2, S2)], ry.at[y], o_y + k, o_y + y, dev(c, p, x, z))
          for k, p in enumerate(y_peers)]
    for k in range(1, Y):
        s = (y - k + Y) % Y
        wait_recv(a1.at[rows(0, S2)], ry.at[s], o_y + s, dev(c, s, x, z))
    for d in ds:
        d.wait_send()
    acc = a1[rows(y * S2, S2), :]
    for k in range(1, Y):
        acc = acc + ry[(y - k + Y) % Y]
    a2[...] = acc

    ds = [send(a2.at[rows(p * S3, S3)], rx.at[x], o_x + k, o_x + x, dev(c, y, p, z))
          for k, p in enumerate(x_peers)]
    for k in range(1, X):
        s = (x - k + X) % X
        wait_recv(a2.at[rows(0, S3)], rx.at[s], o_x + s, dev(c, y, s, z))
    for d in ds:
        d.wait_send()
    acc = a2[rows(x * S3, S3), :]
    for k in range(1, X):
        acc = acc + rx[(x - k + X) % X]
    a3[...] = acc

    d = send(a3.at[rows((1 - zl) * S4, S4)], rzl, o_zl, o_zl, zl_peer)
    wait_recv(a3.at[rows(zl * S4, S4)], rzl, o_zl, zl_peer)
    d.wait_send()
    a4[...] = a3[rows(zl * S4, S4), :] + rzl[...]

    ds = [send(a4, rzh.at[zh], o_zh + k, o_zh + zh, dev(c, y, x, p * 2 + zl))
          for k, p in enumerate(zh_peers)]
    rzh[zh] = a4[...]
    for k in range(1, ZH):
        s = (zh - k + ZH) % ZH
        wait_recv(a4, rzh.at[s], o_zh + s, dev(c, y, x, s * 2 + zl))
    for d in ds:
        d.wait_send()
    acc = rzh[0]
    for j in range(1, ZH):
        acc = acc + rzh[j]
    base = c * S1 + y * S2 + x * S3
    full[rows(base + zl * S4, S4), :] = acc

    mine = rows(base + zl * S4, S4)
    d = send(full.at[mine], full.at[mine], o_agzl, o_agzl, zl_peer)
    wait_recv(full.at[mine], full.at[rows(base + (1 - zl) * S4, S4)], o_agzl, zl_peer)
    d.wait_send()

    mine = rows(c * S1 + y * S2 + x * S3, S3)
    ds = [send(full.at[mine], full.at[mine], o_agx + k, o_agx + x, dev(c, y, p, z))
          for k, p in enumerate(x_peers)]
    for k in range(1, X):
        s = (x - k + X) % X
        wait_recv(full.at[mine], full.at[rows(c * S1 + y * S2 + s * S3, S3)], o_agx + s, dev(c, y, s, z))
    for d in ds:
        d.wait_send()

    mine = rows(c * S1 + y * S2, S2)
    ds = [send(full.at[mine], full.at[mine], o_agy + k, o_agy + y, dev(c, p, x, z))
          for k, p in enumerate(y_peers)]
    for k in range(1, Y):
        s = (y - k + Y) % Y
        wait_recv(full.at[mine], full.at[rows(c * S1 + s * S2, S2)], o_agy + s, dev(c, s, x, z))
    for d in ds:
        d.wait_send()

    mine = rows(c * S1, S1)
    d = send(full.at[mine], full.at[mine], o_agc, o_agc, core_peer)
    wait_recv(full.at[mine], full.at[rows((1 - c) * S1, S1)], o_agc, core_peer)
    d.wait_send()

    out_ref[...] = full[...]


def _window_gather_kernel(nr, nb, p_ref, out_ref, zbuf, ssem, rsem, lsem):
    T = p_ref.shape[0]
    r = lax.axis_index("rows")
    b = lax.axis_index("blk")
    has_up = r > 0
    has_dn = r < nr - 1
    barrier = pltpu.get_barrier_semaphore()
    for k in range(1, nb):
        pl.semaphore_signal(barrier, inc=1, device_id=(r, (b + k) % nb), device_id_type=MESH_ID)

    @pl.when(has_up)
    def _():
        pl.semaphore_signal(barrier, inc=1, device_id=(r - 1, b), device_id_type=MESH_ID)

    @pl.when(has_dn)
    def _():
        pl.semaphore_signal(barrier, inc=1, device_id=(r + 1, b), device_id_type=MESH_ID)

    pl.semaphore_wait(barrier, nb - 1 + has_up.astype(jnp.int32) + has_dn.astype(jnp.int32))

    def block(j):
        return pl.ds(pl.multiple_of(j * T, 8), T)

    def copy(src, slot, j, sidx, peer):
        return pltpu.make_async_remote_copy(
            src_ref=src, dst_ref=out_ref.at[slot, block(j)], send_sem=ssem.at[sidx],
            recv_sem=rsem.at[slot * nb + j], device_id=peer, device_id_type=MESH_ID)

    def to_neighbours(src, j, start):
        @pl.when(has_dn)
        def _():
            d = copy(src, 0, j, nb - 1 + j, (r + 1, b))
            d.start() if start else d.wait_send()

        @pl.when(has_up)
        def _():
            d = copy(src, 2, j, 2 * nb - 1 + j, (r - 1, b))
            d.start() if start else d.wait_send()

    zone_peers = [(k, (b + k) % nb) for k in range(1, nb)]
    for k, p in zone_peers:
        copy(p_ref, 1, b, k - 1, (r, p)).start()
    to_neighbours(p_ref, b, True)
    own = pltpu.make_async_copy(p_ref, out_ref.at[1, block(b)], lsem.at[0])
    own.start()
    for k in range(1, nb):
        s = (b - k + nb) % nb
        copy(p_ref, 1, s, 0, (r, s)).wait_recv()
        to_neighbours(out_ref.at[1, block(s)], s, True)

    for slot, cond, src_row in ((0, has_up, r - 1), (2, has_dn, r + 1)):
        @pl.when(cond)
        def _():
            for j in range(nb):
                copy(p_ref, slot, j, 0, (src_row, b)).wait_recv()

        @pl.when(jnp.logical_not(cond))
        def _():
            zbuf[...] = jnp.zeros_like(zbuf)
            fill = pltpu.make_async_copy(zbuf, out_ref.at[slot], lsem.at[1])
            fill.start()
            fill.wait()

    for k, p in zone_peers:
        copy(p_ref, 1, b, k - 1, (r, p)).wait_send()
    own.wait()
    for j in range(nb):
        to_neighbours(p_ref, j, False)


def window_gather(p, nr, nb):
    T, K = p.shape
    return pl.pallas_call(
        functools.partial(_window_gather_kernel, nr, nb),
        out_shape=jax.ShapeDtypeStruct((3, nb * T, K), p.dtype),
        in_specs=[pl.BlockSpec(memory_space=pl.ANY)],
        out_specs=pl.BlockSpec(memory_space=pl.ANY),
        scratch_shapes=[
            pltpu.VMEM((nb * T, K), p.dtype),
            pltpu.SemaphoreType.DMA((3 * nb,)),
            pltpu.SemaphoreType.DMA((3 * nb,)),
            pltpu.SemaphoreType.DMA((2,)),
        ],
        compiler_params=pltpu.CompilerParams(collective_id=1, has_side_effects=True),
    )(p)


HI = lax.Precision.HIGHEST


def _mm(a, b):
    return jnp.dot(a, b, precision=HI, preferred_element_type=jnp.float32)


def _mm_t(a, b):
    return lax.dot_general(a, b, (((1,), (1,)), ((), ())), precision=HI, preferred_element_type=jnp.float32)


def _chol_inv_kernel(count, g_ref, m_ref, a_ref, d_ref, b_ref, l_ref):
    n = g_ref.shape[0]
    t = d_ref.shape[0]
    nb = n // t
    gram = g_ref[...] / count
    a_ref[...] = (gram + gram.T) / 2
    m_ref[...] = jnp.zeros_like(m_ref)
    lane = lax.broadcasted_iota(jnp.int32, (1, t), 1)
    eye = (lax.broadcasted_iota(jnp.int32, (t, t), 0) == lax.broadcasted_iota(jnp.int32, (t, t), 1)).astype(jnp.float32)

    def step(r0, j, carry):
        lane2 = lax.broadcasted_iota(jnp.int32, (t - r0, t), 1)
        sub = lax.broadcasted_iota(jnp.int32, (t - r0, 1), 0) + r0
        row = d_ref[pl.ds(j, 1), :]
        piv2 = jnp.sum(jnp.where(lane == j, row, 0.0), axis=1, keepdims=True)
        inv = 1.0 / jnp.sqrt(piv2)
        dmat = d_ref[r0:, :]
        colfull = jnp.sum(jnp.where(lane2 == j, dmat, 0.0), axis=1, keepdims=True)
        col = jnp.where(sub >= j, colfull * inv, 0.0)
        lrow = jnp.where(lane >= j, row * inv, 0.0)
        d_ref[r0:, :] = dmat - col * lrow
        brow = b_ref[pl.ds(j, 1), :] * inv
        bmat = b_ref[r0:, :]
        b_ref[r0:, :] = bmat - jnp.where(sub > j, col, 0.0) * brow
        b_ref[pl.ds(j, 1), :] = brow
        return carry

    for k in range(nb):
        lo = k * t
        d_ref[...] = a_ref[lo:lo + t, lo:lo + t]
        b_ref[...] = eye
        for r0 in range(0, t, 8):
            lax.fori_loop(r0, r0 + 8, functools.partial(step, r0), 0)
        m_ref[lo:lo + t, lo:lo + t] = b_ref[...]
        if k < nb - 1:
            hi = lo + t
            panel = _mm_t(a_ref[hi:, lo:lo + t], b_ref[...])
            l_ref[hi:, lo:lo + t] = panel
            a_ref[hi:, hi:] = a_ref[hi:, hi:] - _mm_t(panel, panel)
    for dist in range(1, nb):
        for i in range(dist, nb):
            j = i - dist
            acc = None
            for k in range(j, i):
                term = _mm(l_ref[i * t:(i + 1) * t, k * t:(k + 1) * t], m_ref[k * t:(k + 1) * t, j * t:(j + 1) * t])
                acc = term if acc is None else acc + term
            m_ref[i * t:(i + 1) * t, j * t:(j + 1) * t] = -_mm(m_ref[i * t:(i + 1) * t, i * t:(i + 1) * t], acc)


def chol_inverse(g, count, t=128):
    n = g.shape[0]
    vmem = pltpu.VMEM
    return pl.pallas_call(
        functools.partial(_chol_inv_kernel, count),
        out_shape=jax.ShapeDtypeStruct((n, n), jnp.float32),
        in_specs=[pl.BlockSpec(memory_space=vmem)],
        out_specs=pl.BlockSpec(memory_space=vmem),
        scratch_shapes=[
            vmem((n, n), jnp.float32),
            vmem((t, t), jnp.float32),
            vmem((t, t), jnp.float32),
            vmem((n, n), jnp.float32),
        ],
    )(g)


def gram_allreduce(g, dims):
    XL, Z, C, XH, Y = dims
    X = XL * XH
    ZH = Z // 2
    N, M = g.shape
    S1 = N // C
    S2 = S1 // Y
    S3 = S2 // X
    S4 = S3 // 2
    nsem = 4 + 2 * Y + 2 * X + ZH
    vmem = pltpu.VMEM
    return pl.pallas_call(
        functools.partial(_ar_kernel, dims),
        out_shape=jax.ShapeDtypeStruct((N, M), jnp.float32),
        in_specs=[pl.BlockSpec(memory_space=vmem)],
        out_specs=pl.BlockSpec(memory_space=vmem),
        scratch_shapes=[
            vmem((S1, M), jnp.float32),
            vmem((Y, S2, M), jnp.float32),
            vmem((X, S3, M), jnp.float32),
            vmem((S4, M), jnp.float32),
            vmem((ZH, S4, M), jnp.float32),
            vmem((S1, M), jnp.float32),
            vmem((S2, M), jnp.float32),
            vmem((S3, M), jnp.float32),
            vmem((S4, M), jnp.float32),
            vmem((N, M), jnp.float32),
            pltpu.SemaphoreType.DMA((nsem,)),
            pltpu.SemaphoreType.DMA((nsem,)),
        ],
        compiler_params=pltpu.CompilerParams(collective_id=0, has_side_effects=True),
    )(g)


def _dims():
    rows, blk = lax.axis_size("rows"), lax.axis_size("blk")
    return (2, rows // 4, 2, 2, blk // 2)


def local(cov_blocks, col_index, block_count, probes):
    rows_here, slots, block, _ = cov_blocks.shape
    tile_rows = probes.shape[0]
    probe_cols = probes.shape[1]
    zone_blocks = rows_here * lax.axis_size("blk")
    zone_number = lax.axis_index("rows")
    relative = col_index - (zone_number - 1) * zone_blocks
    window_blocks = 3 * zone_blocks
    inside = (relative >= 0) & (relative < window_blocks)
    slot_ids = lax.broadcasted_iota(jnp.int32, (rows_here, slots), 1)
    live_mask = inside & (slot_ids < block_count[:, None])
    column_ids = jnp.arange(window_blocks, dtype=jnp.int32)
    hits = (relative[:, :, None] == column_ids[None, None, :]) & live_mask[:, :, None]
    selector = hits.astype(jnp.bfloat16)
    window_matrix = jnp.einsum(
        "lsp,lsac->lapc", selector, cov_blocks, preferred_element_type=jnp.float32
    )
    window_matrix = window_matrix.astype(jnp.bfloat16).reshape(
        rows_here * block, window_blocks * block
    )

    window = window_gather(probes, lax.axis_size("rows"), lax.axis_size("blk"))
    images = jnp.dot(
        window_matrix, window.reshape(window_blocks * block, probe_cols), preferred_element_type=jnp.float32
    )
    gram_local = lax.dot_general(
        images,
        images,
        (((0,), (0,)), ((), ())),
        precision=lax.Precision.HIGHEST,
        preferred_element_type=jnp.float32,
    )
    gram_total = gram_allreduce(gram_local, _dims())
    point_count = tile_rows * lax.axis_size("rows") * lax.axis_size("blk")
    factor_inverse = chol_inverse(gram_total, float(point_count))
    return _mm_t(images, factor_inverse)


def solution(mesh):
    return jax.shard_map(
        local,
        mesh=mesh,
        in_specs=(
            P(("rows", "blk"), None, None, None),
            P(("rows", "blk"), None),
            P(("rows", "blk")),
            P(("rows", "blk"), None),
        ),
        out_specs=P(("rows", "blk"), None),
        check_vma=False,
    )
```

```python
import functools
import jax
import jax.numpy as jnp
from jax import lax
from jax.experimental import pallas as pl
from jax.experimental.pallas import tpu as pltpu
from jax.sharding import PartitionSpec as P

MESH_ID = pl.DeviceIdType.MESH


def _ar_kernel(dims, g_ref, out_ref, rc, ry, rx, rzl, rzh, a1, a2, a3, a4, full, ssem, rsem):
    XL, Z, C, XH, Y = dims
    X = XL * XH
    ZH = Z // 2
    N = g_ref.shape[0]
    S1 = N // C
    S2 = S1 // Y
    S3 = S2 // X
    S4 = S3 // 2
    r = lax.axis_index("rows")
    b = lax.axis_index("blk")
    c = r % C
    z = (r // C) % Z
    xl = r // (C * Z)
    xh = b // Y
    y = b % Y
    x = xh * XL + xl
    zl = z % 2
    zh = z // 2

    def dev(c_, y_, x_, z_):
        return ((x_ % XL) * (Z * C) + z_ * C + c_, (x_ // XL) * Y + y_)

    core_peer = dev(1 - c, y, x, z)
    y_peers = [(y + k) % Y for k in range(1, Y)]
    x_peers = [(x + k) % X for k in range(1, X)]
    zl_peer = dev(c, y, x, zh * 2 + 1 - zl)
    zh_peers = [(zh + k) % ZH for k in range(1, ZH)]
    peers = [core_peer, zl_peer]
    peers += [dev(c, p, x, z) for p in y_peers]
    peers += [dev(c, y, p, z) for p in x_peers]
    peers += [dev(c, y, x, p * 2 + zl) for p in zh_peers]

    barrier = pltpu.get_barrier_semaphore()
    for p in peers:
        pl.semaphore_signal(barrier, inc=1, device_id=p, device_id_type=MESH_ID)
    pl.semaphore_wait(barrier, len(peers))

    o_core, o_y, o_x, o_zl, o_zh = 0, 1, 1 + Y, 1 + Y + X, 2 + Y + X
    o_agzl, o_agx, o_agy, o_agc = 2 + Y + X + ZH, 3 + Y + X + ZH, 3 + Y + 2 * X + ZH, 3 + 2 * Y + 2 * X + ZH

    def send(src, dst, sidx, ridx, peer):
        d = pltpu.make_async_remote_copy(
            src_ref=src, dst_ref=dst, send_sem=ssem.at[sidx], recv_sem=rsem.at[ridx],
            device_id=peer, device_id_type=MESH_ID)
        d.start()
        return d

    def wait_recv(src, dst, ridx, peer):
        pltpu.make_async_remote_copy(
            src_ref=src, dst_ref=dst, send_sem=ssem.at[0], recv_sem=rsem.at[ridx],
            device_id=peer, device_id_type=MESH_ID).wait_recv()

    def rows(start, size):
        return pl.ds(pl.multiple_of(start, 8), size)

    d = send(g_ref.at[rows((1 - c) * S1, S1)], rc, o_core, o_core, core_peer)
    wait_recv(g_ref.at[rows(c * S1, S1)], rc, o_core, core_peer)
    d.wait_send()
    a1[...] = g_ref[rows(c * S1, S1), :] + rc[...]

    ds = [send(a1.at[rows(p * S2, S2)], ry.at[y], o_y + k, o_y + y, dev(c, p, x, z))
          for k, p in enumerate(y_peers)]
    for k in range(1, Y):
        s = (y - k + Y) % Y
        wait_recv(a1.at[rows(0, S2)], ry.at[s], o_y + s, dev(c, s, x, z))
    for d in ds:
        d.wait_send()
    acc = a1[rows(y * S2, S2), :]
    for k in range(1, Y):
        acc = acc + ry[(y - k + Y) % Y]
    a2[...] = acc

    ds = [send(a2.at[rows(p * S3, S3)], rx.at[x], o_x + k, o_x + x, dev(c, y, p, z))
          for k, p in enumerate(x_peers)]
    for k in range(1, X):
        s = (x - k + X) % X
        wait_recv(a2.at[rows(0, S3)], rx.at[s], o_x + s, dev(c, y, s, z))
    for d in ds:
        d.wait_send()
    acc = a2[rows(x * S3, S3), :]
    for k in range(1, X):
        acc = acc + rx[(x - k + X) % X]
    a3[...] = acc

    d = send(a3.at[rows((1 - zl) * S4, S4)], rzl, o_zl, o_zl, zl_peer)
    wait_recv(a3.at[rows(zl * S4, S4)], rzl, o_zl, zl_peer)
    d.wait_send()
    a4[...] = a3[rows(zl * S4, S4), :] + rzl[...]

    ds = [send(a4, rzh.at[zh], o_zh + k, o_zh + zh, dev(c, y, x, p * 2 + zl))
          for k, p in enumerate(zh_peers)]
    rzh[zh] = a4[...]
    for k in range(1, ZH):
        s = (zh - k + ZH) % ZH
        wait_recv(a4, rzh.at[s], o_zh + s, dev(c, y, x, s * 2 + zl))
    for d in ds:
        d.wait_send()
    acc = rzh[0]
    for j in range(1, ZH):
        acc = acc + rzh[j]
    base = c * S1 + y * S2 + x * S3
    full[rows(base + zl * S4, S4), :] = acc

    mine = rows(base + zl * S4, S4)
    d = send(full.at[mine], full.at[mine], o_agzl, o_agzl, zl_peer)
    wait_recv(full.at[mine], full.at[rows(base + (1 - zl) * S4, S4)], o_agzl, zl_peer)
    d.wait_send()

    mine = rows(c * S1 + y * S2 + x * S3, S3)
    ds = [send(full.at[mine], full.at[mine], o_agx + k, o_agx + x, dev(c, y, p, z))
          for k, p in enumerate(x_peers)]
    for k in range(1, X):
        s = (x - k + X) % X
        wait_recv(full.at[mine], full.at[rows(c * S1 + y * S2 + s * S3, S3)], o_agx + s, dev(c, y, s, z))
    for d in ds:
        d.wait_send()

    mine = rows(c * S1 + y * S2, S2)
    ds = [send(full.at[mine], full.at[mine], o_agy + k, o_agy + y, dev(c, p, x, z))
          for k, p in enumerate(y_peers)]
    for k in range(1, Y):
        s = (y - k + Y) % Y
        wait_recv(full.at[mine], full.at[rows(c * S1 + s * S2, S2)], o_agy + s, dev(c, s, x, z))
    for d in ds:
        d.wait_send()

    mine = rows(c * S1, S1)
    d = send(full.at[mine], full.at[mine], o_agc, o_agc, core_peer)
    wait_recv(full.at[mine], full.at[rows((1 - c) * S1, S1)], o_agc, core_peer)
    d.wait_send()

    out_ref[...] = full[...]


def _zone_gather_kernel(nb, p_ref, out_ref, ssem, rsem, lsem):
    T = p_ref.shape[0]
    r = lax.axis_index("rows")
    b = lax.axis_index("blk")
    barrier = pltpu.get_barrier_semaphore()
    for k in range(1, nb):
        pl.semaphore_signal(barrier, inc=1, device_id=(r, (b + k) % nb), device_id_type=MESH_ID)
    pl.semaphore_wait(barrier, nb - 1)
    here = pl.ds(pl.multiple_of(b * T, 8), T)
    ds = []
    for k in range(1, nb):
        d = pltpu.make_async_remote_copy(
            src_ref=p_ref, dst_ref=out_ref.at[here], send_sem=ssem.at[k - 1], recv_sem=rsem.at[b],
            device_id=(r, (b + k) % nb), device_id_type=MESH_ID)
        d.start()
        ds.append(d)
    own = pltpu.make_async_copy(p_ref, out_ref.at[here], lsem.at[0])
    own.start()
    for k in range(1, nb):
        s = (b - k + nb) % nb
        pltpu.make_async_remote_copy(
            src_ref=p_ref, dst_ref=out_ref.at[pl.ds(pl.multiple_of(s * T, 8), T)], send_sem=ssem.at[0],
            recv_sem=rsem.at[s], device_id=(r, s), device_id_type=MESH_ID).wait_recv()
    for d in ds:
        d.wait_send()
    own.wait()


def zone_gather(p, nb):
    T, K = p.shape
    return pl.pallas_call(
        functools.partial(_zone_gather_kernel, nb),
        out_shape=jax.ShapeDtypeStruct((nb * T, K), p.dtype),
        in_specs=[pl.BlockSpec(memory_space=pl.ANY)],
        out_specs=pl.BlockSpec(memory_space=pl.ANY),
        scratch_shapes=[
            pltpu.SemaphoreType.DMA((nb - 1,)),
            pltpu.SemaphoreType.DMA((nb,)),
            pltpu.SemaphoreType.DMA((1,)),
        ],
        compiler_params=pltpu.CompilerParams(collective_id=1, has_side_effects=True),
    )(p)


HI = lax.Precision.HIGHEST


def _mm(a, b):
    return jnp.dot(a, b, precision=HI, preferred_element_type=jnp.float32)


def _mm_t(a, b):
    return lax.dot_general(a, b, (((1,), (1,)), ((), ())), precision=HI, preferred_element_type=jnp.float32)


def _chol_inv_kernel(count, g_ref, m_ref, a_ref, d_ref, b_ref, l_ref):
    n = g_ref.shape[0]
    t = d_ref.shape[0]
    nb = n // t
    gram = g_ref[...] / count
    a_ref[...] = (gram + gram.T) / 2
    m_ref[...] = jnp.zeros_like(m_ref)
    lane = lax.broadcasted_iota(jnp.int32, (1, t), 1)
    eye = (lax.broadcasted_iota(jnp.int32, (t, t), 0) == lax.broadcasted_iota(jnp.int32, (t, t), 1)).astype(jnp.float32)

    def step(r0, j, carry):
        lane2 = lax.broadcasted_iota(jnp.int32, (t - r0, t), 1)
        sub = lax.broadcasted_iota(jnp.int32, (t - r0, 1), 0) + r0
        row = d_ref[pl.ds(j, 1), :]
        piv2 = jnp.sum(jnp.where(lane == j, row, 0.0), axis=1, keepdims=True)
        inv = lax.rsqrt(piv2)
        dmat = d_ref[r0:, :]
        colfull = jnp.sum(jnp.where(lane2 == j, dmat, 0.0), axis=1, keepdims=True)
        col = jnp.where(sub >= j, colfull * inv, 0.0)
        lrow = jnp.where(lane >= j, row * inv, 0.0)
        d_ref[r0:, :] = dmat - col * lrow
        brow = b_ref[pl.ds(j, 1), :] * inv
        bmat = b_ref[r0:, :]
        b_ref[r0:, :] = bmat - jnp.where(sub > j, col, 0.0) * brow
        b_ref[pl.ds(j, 1), :] = brow
        return carry

    for k in range(nb):
        lo = k * t
        d_ref[...] = a_ref[lo:lo + t, lo:lo + t]
        b_ref[...] = eye
        for r0 in range(0, t, 8):
            lax.fori_loop(r0, r0 + 8, functools.partial(step, r0), 0)
        m_ref[lo:lo + t, lo:lo + t] = b_ref[...]
        if k < nb - 1:
            hi = lo + t
            panel = _mm_t(a_ref[hi:, lo:lo + t], b_ref[...])
            l_ref[hi:, lo:lo + t] = panel
            a_ref[hi:, hi:] = a_ref[hi:, hi:] - _mm_t(panel, panel)
    for dist in range(1, nb):
        for i in range(dist, nb):
            j = i - dist
            acc = None
            for k in range(j, i):
                term = _mm(l_ref[i * t:(i + 1) * t, k * t:(k + 1) * t], m_ref[k * t:(k + 1) * t, j * t:(j + 1) * t])
                acc = term if acc is None else acc + term
            m_ref[i * t:(i + 1) * t, j * t:(j + 1) * t] = -_mm(m_ref[i * t:(i + 1) * t, i * t:(i + 1) * t], acc)


def chol_inverse(g, count, t=128):
    n = g.shape[0]
    vmem = pltpu.VMEM
    return pl.pallas_call(
        functools.partial(_chol_inv_kernel, count),
        out_shape=jax.ShapeDtypeStruct((n, n), jnp.float32),
        in_specs=[pl.BlockSpec(memory_space=vmem)],
        out_specs=pl.BlockSpec(memory_space=vmem),
        scratch_shapes=[
            vmem((n, n), jnp.float32),
            vmem((t, t), jnp.float32),
            vmem((t, t), jnp.float32),
            vmem((n, n), jnp.float32),
        ],
    )(g)


def gram_allreduce(g, dims):
    XL, Z, C, XH, Y = dims
    X = XL * XH
    ZH = Z // 2
    N, M = g.shape
    S1 = N // C
    S2 = S1 // Y
    S3 = S2 // X
    S4 = S3 // 2
    nsem = 4 + 2 * Y + 2 * X + ZH
    vmem = pltpu.VMEM
    return pl.pallas_call(
        functools.partial(_ar_kernel, dims),
        out_shape=jax.ShapeDtypeStruct((N, M), jnp.float32),
        in_specs=[pl.BlockSpec(memory_space=vmem)],
        out_specs=pl.BlockSpec(memory_space=vmem),
        scratch_shapes=[
            vmem((S1, M), jnp.float32),
            vmem((Y, S2, M), jnp.float32),
            vmem((X, S3, M), jnp.float32),
            vmem((S4, M), jnp.float32),
            vmem((ZH, S4, M), jnp.float32),
            vmem((S1, M), jnp.float32),
            vmem((S2, M), jnp.float32),
            vmem((S3, M), jnp.float32),
            vmem((S4, M), jnp.float32),
            vmem((N, M), jnp.float32),
            pltpu.SemaphoreType.DMA((nsem,)),
            pltpu.SemaphoreType.DMA((nsem,)),
        ],
        compiler_params=pltpu.CompilerParams(collective_id=0, has_side_effects=True),
    )(g)


def extended(x, sides, width):
    for axis, dim in sides:
        devices, length = (lax.axis_size(axis), x.shape[dim])
        up = [(i, (i + 1) % devices) for i in range(devices - 1)]
        down = [(j, i) for i, j in up]
        last = lax.slice_in_dim(x, length - width, length, axis=dim)
        first = lax.slice_in_dim(x, 0, width, axis=dim)
        before = lax.ppermute(last, axis, up)
        after = lax.ppermute(first, axis, down)
        x = jnp.concatenate([before, x, after], axis=dim)
    return x


def _dims():
    rows, blk = lax.axis_size("rows"), lax.axis_size("blk")
    return (2, rows // 4, 2, 2, blk // 2)


def local(cov_blocks, col_index, block_count, probes):
    rows_here, slots, block, _ = cov_blocks.shape
    tile_rows = probes.shape[0]
    probe_cols = probes.shape[1]
    zone_blocks = rows_here * lax.axis_size("blk")
    zone_number = lax.axis_index("rows")
    relative = col_index - (zone_number - 1) * zone_blocks
    window_blocks = 3 * zone_blocks
    inside = (relative >= 0) & (relative < window_blocks)
    slot_ids = lax.broadcasted_iota(jnp.int32, (rows_here, slots), 1)
    live_mask = inside & (slot_ids < block_count[:, None])
    column_ids = jnp.arange(window_blocks, dtype=jnp.int32)
    hits = (relative[:, :, None] == column_ids[None, None, :]) & live_mask[:, :, None]
    selector = hits.astype(jnp.bfloat16)
    window_matrix = jnp.einsum(
        "lsp,lsac->lapc", selector, cov_blocks, preferred_element_type=jnp.float32
    )
    window_matrix = window_matrix.astype(jnp.bfloat16).reshape(
        rows_here * block, window_blocks * block
    )

    def add_columns(running, shard_rows, first_row):
        length = shard_rows.shape[0]
        columns = lax.dynamic_slice_in_dim(window_matrix, first_row, length, 1)
        return running + jnp.dot(columns, shard_rows, preferred_element_type=jnp.float32)

    zeros_out = jnp.zeros((tile_rows, probe_cols), jnp.float32)
    own_zone = zone_gather(probes, lax.axis_size("blk"))
    zone_length = own_zone.shape[0]
    images = add_columns(zeros_out, own_zone, zone_length)
    near_zones = extended(own_zone, (("rows", 0),), zone_length)
    images = add_columns(images, lax.slice_in_dim(near_zones, 0, zone_length, axis=0), 0)
    images = add_columns(
        images,
        lax.slice_in_dim(near_zones, 2 * zone_length, 3 * zone_length, axis=0),
        2 * zone_length,
    )
    gram_local = lax.dot_general(
        images,
        images,
        (((0,), (0,)), ((), ())),
        precision=lax.Precision.HIGHEST,
        preferred_element_type=jnp.float32,
    )
    gram_total = gram_allreduce(gram_local, _dims())
    point_count = tile_rows * lax.axis_size("rows") * lax.axis_size("blk")
    factor_inverse = chol_inverse(gram_total, float(point_count))
    return _mm_t(images, factor_inverse)


def solution(mesh):
    return jax.shard_map(
        local,
        mesh=mesh,
        in_specs=(
            P(("rows", "blk"), None, None, None),
            P(("rows", "blk"), None),
            P(("rows", "blk")),
            P(("rows", "blk"), None),
        ),
        out_specs=P(("rows", "blk"), None),
        check_vma=False,
    )
```

```python
import functools
import jax
import jax.numpy as jnp
from jax import lax
from jax.experimental import pallas as pl
from jax.experimental.pallas import tpu as pltpu
from jax.sharding import PartitionSpec as P

MESH_ID = pl.DeviceIdType.MESH


def _ar_kernel(dims, g_ref, out_ref, rc, ry, rx, rzl, rzh, a1, a2, a3, a4, full, ssem, rsem):
    XL, Z, C, XH, Y = dims
    X = XL * XH
    ZH = Z // 2
    N = g_ref.shape[0]
    S1 = N // C
    S2 = S1 // Y
    S3 = S2 // X
    S4 = S3 // 2
    r = lax.axis_index("rows")
    b = lax.axis_index("blk")
    c = r % C
    z = (r // C) % Z
    xl = r // (C * Z)
    xh = b // Y
    y = b % Y
    x = xh * XL + xl
    zl = z % 2
    zh = z // 2

    def dev(c_, y_, x_, z_):
        return ((x_ % XL) * (Z * C) + z_ * C + c_, (x_ // XL) * Y + y_)

    core_peer = dev(1 - c, y, x, z)
    y_peers = [(y + k) % Y for k in range(1, Y)]
    x_peers = [(x + k) % X for k in range(1, X)]
    zl_peer = dev(c, y, x, zh * 2 + 1 - zl)
    zh_peers = [(zh + k) % ZH for k in range(1, ZH)]
    peers = [core_peer, zl_peer]
    peers += [dev(c, p, x, z) for p in y_peers]
    peers += [dev(c, y, p, z) for p in x_peers]
    peers += [dev(c, y, x, p * 2 + zl) for p in zh_peers]

    barrier = pltpu.get_barrier_semaphore()
    for p in peers:
        pl.semaphore_signal(barrier, inc=1, device_id=p, device_id_type=MESH_ID)
    pl.semaphore_wait(barrier, len(peers))

    o_core, o_y, o_x, o_zl, o_zh = 0, 1, 1 + Y, 1 + Y + X, 2 + Y + X
    o_agzl, o_agx, o_agy, o_agc = 2 + Y + X + ZH, 3 + Y + X + ZH, 3 + Y + 2 * X + ZH, 3 + 2 * Y + 2 * X + ZH

    def send(src, dst, sidx, ridx, peer):
        d = pltpu.make_async_remote_copy(
            src_ref=src, dst_ref=dst, send_sem=ssem.at[sidx], recv_sem=rsem.at[ridx],
            device_id=peer, device_id_type=MESH_ID)
        d.start()
        return d

    def wait_recv(src, dst, ridx, peer):
        pltpu.make_async_remote_copy(
            src_ref=src, dst_ref=dst, send_sem=ssem.at[0], recv_sem=rsem.at[ridx],
            device_id=peer, device_id_type=MESH_ID).wait_recv()

    def rows(start, size):
        return pl.ds(pl.multiple_of(start, 8), size)

    d = send(g_ref.at[rows((1 - c) * S1, S1)], rc, o_core, o_core, core_peer)
    wait_recv(g_ref.at[rows(c * S1, S1)], rc, o_core, core_peer)
    d.wait_send()
    a1[...] = g_ref[rows(c * S1, S1), :] + rc[...]

    ds = [send(a1.at[rows(p * S2, S2)], ry.at[y], o_y + k, o_y + y, dev(c, p, x, z))
          for k, p in enumerate(y_peers)]
    for k in range(1, Y):
        s = (y - k + Y) % Y
        wait_recv(a1.at[rows(0, S2)], ry.at[s], o_y + s, dev(c, s, x, z))
    for d in ds:
        d.wait_send()
    acc = a1[rows(y * S2, S2), :]
    for k in range(1, Y):
        acc = acc + ry[(y - k + Y) % Y]
    a2[...] = acc

    ds = [send(a2.at[rows(p * S3, S3)], rx.at[x], o_x + k, o_x + x, dev(c, y, p, z))
          for k, p in enumerate(x_peers)]
    for k in range(1, X):
        s = (x - k + X) % X
        wait_recv(a2.at[rows(0, S3)], rx.at[s], o_x + s, dev(c, y, s, z))
    for d in ds:
        d.wait_send()
    acc = a2[rows(x * S3, S3), :]
    for k in range(1, X):
        acc = acc + rx[(x - k + X) % X]
    a3[...] = acc

    d = send(a3.at[rows((1 - zl) * S4, S4)], rzl, o_zl, o_zl, zl_peer)
    wait_recv(a3.at[rows(zl * S4, S4)], rzl, o_zl, zl_peer)
    d.wait_send()
    a4[...] = a3[rows(zl * S4, S4), :] + rzl[...]

    ds = [send(a4, rzh.at[zh], o_zh + k, o_zh + zh, dev(c, y, x, p * 2 + zl))
          for k, p in enumerate(zh_peers)]
    rzh[zh] = a4[...]
    for k in range(1, ZH):
        s = (zh - k + ZH) % ZH
        wait_recv(a4, rzh.at[s], o_zh + s, dev(c, y, x, s * 2 + zl))
    for d in ds:
        d.wait_send()
    acc = rzh[0]
    for j in range(1, ZH):
        acc = acc + rzh[j]
    base = c * S1 + y * S2 + x * S3
    full[rows(base + zl * S4, S4), :] = acc

    mine = rows(base + zl * S4, S4)
    d = send(full.at[mine], full.at[mine], o_agzl, o_agzl, zl_peer)
    wait_recv(full.at[mine], full.at[rows(base + (1 - zl) * S4, S4)], o_agzl, zl_peer)
    d.wait_send()

    mine = rows(c * S1 + y * S2 + x * S3, S3)
    ds = [send(full.at[mine], full.at[mine], o_agx + k, o_agx + x, dev(c, y, p, z))
          for k, p in enumerate(x_peers)]
    for k in range(1, X):
        s = (x - k + X) % X
        wait_recv(full.at[mine], full.at[rows(c * S1 + y * S2 + s * S3, S3)], o_agx + s, dev(c, y, s, z))
    for d in ds:
        d.wait_send()

    mine = rows(c * S1 + y * S2, S2)
    ds = [send(full.at[mine], full.at[mine], o_agy + k, o_agy + y, dev(c, p, x, z))
          for k, p in enumerate(y_peers)]
    for k in range(1, Y):
        s = (y - k + Y) % Y
        wait_recv(full.at[mine], full.at[rows(c * S1 + s * S2, S2)], o_agy + s, dev(c, s, x, z))
    for d in ds:
        d.wait_send()

    mine = rows(c * S1, S1)
    d = send(full.at[mine], full.at[mine], o_agc, o_agc, core_peer)
    wait_recv(full.at[mine], full.at[rows((1 - c) * S1, S1)], o_agc, core_peer)
    d.wait_send()

    out_ref[...] = full[...]


def _zone_gather_kernel(nb, p_ref, out_ref, ssem, rsem, lsem):
    T = p_ref.shape[0]
    r = lax.axis_index("rows")
    b = lax.axis_index("blk")
    barrier = pltpu.get_barrier_semaphore()
    for k in range(1, nb):
        pl.semaphore_signal(barrier, inc=1, device_id=(r, (b + k) % nb), device_id_type=MESH_ID)
    pl.semaphore_wait(barrier, nb - 1)
    here = pl.ds(pl.multiple_of(b * T, 8), T)
    ds = []
    for k in range(1, nb):
        d = pltpu.make_async_remote_copy(
            src_ref=p_ref, dst_ref=out_ref.at[here], send_sem=ssem.at[k - 1], recv_sem=rsem.at[b],
            device_id=(r, (b + k) % nb), device_id_type=MESH_ID)
        d.start()
        ds.append(d)
    own = pltpu.make_async_copy(p_ref, out_ref.at[here], lsem.at[0])
    own.start()
    for k in range(1, nb):
        s = (b - k + nb) % nb
        pltpu.make_async_remote_copy(
            src_ref=p_ref, dst_ref=out_ref.at[pl.ds(pl.multiple_of(s * T, 8), T)], send_sem=ssem.at[0],
            recv_sem=rsem.at[s], device_id=(r, s), device_id_type=MESH_ID).wait_recv()
    for d in ds:
        d.wait_send()
    own.wait()


def zone_gather(p, nb):
    T, K = p.shape
    return pl.pallas_call(
        functools.partial(_zone_gather_kernel, nb),
        out_shape=jax.ShapeDtypeStruct((nb * T, K), p.dtype),
        in_specs=[pl.BlockSpec(memory_space=pl.ANY)],
        out_specs=pl.BlockSpec(memory_space=pl.ANY),
        scratch_shapes=[
            pltpu.SemaphoreType.DMA((nb - 1,)),
            pltpu.SemaphoreType.DMA((nb,)),
            pltpu.SemaphoreType.DMA((1,)),
        ],
        compiler_params=pltpu.CompilerParams(collective_id=1, has_side_effects=True),
    )(p)


HI = lax.Precision.HIGHEST


def _mm(a, b):
    return jnp.dot(a, b, precision=HI, preferred_element_type=jnp.float32)


def _mm_t(a, b):
    return lax.dot_general(a, b, (((1,), (1,)), ((), ())), precision=HI, preferred_element_type=jnp.float32)


def _chol_inv_kernel(count, g_ref, m_ref, a_ref, d_ref, b_ref, l_ref):
    n = g_ref.shape[0]
    t = d_ref.shape[0]
    nb = n // t
    gram = g_ref[...] / count
    a_ref[...] = (gram + gram.T) / 2
    m_ref[...] = jnp.zeros_like(m_ref)
    lane = lax.broadcasted_iota(jnp.int32, (1, t), 1)
    eye = (lax.broadcasted_iota(jnp.int32, (t, t), 0) == lax.broadcasted_iota(jnp.int32, (t, t), 1)).astype(jnp.float32)

    for k in range(nb):
        lo = k * t
        d_ref[...] = a_ref[lo:lo + t, lo:lo + t]
        b_ref[...] = eye
        for r0 in range(0, t, 8):
            sub = lax.broadcasted_iota(jnp.int32, (t - r0, 1), 0) + r0
            dl = d_ref[r0:, :]
            bl = b_ref[r0:, :]
            for i in range(8):
                j = r0 + i
                inv = lax.rsqrt(dl[i:i + 1, j:j + 1])
                col = jnp.where(sub >= j, dl[:, j:j + 1] * inv, 0.0)
                lrow = jnp.where(lane >= j, dl[i:i + 1, :] * inv, 0.0)
                dl = dl - col * lrow
                brow = bl[i:i + 1, :] * inv
                bl = jnp.where(sub == j, brow, bl - jnp.where(sub > j, col, 0.0) * brow)
            d_ref[r0:, :] = dl
            b_ref[r0:, :] = bl
        m_ref[lo:lo + t, lo:lo + t] = b_ref[...]
        if k < nb - 1:
            hi = lo + t
            panel = _mm_t(a_ref[hi:, lo:lo + t], b_ref[...])
            l_ref[hi:, lo:lo + t] = panel
            a_ref[hi:, hi:] = a_ref[hi:, hi:] - _mm_t(panel, panel)
    for dist in range(1, nb):
        for i in range(dist, nb):
            j = i - dist
            acc = None
            for k in range(j, i):
                term = _mm(l_ref[i * t:(i + 1) * t, k * t:(k + 1) * t], m_ref[k * t:(k + 1) * t, j * t:(j + 1) * t])
                acc = term if acc is None else acc + term
            m_ref[i * t:(i + 1) * t, j * t:(j + 1) * t] = -_mm(m_ref[i * t:(i + 1) * t, i * t:(i + 1) * t], acc)


def chol_inverse(g, count, t=128):
    n = g.shape[0]
    vmem = pltpu.VMEM
    return pl.pallas_call(
        functools.partial(_chol_inv_kernel, count),
        out_shape=jax.ShapeDtypeStruct((n, n), jnp.float32),
        in_specs=[pl.BlockSpec(memory_space=vmem)],
        out_specs=pl.BlockSpec(memory_space=vmem),
        scratch_shapes=[
            vmem((n, n), jnp.float32),
            vmem((t, t), jnp.float32),
            vmem((t, t), jnp.float32),
            vmem((n, n), jnp.float32),
        ],
    )(g)


def gram_allreduce(g, dims):
    XL, Z, C, XH, Y = dims
    X = XL * XH
    ZH = Z // 2
    N, M = g.shape
    S1 = N // C
    S2 = S1 // Y
    S3 = S2 // X
    S4 = S3 // 2
    nsem = 4 + 2 * Y + 2 * X + ZH
    vmem = pltpu.VMEM
    return pl.pallas_call(
        functools.partial(_ar_kernel, dims),
        out_shape=jax.ShapeDtypeStruct((N, M), jnp.float32),
        in_specs=[pl.BlockSpec(memory_space=vmem)],
        out_specs=pl.BlockSpec(memory_space=vmem),
        scratch_shapes=[
            vmem((S1, M), jnp.float32),
            vmem((Y, S2, M), jnp.float32),
            vmem((X, S3, M), jnp.float32),
            vmem((S4, M), jnp.float32),
            vmem((ZH, S4, M), jnp.float32),
            vmem((S1, M), jnp.float32),
            vmem((S2, M), jnp.float32),
            vmem((S3, M), jnp.float32),
            vmem((S4, M), jnp.float32),
            vmem((N, M), jnp.float32),
            pltpu.SemaphoreType.DMA((nsem,)),
            pltpu.SemaphoreType.DMA((nsem,)),
        ],
        compiler_params=pltpu.CompilerParams(collective_id=0, has_side_effects=True),
    )(g)


def extended(x, sides, width):
    for axis, dim in sides:
        devices, length = (lax.axis_size(axis), x.shape[dim])
        up = [(i, (i + 1) % devices) for i in range(devices - 1)]
        down = [(j, i) for i, j in up]
        last = lax.slice_in_dim(x, length - width, length, axis=dim)
        first = lax.slice_in_dim(x, 0, width, axis=dim)
        before = lax.ppermute(last, axis, up)
        after = lax.ppermute(first, axis, down)
        x = jnp.concatenate([before, x, after], axis=dim)
    return x


def _dims():
    rows, blk = lax.axis_size("rows"), lax.axis_size("blk")
    return (2, rows // 4, 2, 2, blk // 2)


def local(cov_blocks, col_index, block_count, probes):
    rows_here, slots, block, _ = cov_blocks.shape
    tile_rows = probes.shape[0]
    probe_cols = probes.shape[1]
    zone_blocks = rows_here * lax.axis_size("blk")
    zone_number = lax.axis_index("rows")
    relative = col_index - (zone_number - 1) * zone_blocks
    window_blocks = 3 * zone_blocks
    inside = (relative >= 0) & (relative < window_blocks)
    slot_ids = lax.broadcasted_iota(jnp.int32, (rows_here, slots), 1)
    live_mask = inside & (slot_ids < block_count[:, None])
    column_ids = jnp.arange(window_blocks, dtype=jnp.int32)
    hits = (relative[:, :, None] == column_ids[None, None, :]) & live_mask[:, :, None]
    selector = hits.astype(jnp.bfloat16)
    window_matrix = jnp.einsum(
        "lsp,lsac->lapc", selector, cov_blocks, preferred_element_type=jnp.float32
    )
    window_matrix = window_matrix.astype(jnp.bfloat16).reshape(
        rows_here * block, window_blocks * block
    )

    def add_columns(running, shard_rows, first_row):
        length = shard_rows.shape[0]
        columns = lax.dynamic_slice_in_dim(window_matrix, first_row, length, 1)
        return running + jnp.dot(columns, shard_rows, preferred_element_type=jnp.float32)

    zeros_out = jnp.zeros((tile_rows, probe_cols), jnp.float32)
    own_zone = zone_gather(probes, lax.axis_size("blk"))
    zone_length = own_zone.shape[0]
    images = add_columns(zeros_out, own_zone, zone_length)
    near_zones = extended(own_zone, (("rows", 0),), zone_length)
    images = add_columns(images, lax.slice_in_dim(near_zones, 0, zone_length, axis=0), 0)
    images = add_columns(
        images,
        lax.slice_in_dim(near_zones, 2 * zone_length, 3 * zone_length, axis=0),
        2 * zone_length,
    )
    gram_local = lax.dot_general(
        images,
        images,
        (((0,), (0,)), ((), ())),
        precision=lax.Precision.HIGHEST,
        preferred_element_type=jnp.float32,
    )
    gram_total = gram_allreduce(gram_local, _dims())
    point_count = tile_rows * lax.axis_size("rows") * lax.axis_size("blk")
    factor_inverse = chol_inverse(gram_total, float(point_count))
    return _mm_t(images, factor_inverse)


def solution(mesh):
    return jax.shard_map(
        local,
        mesh=mesh,
        in_specs=(
            P(("rows", "blk"), None, None, None),
            P(("rows", "blk"), None),
            P(("rows", "blk")),
            P(("rows", "blk"), None),
        ),
        out_specs=P(("rows", "blk"), None),
        check_vma=False,
    )
```

```python
import functools
import jax
import jax.numpy as jnp
from jax import lax
from jax.experimental import pallas as pl
from jax.experimental.pallas import tpu as pltpu
from jax.sharding import PartitionSpec as P

MESH_ID = pl.DeviceIdType.MESH


def _ar_kernel(dims, g_ref, out_ref, rc, ry, rx, rzl, rzh, a1, a2, a3, a4, full, ssem, rsem):
    XL, Z, C, XH, Y = dims
    X = XL * XH
    ZH = Z // 2
    N = g_ref.shape[0]
    S1 = N // C
    S2 = S1 // Y
    S3 = S2 // X
    S4 = S3 // 2
    r = lax.axis_index("rows")
    b = lax.axis_index("blk")
    c = r % C
    z = (r // C) % Z
    xl = r // (C * Z)
    xh = b // Y
    y = b % Y
    x = xh * XL + xl
    zl = z % 2
    zh = z // 2

    def dev(c_, y_, x_, z_):
        return ((x_ % XL) * (Z * C) + z_ * C + c_, (x_ // XL) * Y + y_)

    core_peer = dev(1 - c, y, x, z)
    y_peers = [(y + k) % Y for k in range(1, Y)]
    x_peers = [(x + k) % X for k in range(1, X)]
    zl_peer = dev(c, y, x, zh * 2 + 1 - zl)
    zh_peers = [(zh + k) % ZH for k in range(1, ZH)]
    peers = [core_peer, zl_peer]
    peers += [dev(c, p, x, z) for p in y_peers]
    peers += [dev(c, y, p, z) for p in x_peers]
    peers += [dev(c, y, x, p * 2 + zl) for p in zh_peers]

    barrier = pltpu.get_barrier_semaphore()
    for p in peers:
        pl.semaphore_signal(barrier, inc=1, device_id=p, device_id_type=MESH_ID)
    pl.semaphore_wait(barrier, len(peers))

    o_core, o_y, o_x, o_zl, o_zh = 0, 1, 1 + Y, 1 + Y + X, 2 + Y + X
    o_agzl, o_agx, o_agy, o_agc = 2 + Y + X + ZH, 3 + Y + X + ZH, 3 + Y + 2 * X + ZH, 3 + 2 * Y + 2 * X + ZH

    def send(src, dst, sidx, ridx, peer):
        d = pltpu.make_async_remote_copy(
            src_ref=src, dst_ref=dst, send_sem=ssem.at[sidx], recv_sem=rsem.at[ridx],
            device_id=peer, device_id_type=MESH_ID)
        d.start()
        return d

    def wait_recv(src, dst, ridx, peer):
        pltpu.make_async_remote_copy(
            src_ref=src, dst_ref=dst, send_sem=ssem.at[0], recv_sem=rsem.at[ridx],
            device_id=peer, device_id_type=MESH_ID).wait_recv()

    def rows(start, size):
        return pl.ds(pl.multiple_of(start, 8), size)

    d = send(g_ref.at[rows((1 - c) * S1, S1)], rc, o_core, o_core, core_peer)
    wait_recv(g_ref.at[rows(c * S1, S1)], rc, o_core, core_peer)
    d.wait_send()
    a1[...] = g_ref[rows(c * S1, S1), :] + rc[...]

    ds = [send(a1.at[rows(p * S2, S2)], ry.at[y], o_y + k, o_y + y, dev(c, p, x, z))
          for k, p in enumerate(y_peers)]
    for k in range(1, Y):
        s = (y - k + Y) % Y
        wait_recv(a1.at[rows(0, S2)], ry.at[s], o_y + s, dev(c, s, x, z))
    for d in ds:
        d.wait_send()
    acc = a1[rows(y * S2, S2), :]
    for k in range(1, Y):
        acc = acc + ry[(y - k + Y) % Y]
    a2[...] = acc

    ds = [send(a2.at[rows(p * S3, S3)], rx.at[x], o_x + k, o_x + x, dev(c, y, p, z))
          for k, p in enumerate(x_peers)]
    for k in range(1, X):
        s = (x - k + X) % X
        wait_recv(a2.at[rows(0, S3)], rx.at[s], o_x + s, dev(c, y, s, z))
    for d in ds:
        d.wait_send()
    acc = a2[rows(x * S3, S3), :]
    for k in range(1, X):
        acc = acc + rx[(x - k + X) % X]
    a3[...] = acc

    d = send(a3.at[rows((1 - zl) * S4, S4)], rzl, o_zl, o_zl, zl_peer)
    wait_recv(a3.at[rows(zl * S4, S4)], rzl, o_zl, zl_peer)
    d.wait_send()
    a4[...] = a3[rows(zl * S4, S4), :] + rzl[...]

    ds = [send(a4, rzh.at[zh], o_zh + k, o_zh + zh, dev(c, y, x, p * 2 + zl))
          for k, p in enumerate(zh_peers)]
    rzh[zh] = a4[...]
    for k in range(1, ZH):
        s = (zh - k + ZH) % ZH
        wait_recv(a4, rzh.at[s], o_zh + s, dev(c, y, x, s * 2 + zl))
    for d in ds:
        d.wait_send()
    acc = rzh[0]
    for j in range(1, ZH):
        acc = acc + rzh[j]
    base = c * S1 + y * S2 + x * S3
    full[rows(base + zl * S4, S4), :] = acc

    mine = rows(base + zl * S4, S4)
    d = send(full.at[mine], full.at[mine], o_agzl, o_agzl, zl_peer)
    wait_recv(full.at[mine], full.at[rows(base + (1 - zl) * S4, S4)], o_agzl, zl_peer)
    d.wait_send()

    mine = rows(c * S1 + y * S2 + x * S3, S3)
    ds = [send(full.at[mine], full.at[mine], o_agx + k, o_agx + x, dev(c, y, p, z))
          for k, p in enumerate(x_peers)]
    for k in range(1, X):
        s = (x - k + X) % X
        wait_recv(full.at[mine], full.at[rows(c * S1 + y * S2 + s * S3, S3)], o_agx + s, dev(c, y, s, z))
    for d in ds:
        d.wait_send()

    mine = rows(c * S1 + y * S2, S2)
    ds = [send(full.at[mine], full.at[mine], o_agy + k, o_agy + y, dev(c, p, x, z))
          for k, p in enumerate(y_peers)]
    for k in range(1, Y):
        s = (y - k + Y) % Y
        wait_recv(full.at[mine], full.at[rows(c * S1 + s * S2, S2)], o_agy + s, dev(c, s, x, z))
    for d in ds:
        d.wait_send()

    mine = rows(c * S1, S1)
    d = send(full.at[mine], full.at[mine], o_agc, o_agc, core_peer)
    wait_recv(full.at[mine], full.at[rows((1 - c) * S1, S1)], o_agc, core_peer)
    d.wait_send()

    if out_ref is not None:
        out_ref[...] = full[...]


def _zone_gather_kernel(nb, p_ref, out_ref, ssem, rsem, lsem):
    T = p_ref.shape[0]
    r = lax.axis_index("rows")
    b = lax.axis_index("blk")
    barrier = pltpu.get_barrier_semaphore()
    for k in range(1, nb):
        pl.semaphore_signal(barrier, inc=1, device_id=(r, (b + k) % nb), device_id_type=MESH_ID)
    pl.semaphore_wait(barrier, nb - 1)
    here = pl.ds(pl.multiple_of(b * T, 8), T)
    ds = []
    for k in range(1, nb):
        d = pltpu.make_async_remote_copy(
            src_ref=p_ref, dst_ref=out_ref.at[here], send_sem=ssem.at[k - 1], recv_sem=rsem.at[b],
            device_id=(r, (b + k) % nb), device_id_type=MESH_ID)
        d.start()
        ds.append(d)
    own = pltpu.make_async_copy(p_ref, out_ref.at[here], lsem.at[0])
    own.start()
    for k in range(1, nb):
        s = (b - k + nb) % nb
        pltpu.make_async_remote_copy(
            src_ref=p_ref, dst_ref=out_ref.at[pl.ds(pl.multiple_of(s * T, 8), T)], send_sem=ssem.at[0],
            recv_sem=rsem.at[s], device_id=(r, s), device_id_type=MESH_ID).wait_recv()
    for d in ds:
        d.wait_send()
    own.wait()


def zone_gather(p, nb):
    T, K = p.shape
    return pl.pallas_call(
        functools.partial(_zone_gather_kernel, nb),
        out_shape=jax.ShapeDtypeStruct((nb * T, K), p.dtype),
        in_specs=[pl.BlockSpec(memory_space=pl.ANY)],
        out_specs=pl.BlockSpec(memory_space=pl.ANY),
        scratch_shapes=[
            pltpu.SemaphoreType.DMA((nb - 1,)),
            pltpu.SemaphoreType.DMA((nb,)),
            pltpu.SemaphoreType.DMA((1,)),
        ],
        compiler_params=pltpu.CompilerParams(collective_id=1, has_side_effects=True),
    )(p)


HI = lax.Precision.HIGHEST


def _mm(a, b):
    return jnp.dot(a, b, precision=HI, preferred_element_type=jnp.float32)


def _mm_t(a, b):
    return lax.dot_general(a, b, (((1,), (1,)), ((), ())), precision=HI, preferred_element_type=jnp.float32)


def _chol_inv_kernel(count, g_ref, m_ref, a_ref, d_ref, b_ref, l_ref):
    n = g_ref.shape[0]
    t = d_ref.shape[0]
    nb = n // t
    gram = g_ref[...] / count
    a_ref[...] = (gram + gram.T) / 2
    m_ref[...] = jnp.zeros_like(m_ref)
    lane = lax.broadcasted_iota(jnp.int32, (1, t), 1)
    eye = (lax.broadcasted_iota(jnp.int32, (t, t), 0) == lax.broadcasted_iota(jnp.int32, (t, t), 1)).astype(jnp.float32)

    for k in range(nb):
        lo = k * t
        d_ref[...] = a_ref[lo:lo + t, lo:lo + t]
        b_ref[...] = eye
        for r0 in range(0, t, 8):
            sub = lax.broadcasted_iota(jnp.int32, (t - r0, 1), 0) + r0
            dl = d_ref[r0:, :]
            bl = b_ref[r0:, :]
            for i in range(8):
                j = r0 + i
                inv = lax.rsqrt(dl[i:i + 1, j:j + 1])
                col = jnp.where(sub >= j, dl[:, j:j + 1] * inv, 0.0)
                lrow = jnp.where(lane >= j, dl[i:i + 1, :] * inv, 0.0)
                dl = dl - col * lrow
                brow = bl[i:i + 1, :] * inv
                bl = jnp.where(sub == j, brow, bl - jnp.where(sub > j, col, 0.0) * brow)
            d_ref[r0:, :] = dl
            b_ref[r0:, :] = bl
        m_ref[lo:lo + t, lo:lo + t] = b_ref[...]
        if k < nb - 1:
            hi = lo + t
            panel = _mm_t(a_ref[hi:, lo:lo + t], b_ref[...])
            l_ref[hi:, lo:lo + t] = panel
            a_ref[hi:, hi:] = a_ref[hi:, hi:] - _mm_t(panel, panel)
    for dist in range(1, nb):
        for i in range(dist, nb):
            j = i - dist
            acc = None
            for k in range(j, i):
                term = _mm(l_ref[i * t:(i + 1) * t, k * t:(k + 1) * t], m_ref[k * t:(k + 1) * t, j * t:(j + 1) * t])
                acc = term if acc is None else acc + term
            m_ref[i * t:(i + 1) * t, j * t:(j + 1) * t] = -_mm(m_ref[i * t:(i + 1) * t, i * t:(i + 1) * t], acc)


def gram_factor_inverse(g, dims, count, t=128):
    XL, Z, C, XH, Y = dims
    X = XL * XH
    ZH = Z // 2
    N, M = g.shape
    S1 = N // C
    S2 = S1 // Y
    S3 = S2 // X
    S4 = S3 // 2
    nsem = 4 + 2 * Y + 2 * X + ZH
    vmem = pltpu.VMEM

    def kernel(g_ref, m_ref, rc, ry, rx, rzl, rzh, a1, a2, a3, a4, full, ssem, rsem, ca, cd, cb, cl):
        _ar_kernel(dims, g_ref, None, rc, ry, rx, rzl, rzh, a1, a2, a3, a4, full, ssem, rsem)
        _chol_inv_kernel(count, full, m_ref, ca, cd, cb, cl)

    return pl.pallas_call(
        kernel,
        out_shape=jax.ShapeDtypeStruct((N, M), jnp.float32),
        in_specs=[pl.BlockSpec(memory_space=vmem)],
        out_specs=pl.BlockSpec(memory_space=vmem),
        scratch_shapes=[
            vmem((S1, M), jnp.float32),
            vmem((Y, S2, M), jnp.float32),
            vmem((X, S3, M), jnp.float32),
            vmem((S4, M), jnp.float32),
            vmem((ZH, S4, M), jnp.float32),
            vmem((S1, M), jnp.float32),
            vmem((S2, M), jnp.float32),
            vmem((S3, M), jnp.float32),
            vmem((S4, M), jnp.float32),
            vmem((N, M), jnp.float32),
            pltpu.SemaphoreType.DMA((nsem,)),
            pltpu.SemaphoreType.DMA((nsem,)),
            vmem((N, N), jnp.float32),
            vmem((t, t), jnp.float32),
            vmem((t, t), jnp.float32),
            vmem((N, N), jnp.float32),
        ],
        compiler_params=pltpu.CompilerParams(collective_id=0, has_side_effects=True),
    )(g)


def extended(x, sides, width):
    for axis, dim in sides:
        devices, length = (lax.axis_size(axis), x.shape[dim])
        up = [(i, (i + 1) % devices) for i in range(devices - 1)]
        down = [(j, i) for i, j in up]
        last = lax.slice_in_dim(x, length - width, length, axis=dim)
        first = lax.slice_in_dim(x, 0, width, axis=dim)
        before = lax.ppermute(last, axis, up)
        after = lax.ppermute(first, axis, down)
        x = jnp.concatenate([before, x, after], axis=dim)
    return x


def _dims():
    rows, blk = lax.axis_size("rows"), lax.axis_size("blk")
    return (2, rows // 4, 2, 2, blk // 2)


def local(cov_blocks, col_index, block_count, probes):
    rows_here, slots, block, _ = cov_blocks.shape
    tile_rows = probes.shape[0]
    probe_cols = probes.shape[1]
    zone_blocks = rows_here * lax.axis_size("blk")
    zone_number = lax.axis_index("rows")
    relative = col_index - (zone_number - 1) * zone_blocks
    window_blocks = 3 * zone_blocks
    inside = (relative >= 0) & (relative < window_blocks)
    slot_ids = lax.broadcasted_iota(jnp.int32, (rows_here, slots), 1)
    live_mask = inside & (slot_ids < block_count[:, None])
    column_ids = jnp.arange(window_blocks, dtype=jnp.int32)
    hits = (relative[:, :, None] == column_ids[None, None, :]) & live_mask[:, :, None]
    selector = hits.astype(jnp.bfloat16)
    window_matrix = jnp.einsum(
        "lsp,lsac->lapc", selector, cov_blocks, preferred_element_type=jnp.float32
    )
    window_matrix = window_matrix.astype(jnp.bfloat16).reshape(
        rows_here * block, window_blocks * block
    )

    def add_columns(running, shard_rows, first_row):
        length = shard_rows.shape[0]
        columns = lax.dynamic_slice_in_dim(window_matrix, first_row, length, 1)
        return running + jnp.dot(columns, shard_rows, preferred_element_type=jnp.float32)

    zeros_out = jnp.zeros((tile_rows, probe_cols), jnp.float32)
    own_zone = zone_gather(probes, lax.axis_size("blk"))
    zone_length = own_zone.shape[0]
    images = add_columns(zeros_out, own_zone, zone_length)
    near_zones = extended(own_zone, (("rows", 0),), zone_length)
    images = add_columns(images, lax.slice_in_dim(near_zones, 0, zone_length, axis=0), 0)
    images = add_columns(
        images,
        lax.slice_in_dim(near_zones, 2 * zone_length, 3 * zone_length, axis=0),
        2 * zone_length,
    )
    gram_local = lax.dot_general(
        images,
        images,
        (((0,), (0,)), ((), ())),
        precision=lax.Precision.HIGHEST,
        preferred_element_type=jnp.float32,
    )
    point_count = tile_rows * lax.axis_size("rows") * lax.axis_size("blk")
    factor_inverse = gram_factor_inverse(gram_local, _dims(), float(point_count))
    return _mm_t(images, factor_inverse)


def solution(mesh):
    return jax.shard_map(
        local,
        mesh=mesh,
        in_specs=(
            P(("rows", "blk"), None, None, None),
            P(("rows", "blk"), None),
            P(("rows", "blk")),
            P(("rows", "blk"), None),
        ),
        out_specs=P(("rows", "blk"), None),
        check_vma=False,
    )
```

```python
import functools
import jax
import jax.numpy as jnp
from jax import lax
from jax.experimental import pallas as pl
from jax.experimental.pallas import tpu as pltpu
from jax.sharding import PartitionSpec as P

MESH_ID = pl.DeviceIdType.MESH


def _ar_kernel(dims, g_ref, out_ref, rc, ry, rx, rzl, rzh, a1, a2, a3, a4, full, ssem, rsem):
    XL, Z, C, XH, Y = dims
    X = XL * XH
    ZH = Z // 2
    N = g_ref.shape[0]
    S1 = N // C
    S2 = S1 // Y
    S3 = S2 // X
    S4 = S3 // 2
    r = lax.axis_index("rows")
    b = lax.axis_index("blk")
    c = r % C
    z = (r // C) % Z
    xl = r // (C * Z)
    xh = b // Y
    y = b % Y
    x = xh * XL + xl
    zl = z % 2
    zh = z // 2

    def dev(c_, y_, x_, z_):
        return ((x_ % XL) * (Z * C) + z_ * C + c_, (x_ // XL) * Y + y_)

    core_peer = dev(1 - c, y, x, z)
    y_peers = [(y + k) % Y for k in range(1, Y)]
    x_peers = [(x + k) % X for k in range(1, X)]
    zl_peer = dev(c, y, x, zh * 2 + 1 - zl)
    zh_peers = [(zh + k) % ZH for k in range(1, ZH)]
    peers = [core_peer, zl_peer]
    peers += [dev(c, p, x, z) for p in y_peers]
    peers += [dev(c, y, p, z) for p in x_peers]
    peers += [dev(c, y, x, p * 2 + zl) for p in zh_peers]

    barrier = pltpu.get_barrier_semaphore()
    for p in peers:
        pl.semaphore_signal(barrier, inc=1, device_id=p, device_id_type=MESH_ID)
    pl.semaphore_wait(barrier, len(peers))

    o_core, o_y, o_x, o_zl, o_zh = 0, 1, 1 + Y, 1 + Y + X, 2 + Y + X
    o_agzl, o_agx, o_agy, o_agc = 2 + Y + X + ZH, 3 + Y + X + ZH, 3 + Y + 2 * X + ZH, 3 + 2 * Y + 2 * X + ZH

    def send(src, dst, sidx, ridx, peer):
        d = pltpu.make_async_remote_copy(
            src_ref=src, dst_ref=dst, send_sem=ssem.at[sidx], recv_sem=rsem.at[ridx],
            device_id=peer, device_id_type=MESH_ID)
        d.start()
        return d

    def wait_recv(src, dst, ridx, peer):
        pltpu.make_async_remote_copy(
            src_ref=src, dst_ref=dst, send_sem=ssem.at[0], recv_sem=rsem.at[ridx],
            device_id=peer, device_id_type=MESH_ID).wait_recv()

    def rows(start, size):
        return pl.ds(pl.multiple_of(start, 8), size)

    d = send(g_ref.at[rows((1 - c) * S1, S1)], rc, o_core, o_core, core_peer)
    wait_recv(g_ref.at[rows(c * S1, S1)], rc, o_core, core_peer)
    d.wait_send()
    a1[...] = g_ref[rows(c * S1, S1), :] + rc[...]

    ds = [send(a1.at[rows(p * S2, S2)], ry.at[y], o_y + k, o_y + y, dev(c, p, x, z))
          for k, p in enumerate(y_peers)]
    for k in range(1, Y):
        s = (y - k + Y) % Y
        wait_recv(a1.at[rows(0, S2)], ry.at[s], o_y + s, dev(c, s, x, z))
    for d in ds:
        d.wait_send()
    acc = a1[rows(y * S2, S2), :]
    for k in range(1, Y):
        acc = acc + ry[(y - k + Y) % Y]
    a2[...] = acc

    ds = [send(a2.at[rows(p * S3, S3)], rx.at[x], o_x + k, o_x + x, dev(c, y, p, z))
          for k, p in enumerate(x_peers)]
    for k in range(1, X):
        s = (x - k + X) % X
        wait_recv(a2.at[rows(0, S3)], rx.at[s], o_x + s, dev(c, y, s, z))
    for d in ds:
        d.wait_send()
    acc = a2[rows(x * S3, S3), :]
    for k in range(1, X):
        acc = acc + rx[(x - k + X) % X]
    a3[...] = acc

    d = send(a3.at[rows((1 - zl) * S4, S4)], rzl, o_zl, o_zl, zl_peer)
    wait_recv(a3.at[rows(zl * S4, S4)], rzl, o_zl, zl_peer)
    d.wait_send()
    a4[...] = a3[rows(zl * S4, S4), :] + rzl[...]

    ds = [send(a4, rzh.at[zh], o_zh + k, o_zh + zh, dev(c, y, x, p * 2 + zl))
          for k, p in enumerate(zh_peers)]
    rzh[zh] = a4[...]
    for k in range(1, ZH):
        s = (zh - k + ZH) % ZH
        wait_recv(a4, rzh.at[s], o_zh + s, dev(c, y, x, s * 2 + zl))
    for d in ds:
        d.wait_send()
    acc = rzh[0]
    for j in range(1, ZH):
        acc = acc + rzh[j]
    base = c * S1 + y * S2 + x * S3
    full[rows(base + zl * S4, S4), :] = acc

    mine = rows(base + zl * S4, S4)
    d = send(full.at[mine], full.at[mine], o_agzl, o_agzl, zl_peer)
    wait_recv(full.at[mine], full.at[rows(base + (1 - zl) * S4, S4)], o_agzl, zl_peer)
    d.wait_send()

    mine = rows(c * S1 + y * S2 + x * S3, S3)
    ds = [send(full.at[mine], full.at[mine], o_agx + k, o_agx + x, dev(c, y, p, z))
          for k, p in enumerate(x_peers)]
    for k in range(1, X):
        s = (x - k + X) % X
        wait_recv(full.at[mine], full.at[rows(c * S1 + y * S2 + s * S3, S3)], o_agx + s, dev(c, y, s, z))
    for d in ds:
        d.wait_send()

    mine = rows(c * S1 + y * S2, S2)
    ds = [send(full.at[mine], full.at[mine], o_agy + k, o_agy + y, dev(c, p, x, z))
          for k, p in enumerate(y_peers)]
    for k in range(1, Y):
        s = (y - k + Y) % Y
        wait_recv(full.at[mine], full.at[rows(c * S1 + s * S2, S2)], o_agy + s, dev(c, s, x, z))
    for d in ds:
        d.wait_send()

    mine = rows(c * S1, S1)
    d = send(full.at[mine], full.at[mine], o_agc, o_agc, core_peer)
    wait_recv(full.at[mine], full.at[rows((1 - c) * S1, S1)], o_agc, core_peer)
    d.wait_send()

    if out_ref is not None:
        out_ref[...] = full[...]


def _zone_gather_kernel(nb, p_ref, out_ref, ssem, rsem, lsem):
    T = p_ref.shape[0]
    r = lax.axis_index("rows")
    b = lax.axis_index("blk")
    barrier = pltpu.get_barrier_semaphore()
    for k in range(1, nb):
        pl.semaphore_signal(barrier, inc=1, device_id=(r, (b + k) % nb), device_id_type=MESH_ID)
    pl.semaphore_wait(barrier, nb - 1)
    here = pl.ds(pl.multiple_of(b * T, 8), T)
    ds = []
    for k in range(1, nb):
        d = pltpu.make_async_remote_copy(
            src_ref=p_ref, dst_ref=out_ref.at[here], send_sem=ssem.at[k - 1], recv_sem=rsem.at[b],
            device_id=(r, (b + k) % nb), device_id_type=MESH_ID)
        d.start()
        ds.append(d)
    own = pltpu.make_async_copy(p_ref, out_ref.at[here], lsem.at[0])
    own.start()
    for k in range(1, nb):
        s = (b - k + nb) % nb
        pltpu.make_async_remote_copy(
            src_ref=p_ref, dst_ref=out_ref.at[pl.ds(pl.multiple_of(s * T, 8), T)], send_sem=ssem.at[0],
            recv_sem=rsem.at[s], device_id=(r, s), device_id_type=MESH_ID).wait_recv()
    for d in ds:
        d.wait_send()
    own.wait()


def zone_gather(p, nb):
    T, K = p.shape
    return pl.pallas_call(
        functools.partial(_zone_gather_kernel, nb),
        out_shape=jax.ShapeDtypeStruct((nb * T, K), p.dtype),
        in_specs=[pl.BlockSpec(memory_space=pl.ANY)],
        out_specs=pl.BlockSpec(memory_space=pl.ANY),
        scratch_shapes=[
            pltpu.SemaphoreType.DMA((nb - 1,)),
            pltpu.SemaphoreType.DMA((nb,)),
            pltpu.SemaphoreType.DMA((1,)),
        ],
        compiler_params=pltpu.CompilerParams(collective_id=1, has_side_effects=True),
    )(p)


HI = lax.Precision.HIGHEST


def _mm(a, b):
    return jnp.dot(a, b, precision=HI, preferred_element_type=jnp.float32)


def _mm_t(a, b):
    return lax.dot_general(a, b, (((1,), (1,)), ((), ())), precision=HI, preferred_element_type=jnp.float32)


def _chol_inv_kernel(count, g_ref, m_ref, a_ref, d_ref, b_ref, l_ref):
    n = g_ref.shape[0]
    t = d_ref.shape[0]
    nb = n // t
    gram = g_ref[...] / count
    a_ref[...] = (gram + gram.T) / 2
    m_ref[...] = jnp.zeros_like(m_ref)
    lane = lax.broadcasted_iota(jnp.int32, (1, t), 1)
    eye = (lax.broadcasted_iota(jnp.int32, (t, t), 0) == lax.broadcasted_iota(jnp.int32, (t, t), 1)).astype(jnp.float32)

    for k in range(nb):
        lo = k * t
        d_ref[...] = a_ref[lo:lo + t, lo:lo + t]
        b_ref[...] = eye
        dl = d_ref[...]
        bl = b_ref[...]
        sub = lax.broadcasted_iota(jnp.int32, (t, 1), 0)
        inv = lax.rsqrt(dl[0:1, 0:1])
        col = jnp.where(sub >= 0, dl[:, 0:1] * inv, 0.0)
        lrow = jnp.where(lane >= 0, dl[0:1, :] * inv, 0.0)
        for r0 in range(0, t, 8):
            if r0:
                d_ref[r0 - 8:, :] = dl
                b_ref[r0 - 8:, :] = bl
                dl = d_ref[r0:, :]
                bl = b_ref[r0:, :]
                col = col[8:]
                sub = lax.broadcasted_iota(jnp.int32, (t - r0, 1), 0) + r0
            for i in range(8):
                j = r0 + i
                if j + 1 < t:
                    raw_col = dl[:, j + 1:j + 2]
                    raw_row = dl[i + 1:i + 2, :]
                dl = dl - col * lrow
                brow = bl[i:i + 1, :] * inv
                bl = jnp.where(sub == j, brow, bl - jnp.where(sub > j, col, 0.0) * brow)
                if j + 1 < t:
                    new_col = raw_col - col * lrow[:, j + 1:j + 2]
                    new_row = raw_row - col[i + 1:i + 2, :] * lrow
                    inv = lax.rsqrt(new_row[:, j + 1:j + 2])
                    col = jnp.where(sub >= j + 1, new_col * inv, 0.0)
                    lrow = jnp.where(lane >= j + 1, new_row * inv, 0.0)
        d_ref[t - 8:, :] = dl
        b_ref[t - 8:, :] = bl
        m_ref[lo:lo + t, lo:lo + t] = b_ref[...]
        if k < nb - 1:
            hi = lo + t
            panel = _mm_t(a_ref[hi:, lo:lo + t], b_ref[...])
            l_ref[hi:, lo:lo + t] = panel
            a_ref[hi:, hi:] = a_ref[hi:, hi:] - _mm_t(panel, panel)
    for dist in range(1, nb):
        for i in range(dist, nb):
            j = i - dist
            acc = None
            for k in range(j, i):
                term = _mm(l_ref[i * t:(i + 1) * t, k * t:(k + 1) * t], m_ref[k * t:(k + 1) * t, j * t:(j + 1) * t])
                acc = term if acc is None else acc + term
            m_ref[i * t:(i + 1) * t, j * t:(j + 1) * t] = -_mm(m_ref[i * t:(i + 1) * t, i * t:(i + 1) * t], acc)


def gram_factor_inverse(g, dims, count, t=128):
    XL, Z, C, XH, Y = dims
    X = XL * XH
    ZH = Z // 2
    N, M = g.shape
    S1 = N // C
    S2 = S1 // Y
    S3 = S2 // X
    S4 = S3 // 2
    nsem = 4 + 2 * Y + 2 * X + ZH
    vmem = pltpu.VMEM

    def kernel(g_ref, m_ref, rc, ry, rx, rzl, rzh, a1, a2, a3, a4, full, ssem, rsem, ca, cd, cb, cl):
        _ar_kernel(dims, g_ref, None, rc, ry, rx, rzl, rzh, a1, a2, a3, a4, full, ssem, rsem)
        _chol_inv_kernel(count, full, m_ref, ca, cd, cb, cl)

    return pl.pallas_call(
        kernel,
        out_shape=jax.ShapeDtypeStruct((N, M), jnp.float32),
        in_specs=[pl.BlockSpec(memory_space=vmem)],
        out_specs=pl.BlockSpec(memory_space=vmem),
        scratch_shapes=[
            vmem((S1, M), jnp.float32),
            vmem((Y, S2, M), jnp.float32),
            vmem((X, S3, M), jnp.float32),
            vmem((S4, M), jnp.float32),
            vmem((ZH, S4, M), jnp.float32),
            vmem((S1, M), jnp.float32),
            vmem((S2, M), jnp.float32),
            vmem((S3, M), jnp.float32),
            vmem((S4, M), jnp.float32),
            vmem((N, M), jnp.float32),
            pltpu.SemaphoreType.DMA((nsem,)),
            pltpu.SemaphoreType.DMA((nsem,)),
            vmem((N, N), jnp.float32),
            vmem((t, t), jnp.float32),
            vmem((t, t), jnp.float32),
            vmem((N, N), jnp.float32),
        ],
        compiler_params=pltpu.CompilerParams(collective_id=0, has_side_effects=True),
    )(g)


def extended(x, sides, width):
    for axis, dim in sides:
        devices, length = (lax.axis_size(axis), x.shape[dim])
        up = [(i, (i + 1) % devices) for i in range(devices - 1)]
        down = [(j, i) for i, j in up]
        last = lax.slice_in_dim(x, length - width, length, axis=dim)
        first = lax.slice_in_dim(x, 0, width, axis=dim)
        before = lax.ppermute(last, axis, up)
        after = lax.ppermute(first, axis, down)
        x = jnp.concatenate([before, x, after], axis=dim)
    return x


def _dims():
    rows, blk = lax.axis_size("rows"), lax.axis_size("blk")
    return (2, rows // 4, 2, 2, blk // 2)


def local(cov_blocks, col_index, block_count, probes):
    rows_here, slots, block, _ = cov_blocks.shape
    tile_rows = probes.shape[0]
    probe_cols = probes.shape[1]
    zone_blocks = rows_here * lax.axis_size("blk")
    zone_number = lax.axis_index("rows")
    relative = col_index - (zone_number - 1) * zone_blocks
    window_blocks = 3 * zone_blocks
    inside = (relative >= 0) & (relative < window_blocks)
    slot_ids = lax.broadcasted_iota(jnp.int32, (rows_here, slots), 1)
    live_mask = inside & (slot_ids < block_count[:, None])
    column_ids = jnp.arange(window_blocks, dtype=jnp.int32)
    hits = (relative[:, :, None] == column_ids[None, None, :]) & live_mask[:, :, None]
    selector = hits.astype(jnp.bfloat16)
    window_matrix = jnp.einsum(
        "lsp,lsac->lapc", selector, cov_blocks, preferred_element_type=jnp.float32
    )
    window_matrix = window_matrix.astype(jnp.bfloat16).reshape(
        rows_here * block, window_blocks * block
    )

    def add_columns(running, shard_rows, first_row):
        length = shard_rows.shape[0]
        columns = lax.dynamic_slice_in_dim(window_matrix, first_row, length, 1)
        return running + jnp.dot(columns, shard_rows, preferred_element_type=jnp.float32)

    zeros_out = jnp.zeros((tile_rows, probe_cols), jnp.float32)
    own_zone = zone_gather(probes, lax.axis_size("blk"))
    zone_length = own_zone.shape[0]
    images = add_columns(zeros_out, own_zone, zone_length)
    near_zones = extended(own_zone, (("rows", 0),), zone_length)
    images = add_columns(images, lax.slice_in_dim(near_zones, 0, zone_length, axis=0), 0)
    images = add_columns(
        images,
        lax.slice_in_dim(near_zones, 2 * zone_length, 3 * zone_length, axis=0),
        2 * zone_length,
    )
    gram_local = lax.dot_general(
        images,
        images,
        (((0,), (0,)), ((), ())),
        precision=lax.Precision.HIGHEST,
        preferred_element_type=jnp.float32,
    )
    point_count = tile_rows * lax.axis_size("rows") * lax.axis_size("blk")
    factor_inverse = gram_factor_inverse(gram_local, _dims(), float(point_count))
    return _mm_t(images, factor_inverse)


def solution(mesh):
    return jax.shard_map(
        local,
        mesh=mesh,
        in_specs=(
            P(("rows", "blk"), None, None, None),
            P(("rows", "blk"), None),
            P(("rows", "blk")),
            P(("rows", "blk"), None),
        ),
        out_specs=P(("rows", "blk"), None),
        check_vma=False,
    )
```

```python
import functools
import jax
import jax.numpy as jnp
from jax import lax
from jax.experimental import pallas as pl
from jax.experimental.pallas import tpu as pltpu
from jax.sharding import PartitionSpec as P

MESH_ID = pl.DeviceIdType.MESH


def _ar_kernel(dims, g_ref, out_ref, rc, ry, rx, rzl, rzh, a1, a2, a3, a4, full, ssem, rsem):
    XL, Z, C, XH, Y = dims
    X = XL * XH
    ZH = Z // 2
    N = g_ref.shape[0]
    S1 = N // C
    S2 = S1 // Y
    S3 = S2 // X
    S4 = S3 // 2
    r = lax.axis_index("rows")
    b = lax.axis_index("blk")
    c = r % C
    z = (r // C) % Z
    xl = r // (C * Z)
    xh = b // Y
    y = b % Y
    x = xh * XL + xl
    zl = z % 2
    zh = z // 2

    def dev(c_, y_, x_, z_):
        return ((x_ % XL) * (Z * C) + z_ * C + c_, (x_ // XL) * Y + y_)

    core_peer = dev(1 - c, y, x, z)
    y_peers = [(y + k) % Y for k in range(1, Y)]
    x_peers = [(x + k) % X for k in range(1, X)]
    zl_peer = dev(c, y, x, zh * 2 + 1 - zl)
    zh_peers = [(zh + k) % ZH for k in range(1, ZH)]
    peers = [core_peer, zl_peer]
    peers += [dev(c, p, x, z) for p in y_peers]
    peers += [dev(c, y, p, z) for p in x_peers]
    peers += [dev(c, y, x, p * 2 + zl) for p in zh_peers]

    barrier = pltpu.get_barrier_semaphore()
    for p in peers:
        pl.semaphore_signal(barrier, inc=1, device_id=p, device_id_type=MESH_ID)
    pl.semaphore_wait(barrier, len(peers))

    o_core, o_y, o_x, o_zl, o_zh = 0, 1, 1 + Y, 1 + Y + X, 2 + Y + X
    o_agzl, o_agx, o_agy, o_agc = 2 + Y + X + ZH, 3 + Y + X + ZH, 3 + Y + 2 * X + ZH, 3 + 2 * Y + 2 * X + ZH

    def send(src, dst, sidx, ridx, peer):
        d = pltpu.make_async_remote_copy(
            src_ref=src, dst_ref=dst, send_sem=ssem.at[sidx], recv_sem=rsem.at[ridx],
            device_id=peer, device_id_type=MESH_ID)
        d.start()
        return d

    def wait_recv(src, dst, ridx, peer):
        pltpu.make_async_remote_copy(
            src_ref=src, dst_ref=dst, send_sem=ssem.at[0], recv_sem=rsem.at[ridx],
            device_id=peer, device_id_type=MESH_ID).wait_recv()

    def rows(start, size):
        return pl.ds(pl.multiple_of(start, 8), size)

    d = send(g_ref.at[rows((1 - c) * S1, S1)], rc, o_core, o_core, core_peer)
    wait_recv(g_ref.at[rows(c * S1, S1)], rc, o_core, core_peer)
    d.wait_send()
    a1[...] = g_ref[rows(c * S1, S1), :] + rc[...]

    ds = [send(a1.at[rows(p * S2, S2)], ry.at[y], o_y + k, o_y + y, dev(c, p, x, z))
          for k, p in enumerate(y_peers)]
    for k in range(1, Y):
        s = (y - k + Y) % Y
        wait_recv(a1.at[rows(0, S2)], ry.at[s], o_y + s, dev(c, s, x, z))
    for d in ds:
        d.wait_send()
    acc = a1[rows(y * S2, S2), :]
    for k in range(1, Y):
        acc = acc + ry[(y - k + Y) % Y]
    a2[...] = acc

    ds = [send(a2.at[rows(p * S3, S3)], rx.at[x], o_x + k, o_x + x, dev(c, y, p, z))
          for k, p in enumerate(x_peers)]
    for k in range(1, X):
        s = (x - k + X) % X
        wait_recv(a2.at[rows(0, S3)], rx.at[s], o_x + s, dev(c, y, s, z))
    for d in ds:
        d.wait_send()
    acc = a2[rows(x * S3, S3), :]
    for k in range(1, X):
        acc = acc + rx[(x - k + X) % X]
    a3[...] = acc

    d = send(a3.at[rows((1 - zl) * S4, S4)], rzl, o_zl, o_zl, zl_peer)
    wait_recv(a3.at[rows(zl * S4, S4)], rzl, o_zl, zl_peer)
    d.wait_send()
    a4[...] = a3[rows(zl * S4, S4), :] + rzl[...]

    ds = [send(a4, rzh.at[zh], o_zh + k, o_zh + zh, dev(c, y, x, p * 2 + zl))
          for k, p in enumerate(zh_peers)]
    rzh[zh] = a4[...]
    for k in range(1, ZH):
        s = (zh - k + ZH) % ZH
        wait_recv(a4, rzh.at[s], o_zh + s, dev(c, y, x, s * 2 + zl))
    for d in ds:
        d.wait_send()
    acc = rzh[0]
    for j in range(1, ZH):
        acc = acc + rzh[j]
    base = c * S1 + y * S2 + x * S3
    full[rows(base + zl * S4, S4), :] = acc

    mine = rows(base + zl * S4, S4)
    d = send(full.at[mine], full.at[mine], o_agzl, o_agzl, zl_peer)
    wait_recv(full.at[mine], full.at[rows(base + (1 - zl) * S4, S4)], o_agzl, zl_peer)
    d.wait_send()

    mine = rows(c * S1 + y * S2 + x * S3, S3)
    ds = [send(full.at[mine], full.at[mine], o_agx + k, o_agx + x, dev(c, y, p, z))
          for k, p in enumerate(x_peers)]
    for k in range(1, X):
        s = (x - k + X) % X
        wait_recv(full.at[mine], full.at[rows(c * S1 + y * S2 + s * S3, S3)], o_agx + s, dev(c, y, s, z))
    for d in ds:
        d.wait_send()

    mine = rows(c * S1 + y * S2, S2)
    ds = [send(full.at[mine], full.at[mine], o_agy + k, o_agy + y, dev(c, p, x, z))
          for k, p in enumerate(y_peers)]
    for k in range(1, Y):
        s = (y - k + Y) % Y
        wait_recv(full.at[mine], full.at[rows(c * S1 + s * S2, S2)], o_agy + s, dev(c, s, x, z))
    for d in ds:
        d.wait_send()

    mine = rows(c * S1, S1)
    d = send(full.at[mine], full.at[mine], o_agc, o_agc, core_peer)
    wait_recv(full.at[mine], full.at[rows((1 - c) * S1, S1)], o_agc, core_peer)
    d.wait_send()

    if out_ref is not None:
        out_ref[...] = full[...]


def _zone_gather_kernel(nb, p_ref, out_ref, ssem, rsem, lsem):
    T = p_ref.shape[0]
    r = lax.axis_index("rows")
    b = lax.axis_index("blk")
    barrier = pltpu.get_barrier_semaphore()
    for k in range(1, nb):
        pl.semaphore_signal(barrier, inc=1, device_id=(r, (b + k) % nb), device_id_type=MESH_ID)
    pl.semaphore_wait(barrier, nb - 1)
    here = pl.ds(pl.multiple_of(b * T, 8), T)
    ds = []
    for k in range(1, nb):
        d = pltpu.make_async_remote_copy(
            src_ref=p_ref, dst_ref=out_ref.at[here], send_sem=ssem.at[k - 1], recv_sem=rsem.at[b],
            device_id=(r, (b + k) % nb), device_id_type=MESH_ID)
        d.start()
        ds.append(d)
    own = pltpu.make_async_copy(p_ref, out_ref.at[here], lsem.at[0])
    own.start()
    for k in range(1, nb):
        s = (b - k + nb) % nb
        pltpu.make_async_remote_copy(
            src_ref=p_ref, dst_ref=out_ref.at[pl.ds(pl.multiple_of(s * T, 8), T)], send_sem=ssem.at[0],
            recv_sem=rsem.at[s], device_id=(r, s), device_id_type=MESH_ID).wait_recv()
    for d in ds:
        d.wait_send()
    own.wait()


def zone_gather(p, nb):
    T, K = p.shape
    return pl.pallas_call(
        functools.partial(_zone_gather_kernel, nb),
        out_shape=jax.ShapeDtypeStruct((nb * T, K), p.dtype),
        in_specs=[pl.BlockSpec(memory_space=pl.ANY)],
        out_specs=pl.BlockSpec(memory_space=pl.ANY),
        scratch_shapes=[
            pltpu.SemaphoreType.DMA((nb - 1,)),
            pltpu.SemaphoreType.DMA((nb,)),
            pltpu.SemaphoreType.DMA((1,)),
        ],
        compiler_params=pltpu.CompilerParams(collective_id=1, has_side_effects=True),
    )(p)


HI = lax.Precision.HIGHEST


def _mm(a, b):
    return jnp.dot(a, b, precision=HI, preferred_element_type=jnp.float32)


def _mm_t(a, b):
    return lax.dot_general(a, b, (((1,), (1,)), ((), ())), precision=HI, preferred_element_type=jnp.float32)


def _chol_inv_kernel(count, g_ref, m_ref, a_ref, d_ref, b_ref, l_ref):
    n = g_ref.shape[0]
    t = d_ref.shape[0]
    nb = n // t
    gram = g_ref[...] / count
    a_ref[...] = (gram + gram.T) / 2
    m_ref[...] = jnp.zeros_like(m_ref)
    lane = lax.broadcasted_iota(jnp.int32, (1, t), 1)
    eye = (lax.broadcasted_iota(jnp.int32, (t, t), 0) == lax.broadcasted_iota(jnp.int32, (t, t), 1)).astype(jnp.float32)

    for k in range(nb):
        lo = k * t
        d_ref[...] = a_ref[lo:lo + t, lo:lo + t]
        b_ref[...] = eye
        for r0 in range(0, t, 16):
            sub = lax.broadcasted_iota(jnp.int32, (t - r0, 1), 0) + r0
            dl = d_ref[r0:, :]
            bl = b_ref[r0:, :]
            for i in range(16):
                j = r0 + i
                inv = lax.rsqrt(dl[i:i + 1, j:j + 1])
                col = jnp.where(sub >= j, dl[:, j:j + 1] * inv, 0.0)
                lrow = jnp.where(lane >= j, dl[i:i + 1, :] * inv, 0.0)
                dl = dl - col * lrow
                brow = bl[i:i + 1, :] * inv
                bl = jnp.where(sub == j, brow, bl - jnp.where(sub > j, col, 0.0) * brow)
            d_ref[r0:, :] = dl
            b_ref[r0:, :] = bl
        m_ref[lo:lo + t, lo:lo + t] = b_ref[...]
        if k < nb - 1:
            hi = lo + t
            panel = _mm_t(a_ref[hi:, lo:lo + t], b_ref[...])
            l_ref[hi:, lo:lo + t] = panel
            a_ref[hi:, hi:] = a_ref[hi:, hi:] - _mm_t(panel, panel)
    for dist in range(1, nb):
        for i in range(dist, nb):
            j = i - dist
            acc = None
            for k in range(j, i):
                term = _mm(l_ref[i * t:(i + 1) * t, k * t:(k + 1) * t], m_ref[k * t:(k + 1) * t, j * t:(j + 1) * t])
                acc = term if acc is None else acc + term
            m_ref[i * t:(i + 1) * t, j * t:(j + 1) * t] = -_mm(m_ref[i * t:(i + 1) * t, i * t:(i + 1) * t], acc)


def gram_factor_inverse(g, dims, count, t=128):
    XL, Z, C, XH, Y = dims
    X = XL * XH
    ZH = Z // 2
    N, M = g.shape
    S1 = N // C
    S2 = S1 // Y
    S3 = S2 // X
    S4 = S3 // 2
    nsem = 4 + 2 * Y + 2 * X + ZH
    vmem = pltpu.VMEM

    def kernel(g_ref, m_ref, rc, ry, rx, rzl, rzh, a1, a2, a3, a4, full, ssem, rsem, ca, cd, cb, cl):
        _ar_kernel(dims, g_ref, None, rc, ry, rx, rzl, rzh, a1, a2, a3, a4, full, ssem, rsem)
        _chol_inv_kernel(count, full, m_ref, ca, cd, cb, cl)

    return pl.pallas_call(
        kernel,
        out_shape=jax.ShapeDtypeStruct((N, M), jnp.float32),
        in_specs=[pl.BlockSpec(memory_space=vmem)],
        out_specs=pl.BlockSpec(memory_space=vmem),
        scratch_shapes=[
            vmem((S1, M), jnp.float32),
            vmem((Y, S2, M), jnp.float32),
            vmem((X, S3, M), jnp.float32),
            vmem((S4, M), jnp.float32),
            vmem((ZH, S4, M), jnp.float32),
            vmem((S1, M), jnp.float32),
            vmem((S2, M), jnp.float32),
            vmem((S3, M), jnp.float32),
            vmem((S4, M), jnp.float32),
            vmem((N, M), jnp.float32),
            pltpu.SemaphoreType.DMA((nsem,)),
            pltpu.SemaphoreType.DMA((nsem,)),
            vmem((N, N), jnp.float32),
            vmem((t, t), jnp.float32),
            vmem((t, t), jnp.float32),
            vmem((N, N), jnp.float32),
        ],
        compiler_params=pltpu.CompilerParams(collective_id=0, has_side_effects=True),
    )(g)


def extended(x, sides, width):
    for axis, dim in sides:
        devices, length = (lax.axis_size(axis), x.shape[dim])
        up = [(i, (i + 1) % devices) for i in range(devices - 1)]
        down = [(j, i) for i, j in up]
        last = lax.slice_in_dim(x, length - width, length, axis=dim)
        first = lax.slice_in_dim(x, 0, width, axis=dim)
        before = lax.ppermute(last, axis, up)
        after = lax.ppermute(first, axis, down)
        x = jnp.concatenate([before, x, after], axis=dim)
    return x


def _dims():
    rows, blk = lax.axis_size("rows"), lax.axis_size("blk")
    return (2, rows // 4, 2, 2, blk // 2)


def local(cov_blocks, col_index, block_count, probes):
    rows_here, slots, block, _ = cov_blocks.shape
    tile_rows = probes.shape[0]
    probe_cols = probes.shape[1]
    zone_blocks = rows_here * lax.axis_size("blk")
    zone_number = lax.axis_index("rows")
    relative = col_index - (zone_number - 1) * zone_blocks
    window_blocks = 3 * zone_blocks
    inside = (relative >= 0) & (relative < window_blocks)
    slot_ids = lax.broadcasted_iota(jnp.int32, (rows_here, slots), 1)
    live_mask = inside & (slot_ids < block_count[:, None])
    column_ids = jnp.arange(window_blocks, dtype=jnp.int32)
    hits = (relative[:, :, None] == column_ids[None, None, :]) & live_mask[:, :, None]
    selector = hits.astype(jnp.bfloat16)
    window_matrix = jnp.einsum(
        "lsp,lsac->lapc", selector, cov_blocks, preferred_element_type=jnp.float32
    )
    window_matrix = window_matrix.astype(jnp.bfloat16).reshape(
        rows_here * block, window_blocks * block
    )

    def add_columns(running, shard_rows, first_row):
        length = shard_rows.shape[0]
        columns = lax.dynamic_slice_in_dim(window_matrix, first_row, length, 1)
        return running + jnp.dot(columns, shard_rows, preferred_element_type=jnp.float32)

    zeros_out = jnp.zeros((tile_rows, probe_cols), jnp.float32)
    own_zone = zone_gather(probes, lax.axis_size("blk"))
    zone_length = own_zone.shape[0]
    images = add_columns(zeros_out, own_zone, zone_length)
    near_zones = extended(own_zone, (("rows", 0),), zone_length)
    images = add_columns(images, lax.slice_in_dim(near_zones, 0, zone_length, axis=0), 0)
    images = add_columns(
        images,
        lax.slice_in_dim(near_zones, 2 * zone_length, 3 * zone_length, axis=0),
        2 * zone_length,
    )
    gram_local = lax.dot_general(
        images,
        images,
        (((0,), (0,)), ((), ())),
        precision=lax.Precision.HIGHEST,
        preferred_element_type=jnp.float32,
    )
    point_count = tile_rows * lax.axis_size("rows") * lax.axis_size("blk")
    factor_inverse = gram_factor_inverse(gram_local, _dims(), float(point_count))
    return _mm_t(images, factor_inverse)


def solution(mesh):
    return jax.shard_map(
        local,
        mesh=mesh,
        in_specs=(
            P(("rows", "blk"), None, None, None),
            P(("rows", "blk"), None),
            P(("rows", "blk")),
            P(("rows", "blk"), None),
        ),
        out_specs=P(("rows", "blk"), None),
        check_vma=False,
    )
```

```python
import functools
import jax
import jax.numpy as jnp
from jax import lax
from jax.experimental import pallas as pl
from jax.experimental.pallas import tpu as pltpu
from jax.sharding import PartitionSpec as P

MESH_ID = pl.DeviceIdType.MESH


def _ar_kernel(dims, g_ref, out_ref, rc, ry, rx, rzl, rzh, a1, a2, a3, a4, full, ssem, rsem, prologue=None):
    XL, Z, C, XH, Y = dims
    X = XL * XH
    ZH = Z // 2
    N = g_ref.shape[0]
    S1 = N // C
    S2 = S1 // Y
    S3 = S2 // X
    S4 = S3 // 2
    r = lax.axis_index("rows")
    b = lax.axis_index("blk")
    c = r % C
    z = (r // C) % Z
    xl = r // (C * Z)
    xh = b // Y
    y = b % Y
    x = xh * XL + xl
    zl = z % 2
    zh = z // 2

    def dev(c_, y_, x_, z_):
        return ((x_ % XL) * (Z * C) + z_ * C + c_, (x_ // XL) * Y + y_)

    core_peer = dev(1 - c, y, x, z)
    y_peers = [(y + k) % Y for k in range(1, Y)]
    x_peers = [(x + k) % X for k in range(1, X)]
    zl_peer = dev(c, y, x, zh * 2 + 1 - zl)
    zh_peers = [(zh + k) % ZH for k in range(1, ZH)]
    peers = [core_peer, zl_peer]
    peers += [dev(c, p, x, z) for p in y_peers]
    peers += [dev(c, y, p, z) for p in x_peers]
    peers += [dev(c, y, x, p * 2 + zl) for p in zh_peers]

    barrier = pltpu.get_barrier_semaphore()
    for p in peers:
        pl.semaphore_signal(barrier, inc=1, device_id=p, device_id_type=MESH_ID)
    if prologue is not None:
        prologue()
    pl.semaphore_wait(barrier, len(peers))

    o_core, o_y, o_x, o_zl, o_zh = 0, 1, 1 + Y, 1 + Y + X, 2 + Y + X
    o_agzl, o_agx, o_agy, o_agc = 2 + Y + X + ZH, 3 + Y + X + ZH, 3 + Y + 2 * X + ZH, 3 + 2 * Y + 2 * X + ZH

    def send(src, dst, sidx, ridx, peer):
        d = pltpu.make_async_remote_copy(
            src_ref=src, dst_ref=dst, send_sem=ssem.at[sidx], recv_sem=rsem.at[ridx],
            device_id=peer, device_id_type=MESH_ID)
        d.start()
        return d

    def wait_recv(src, dst, ridx, peer):
        pltpu.make_async_remote_copy(
            src_ref=src, dst_ref=dst, send_sem=ssem.at[0], recv_sem=rsem.at[ridx],
            device_id=peer, device_id_type=MESH_ID).wait_recv()

    def rows(start, size):
        return pl.ds(pl.multiple_of(start, 8), size)

    d = send(g_ref.at[rows((1 - c) * S1, S1)], rc, o_core, o_core, core_peer)
    wait_recv(g_ref.at[rows(c * S1, S1)], rc, o_core, core_peer)
    d.wait_send()
    a1[...] = g_ref[rows(c * S1, S1), :] + rc[...]

    ds = [send(a1.at[rows(p * S2, S2)], ry.at[y], o_y + k, o_y + y, dev(c, p, x, z))
          for k, p in enumerate(y_peers)]
    for k in range(1, Y):
        s = (y - k + Y) % Y
        wait_recv(a1.at[rows(0, S2)], ry.at[s], o_y + s, dev(c, s, x, z))
    for d in ds:
        d.wait_send()
    acc = a1[rows(y * S2, S2), :]
    for k in range(1, Y):
        acc = acc + ry[(y - k + Y) % Y]
    a2[...] = acc

    ds = [send(a2.at[rows(p * S3, S3)], rx.at[x], o_x + k, o_x + x, dev(c, y, p, z))
          for k, p in enumerate(x_peers)]
    for k in range(1, X):
        s = (x - k + X) % X
        wait_recv(a2.at[rows(0, S3)], rx.at[s], o_x + s, dev(c, y, s, z))
    for d in ds:
        d.wait_send()
    acc = a2[rows(x * S3, S3), :]
    for k in range(1, X):
        acc = acc + rx[(x - k + X) % X]
    a3[...] = acc

    d = send(a3.at[rows((1 - zl) * S4, S4)], rzl, o_zl, o_zl, zl_peer)
    wait_recv(a3.at[rows(zl * S4, S4)], rzl, o_zl, zl_peer)
    d.wait_send()
    a4[...] = a3[rows(zl * S4, S4), :] + rzl[...]

    ds = [send(a4, rzh.at[zh], o_zh + k, o_zh + zh, dev(c, y, x, p * 2 + zl))
          for k, p in enumerate(zh_peers)]
    rzh[zh] = a4[...]
    for k in range(1, ZH):
        s = (zh - k + ZH) % ZH
        wait_recv(a4, rzh.at[s], o_zh + s, dev(c, y, x, s * 2 + zl))
    for d in ds:
        d.wait_send()
    acc = rzh[0]
    for j in range(1, ZH):
        acc = acc + rzh[j]
    base = c * S1 + y * S2 + x * S3
    full[rows(base + zl * S4, S4), :] = acc

    mine = rows(base + zl * S4, S4)
    d = send(full.at[mine], full.at[mine], o_agzl, o_agzl, zl_peer)
    wait_recv(full.at[mine], full.at[rows(base + (1 - zl) * S4, S4)], o_agzl, zl_peer)
    d.wait_send()

    mine = rows(c * S1 + y * S2 + x * S3, S3)
    ds = [send(full.at[mine], full.at[mine], o_agx + k, o_agx + x, dev(c, y, p, z))
          for k, p in enumerate(x_peers)]
    for k in range(1, X):
        s = (x - k + X) % X
        wait_recv(full.at[mine], full.at[rows(c * S1 + y * S2 + s * S3, S3)], o_agx + s, dev(c, y, s, z))
    for d in ds:
        d.wait_send()

    mine = rows(c * S1 + y * S2, S2)
    ds = [send(full.at[mine], full.at[mine], o_agy + k, o_agy + y, dev(c, p, x, z))
          for k, p in enumerate(y_peers)]
    for k in range(1, Y):
        s = (y - k + Y) % Y
        wait_recv(full.at[mine], full.at[rows(c * S1 + s * S2, S2)], o_agy + s, dev(c, s, x, z))
    for d in ds:
        d.wait_send()

    mine = rows(c * S1, S1)
    d = send(full.at[mine], full.at[mine], o_agc, o_agc, core_peer)
    wait_recv(full.at[mine], full.at[rows((1 - c) * S1, S1)], o_agc, core_peer)
    d.wait_send()

    if out_ref is not None:
        out_ref[...] = full[...]


def _zone_gather_kernel(nb, p_ref, out_ref, ssem, rsem, lsem):
    T = p_ref.shape[0]
    r = lax.axis_index("rows")
    b = lax.axis_index("blk")
    barrier = pltpu.get_barrier_semaphore()
    for k in range(1, nb):
        pl.semaphore_signal(barrier, inc=1, device_id=(r, (b + k) % nb), device_id_type=MESH_ID)
    pl.semaphore_wait(barrier, nb - 1)
    here = pl.ds(pl.multiple_of(b * T, 8), T)
    ds = []
    for k in range(1, nb):
        d = pltpu.make_async_remote_copy(
            src_ref=p_ref, dst_ref=out_ref.at[here], send_sem=ssem.at[k - 1], recv_sem=rsem.at[b],
            device_id=(r, (b + k) % nb), device_id_type=MESH_ID)
        d.start()
        ds.append(d)
    own = pltpu.make_async_copy(p_ref, out_ref.at[here], lsem.at[0])
    own.start()
    for k in range(1, nb):
        s = (b - k + nb) % nb
        pltpu.make_async_remote_copy(
            src_ref=p_ref, dst_ref=out_ref.at[pl.ds(pl.multiple_of(s * T, 8), T)], send_sem=ssem.at[0],
            recv_sem=rsem.at[s], device_id=(r, s), device_id_type=MESH_ID).wait_recv()
    for d in ds:
        d.wait_send()
    own.wait()


def zone_gather(p, nb):
    T, K = p.shape
    return pl.pallas_call(
        functools.partial(_zone_gather_kernel, nb),
        out_shape=jax.ShapeDtypeStruct((nb * T, K), p.dtype),
        in_specs=[pl.BlockSpec(memory_space=pl.ANY)],
        out_specs=pl.BlockSpec(memory_space=pl.ANY),
        scratch_shapes=[
            pltpu.SemaphoreType.DMA((nb - 1,)),
            pltpu.SemaphoreType.DMA((nb,)),
            pltpu.SemaphoreType.DMA((1,)),
        ],
        compiler_params=pltpu.CompilerParams(collective_id=1, has_side_effects=True),
    )(p)


HI = lax.Precision.HIGHEST


def _mm(a, b):
    return jnp.dot(a, b, precision=HI, preferred_element_type=jnp.float32)


def _mm_t(a, b):
    return lax.dot_general(a, b, (((1,), (1,)), ((), ())), precision=HI, preferred_element_type=jnp.float32)


def _chol_inv_kernel(count, g_ref, m_ref, a_ref, d_ref, b_ref, l_ref):
    n = g_ref.shape[0]
    t = d_ref.shape[0]
    nb = n // t
    gram = g_ref[...] / count
    a_ref[...] = (gram + gram.T) / 2
    m_ref[...] = jnp.zeros_like(m_ref)
    lane = lax.broadcasted_iota(jnp.int32, (1, t), 1)
    eye = (lax.broadcasted_iota(jnp.int32, (t, t), 0) == lax.broadcasted_iota(jnp.int32, (t, t), 1)).astype(jnp.float32)

    for k in range(nb):
        lo = k * t
        d_ref[...] = a_ref[lo:lo + t, lo:lo + t]
        b_ref[...] = eye
        for r0 in range(0, t, 8):
            sub = lax.broadcasted_iota(jnp.int32, (t - r0, 1), 0) + r0
            dl = d_ref[r0:, :]
            bl = b_ref[r0:, :]
            for i in range(8):
                j = r0 + i
                inv = lax.rsqrt(dl[i:i + 1, j:j + 1])
                col = jnp.where(sub >= j, dl[:, j:j + 1] * inv, 0.0)
                lrow = jnp.where(lane >= j, dl[i:i + 1, :] * inv, 0.0)
                dl = dl - col * lrow
                brow = bl[i:i + 1, :] * inv
                bl = jnp.where(sub == j, brow, bl - jnp.where(sub > j, col, 0.0) * brow)
            d_ref[r0:, :] = dl
            b_ref[r0:, :] = bl
        m_ref[lo:lo + t, lo:lo + t] = b_ref[...]
        if k < nb - 1:
            hi = lo + t
            panel = _mm_t(a_ref[hi:, lo:lo + t], b_ref[...])
            l_ref[hi:, lo:lo + t] = panel
            a_ref[hi:, hi:] = a_ref[hi:, hi:] - _mm_t(panel, panel)
    for dist in range(1, nb):
        for i in range(dist, nb):
            j = i - dist
            acc = None
            for k in range(j, i):
                term = _mm(l_ref[i * t:(i + 1) * t, k * t:(k + 1) * t], m_ref[k * t:(k + 1) * t, j * t:(j + 1) * t])
                acc = term if acc is None else acc + term
            m_ref[i * t:(i + 1) * t, j * t:(j + 1) * t] = -_mm(m_ref[i * t:(i + 1) * t, i * t:(i + 1) * t], acc)


def orthonormal_basis(images, dims, count, t=128):
    XL, Z, C, XH, Y = dims
    X = XL * XH
    ZH = Z // 2
    N = M = images.shape[1]
    S1 = N // C
    S2 = S1 // Y
    S3 = S2 // X
    S4 = S3 // 2
    nsem = 4 + 2 * Y + 2 * X + ZH
    vmem = pltpu.VMEM

    def kernel(x_ref, out_ref, rc, ry, rx, rzl, rzh, a1, a2, a3, a4, full, ssem, rsem, ca, cd, cb, cl, gsc, msc):
        def local_gram():
            x = x_ref[...]
            gsc[...] = jnp.dot(x.T, x, precision=HI, preferred_element_type=jnp.float32)

        _ar_kernel(dims, gsc, None, rc, ry, rx, rzl, rzh, a1, a2, a3, a4, full, ssem, rsem, local_gram)
        _chol_inv_kernel(count, full, msc, ca, cd, cb, cl)
        out_ref[...] = _mm_t(x_ref[...], msc[...])

    return pl.pallas_call(
        kernel,
        out_shape=jax.ShapeDtypeStruct(images.shape, jnp.float32),
        in_specs=[pl.BlockSpec(memory_space=vmem)],
        out_specs=pl.BlockSpec(memory_space=vmem),
        scratch_shapes=[
            vmem((S1, M), jnp.float32),
            vmem((Y, S2, M), jnp.float32),
            vmem((X, S3, M), jnp.float32),
            vmem((S4, M), jnp.float32),
            vmem((ZH, S4, M), jnp.float32),
            vmem((S1, M), jnp.float32),
            vmem((S2, M), jnp.float32),
            vmem((S3, M), jnp.float32),
            vmem((S4, M), jnp.float32),
            vmem((N, M), jnp.float32),
            pltpu.SemaphoreType.DMA((nsem,)),
            pltpu.SemaphoreType.DMA((nsem,)),
            vmem((N, N), jnp.float32),
            vmem((t, t), jnp.float32),
            vmem((t, t), jnp.float32),
            vmem((N, N), jnp.float32),
            vmem((N, N), jnp.float32),
            vmem((N, N), jnp.float32),
        ],
        compiler_params=pltpu.CompilerParams(collective_id=0, has_side_effects=True),
    )(images)


def extended(x, sides, width):
    for axis, dim in sides:
        devices, length = (lax.axis_size(axis), x.shape[dim])
        up = [(i, (i + 1) % devices) for i in range(devices - 1)]
        down = [(j, i) for i, j in up]
        last = lax.slice_in_dim(x, length - width, length, axis=dim)
        first = lax.slice_in_dim(x, 0, width, axis=dim)
        before = lax.ppermute(last, axis, up)
        after = lax.ppermute(first, axis, down)
        x = jnp.concatenate([before, x, after], axis=dim)
    return x


def _dims():
    rows, blk = lax.axis_size("rows"), lax.axis_size("blk")
    return (2, rows // 4, 2, 2, blk // 2)


def local(cov_blocks, col_index, block_count, probes):
    rows_here, slots, block, _ = cov_blocks.shape
    tile_rows = probes.shape[0]
    probe_cols = probes.shape[1]
    zone_blocks = rows_here * lax.axis_size("blk")
    zone_number = lax.axis_index("rows")
    relative = col_index - (zone_number - 1) * zone_blocks
    window_blocks = 3 * zone_blocks
    inside = (relative >= 0) & (relative < window_blocks)
    slot_ids = lax.broadcasted_iota(jnp.int32, (rows_here, slots), 1)
    live_mask = inside & (slot_ids < block_count[:, None])
    column_ids = jnp.arange(window_blocks, dtype=jnp.int32)
    hits = (relative[:, :, None] == column_ids[None, None, :]) & live_mask[:, :, None]
    selector = hits.astype(jnp.bfloat16)
    window_matrix = jnp.einsum(
        "lsp,lsac->lapc", selector, cov_blocks, preferred_element_type=jnp.float32
    )
    window_matrix = window_matrix.astype(jnp.bfloat16).reshape(
        rows_here * block, window_blocks * block
    )

    def add_columns(running, shard_rows, first_row):
        length = shard_rows.shape[0]
        columns = lax.dynamic_slice_in_dim(window_matrix, first_row, length, 1)
        return running + jnp.dot(columns, shard_rows, preferred_element_type=jnp.float32)

    zeros_out = jnp.zeros((tile_rows, probe_cols), jnp.float32)
    own_zone = zone_gather(probes, lax.axis_size("blk"))
    zone_length = own_zone.shape[0]
    images = add_columns(zeros_out, own_zone, zone_length)
    near_zones = extended(own_zone, (("rows", 0),), zone_length)
    images = add_columns(images, lax.slice_in_dim(near_zones, 0, zone_length, axis=0), 0)
    images = add_columns(
        images,
        lax.slice_in_dim(near_zones, 2 * zone_length, 3 * zone_length, axis=0),
        2 * zone_length,
    )
    point_count = tile_rows * lax.axis_size("rows") * lax.axis_size("blk")
    return orthonormal_basis(images, _dims(), float(point_count))


def solution(mesh):
    return jax.shard_map(
        local,
        mesh=mesh,
        in_specs=(
            P(("rows", "blk"), None, None, None),
            P(("rows", "blk"), None),
            P(("rows", "blk")),
            P(("rows", "blk"), None),
        ),
        out_specs=P(("rows", "blk"), None),
        check_vma=False,
    )
```

```python
import functools
import jax
import jax.numpy as jnp
from jax import lax
from jax.experimental import pallas as pl
from jax.experimental.pallas import tpu as pltpu
from jax.sharding import PartitionSpec as P

MESH_ID = pl.DeviceIdType.MESH


def _ar_kernel(dims, g_ref, out_ref, rc, ry, rx, rzl, rzh, a1, a2, a3, a4, full, ssem, rsem, prologue=None):
    XL, Z, C, XH, Y = dims
    X = XL * XH
    ZH = Z // 2
    N = g_ref.shape[0]
    S1 = N // C
    S2 = S1 // Y
    S3 = S2 // X
    S4 = S3 // 2
    r = lax.axis_index("rows")
    b = lax.axis_index("blk")
    c = r % C
    z = (r // C) % Z
    xl = r // (C * Z)
    xh = b // Y
    y = b % Y
    x = xh * XL + xl
    zl = z % 2
    zh = z // 2

    def dev(c_, y_, x_, z_):
        return ((x_ % XL) * (Z * C) + z_ * C + c_, (x_ // XL) * Y + y_)

    core_peer = dev(1 - c, y, x, z)
    y_peers = [(y + k) % Y for k in range(1, Y)]
    x_peers = [(x + k) % X for k in range(1, X)]
    zl_peer = dev(c, y, x, zh * 2 + 1 - zl)
    zh_peers = [(zh + k) % ZH for k in range(1, ZH)]
    peers = [core_peer, zl_peer]
    peers += [dev(c, p, x, z) for p in y_peers]
    peers += [dev(c, y, p, z) for p in x_peers]
    peers += [dev(c, y, x, p * 2 + zl) for p in zh_peers]

    barrier = pltpu.get_barrier_semaphore()
    for p in peers:
        pl.semaphore_signal(barrier, inc=1, device_id=p, device_id_type=MESH_ID)
    if prologue is not None:
        prologue()
    pl.semaphore_wait(barrier, len(peers))

    o_core, o_y, o_x, o_zl, o_zh = 0, 1, 1 + Y, 1 + Y + X, 2 + Y + X
    o_agzl, o_agx, o_agy, o_agc = 2 + Y + X + ZH, 3 + Y + X + ZH, 3 + Y + 2 * X + ZH, 3 + 2 * Y + 2 * X + ZH

    def send(src, dst, sidx, ridx, peer):
        d = pltpu.make_async_remote_copy(
            src_ref=src, dst_ref=dst, send_sem=ssem.at[sidx], recv_sem=rsem.at[ridx],
            device_id=peer, device_id_type=MESH_ID)
        d.start()
        return d

    def wait_recv(src, dst, ridx, peer):
        pltpu.make_async_remote_copy(
            src_ref=src, dst_ref=dst, send_sem=ssem.at[0], recv_sem=rsem.at[ridx],
            device_id=peer, device_id_type=MESH_ID).wait_recv()

    def rows(start, size):
        return pl.ds(pl.multiple_of(start, 8), size)

    d = send(g_ref.at[rows((1 - c) * S1, S1)], rc, o_core, o_core, core_peer)
    wait_recv(g_ref.at[rows(c * S1, S1)], rc, o_core, core_peer)
    d.wait_send()
    a1[...] = g_ref[rows(c * S1, S1), :] + rc[...]

    ds = [send(a1.at[rows(p * S2, S2)], ry.at[y], o_y + k, o_y + y, dev(c, p, x, z))
          for k, p in enumerate(y_peers)]
    for k in range(1, Y):
        s = (y - k + Y) % Y
        wait_recv(a1.at[rows(0, S2)], ry.at[s], o_y + s, dev(c, s, x, z))
    for d in ds:
        d.wait_send()
    acc = a1[rows(y * S2, S2), :]
    for k in range(1, Y):
        acc = acc + ry[(y - k + Y) % Y]
    a2[...] = acc

    ds = [send(a2.at[rows(p * S3, S3)], rx.at[x], o_x + k, o_x + x, dev(c, y, p, z))
          for k, p in enumerate(x_peers)]
    for k in range(1, X):
        s = (x - k + X) % X
        wait_recv(a2.at[rows(0, S3)], rx.at[s], o_x + s, dev(c, y, s, z))
    for d in ds:
        d.wait_send()
    acc = a2[rows(x * S3, S3), :]
    for k in range(1, X):
        acc = acc + rx[(x - k + X) % X]
    a3[...] = acc

    d = send(a3.at[rows((1 - zl) * S4, S4)], rzl, o_zl, o_zl, zl_peer)
    wait_recv(a3.at[rows(zl * S4, S4)], rzl, o_zl, zl_peer)
    d.wait_send()
    a4[...] = a3[rows(zl * S4, S4), :] + rzl[...]

    ds = [send(a4, rzh.at[zh], o_zh + k, o_zh + zh, dev(c, y, x, p * 2 + zl))
          for k, p in enumerate(zh_peers)]
    rzh[zh] = a4[...]
    for k in range(1, ZH):
        s = (zh - k + ZH) % ZH
        wait_recv(a4, rzh.at[s], o_zh + s, dev(c, y, x, s * 2 + zl))
    for d in ds:
        d.wait_send()
    acc = rzh[0]
    for j in range(1, ZH):
        acc = acc + rzh[j]
    base = c * S1 + y * S2 + x * S3
    full[rows(base + zl * S4, S4), :] = acc

    mine = rows(base + zl * S4, S4)
    d = send(full.at[mine], full.at[mine], o_agzl, o_agzl, zl_peer)
    wait_recv(full.at[mine], full.at[rows(base + (1 - zl) * S4, S4)], o_agzl, zl_peer)
    d.wait_send()

    mine = rows(c * S1 + y * S2 + x * S3, S3)
    ds = [send(full.at[mine], full.at[mine], o_agx + k, o_agx + x, dev(c, y, p, z))
          for k, p in enumerate(x_peers)]
    for k in range(1, X):
        s = (x - k + X) % X
        wait_recv(full.at[mine], full.at[rows(c * S1 + y * S2 + s * S3, S3)], o_agx + s, dev(c, y, s, z))
    for d in ds:
        d.wait_send()

    mine = rows(c * S1 + y * S2, S2)
    ds = [send(full.at[mine], full.at[mine], o_agy + k, o_agy + y, dev(c, p, x, z))
          for k, p in enumerate(y_peers)]
    for k in range(1, Y):
        s = (y - k + Y) % Y
        wait_recv(full.at[mine], full.at[rows(c * S1 + s * S2, S2)], o_agy + s, dev(c, s, x, z))
    for d in ds:
        d.wait_send()

    mine = rows(c * S1, S1)
    d = send(full.at[mine], full.at[mine], o_agc, o_agc, core_peer)
    wait_recv(full.at[mine], full.at[rows((1 - c) * S1, S1)], o_agc, core_peer)
    d.wait_send()

    if out_ref is not None:
        out_ref[...] = full[...]


def _zone_gather_kernel(nb, p_ref, out_ref, ssem, rsem, lsem):
    T = p_ref.shape[0]
    r = lax.axis_index("rows")
    b = lax.axis_index("blk")
    barrier = pltpu.get_barrier_semaphore()
    for k in range(1, nb):
        pl.semaphore_signal(barrier, inc=1, device_id=(r, (b + k) % nb), device_id_type=MESH_ID)
    pl.semaphore_wait(barrier, nb - 1)
    here = pl.ds(pl.multiple_of(b * T, 8), T)
    ds = []
    for k in range(1, nb):
        d = pltpu.make_async_remote_copy(
            src_ref=p_ref, dst_ref=out_ref.at[here], send_sem=ssem.at[k - 1], recv_sem=rsem.at[b],
            device_id=(r, (b + k) % nb), device_id_type=MESH_ID)
        d.start()
        ds.append(d)
    own = pltpu.make_async_copy(p_ref, out_ref.at[here], lsem.at[0])
    own.start()
    for k in range(1, nb):
        s = (b - k + nb) % nb
        pltpu.make_async_remote_copy(
            src_ref=p_ref, dst_ref=out_ref.at[pl.ds(pl.multiple_of(s * T, 8), T)], send_sem=ssem.at[0],
            recv_sem=rsem.at[s], device_id=(r, s), device_id_type=MESH_ID).wait_recv()
    for d in ds:
        d.wait_send()
    own.wait()


def zone_gather(p, nb):
    T, K = p.shape
    return pl.pallas_call(
        functools.partial(_zone_gather_kernel, nb),
        out_shape=jax.ShapeDtypeStruct((nb * T, K), p.dtype),
        in_specs=[pl.BlockSpec(memory_space=pl.ANY)],
        out_specs=pl.BlockSpec(memory_space=pl.ANY),
        scratch_shapes=[
            pltpu.SemaphoreType.DMA((nb - 1,)),
            pltpu.SemaphoreType.DMA((nb,)),
            pltpu.SemaphoreType.DMA((1,)),
        ],
        compiler_params=pltpu.CompilerParams(collective_id=1, has_side_effects=True),
    )(p)


HI = lax.Precision.HIGHEST


def _mm(a, b):
    return jnp.dot(a, b, precision=HI, preferred_element_type=jnp.float32)


def _mm_t(a, b):
    return lax.dot_general(a, b, (((1,), (1,)), ((), ())), precision=HI, preferred_element_type=jnp.float32)


def _chol_inv_kernel(count, g_ref, m_ref, a_ref, d_ref, b_ref, l_ref):
    n = g_ref.shape[0]
    t = d_ref.shape[0]
    nb = n // t
    gram = g_ref[...] / count
    a_ref[...] = (gram + gram.T) / 2
    lane = lax.broadcasted_iota(jnp.int32, (1, t), 1)
    eye = (lax.broadcasted_iota(jnp.int32, (t, t), 0) == lax.broadcasted_iota(jnp.int32, (t, t), 1)).astype(jnp.float32)

    for k in range(nb):
        lo = k * t
        d_ref[...] = a_ref[lo:lo + t, lo:lo + t]
        b_ref[...] = eye
        for r0 in range(0, t, 8):
            sub = lax.broadcasted_iota(jnp.int32, (t - r0, 1), 0) + r0
            dl = d_ref[r0:, :]
            bl = b_ref[r0:, :]
            for i in range(8):
                j = r0 + i
                inv = lax.rsqrt(dl[i:i + 1, j:j + 1])
                col = jnp.where(sub >= j, dl[:, j:j + 1] * inv, 0.0)
                lrow = jnp.where(lane >= j, dl[i:i + 1, :] * inv, 0.0)
                dl = dl - col * lrow
                brow = bl[i:i + 1, :] * inv
                bl = jnp.where(sub == j, brow, bl - jnp.where(sub > j, col, 0.0) * brow)
            d_ref[r0:, :] = dl
            b_ref[r0:, :] = bl
        m_ref[lo:lo + t, lo:lo + t] = b_ref[...]
        if k < nb - 1:
            hi = lo + t
            panel = _mm_t(a_ref[hi:, lo:lo + t], b_ref[...])
            l_ref[hi:, lo:lo + t] = panel
            a_ref[hi:, hi:] = a_ref[hi:, hi:] - _mm_t(panel, panel)
    for dist in range(1, nb):
        for i in range(dist, nb):
            j = i - dist
            acc = None
            for k in range(j, i):
                term = _mm(l_ref[i * t:(i + 1) * t, k * t:(k + 1) * t], m_ref[k * t:(k + 1) * t, j * t:(j + 1) * t])
                acc = term if acc is None else acc + term
            m_ref[i * t:(i + 1) * t, j * t:(j + 1) * t] = -_mm(m_ref[i * t:(i + 1) * t, i * t:(i + 1) * t], acc)


def orthonormal_basis(images, dims, count, t=128):
    XL, Z, C, XH, Y = dims
    X = XL * XH
    ZH = Z // 2
    N = M = images.shape[1]
    S1 = N // C
    S2 = S1 // Y
    S3 = S2 // X
    S4 = S3 // 2
    nsem = 4 + 2 * Y + 2 * X + ZH
    vmem = pltpu.VMEM

    def kernel(x_ref, out_ref, rc, ry, rx, rzl, rzh, a1, a2, a3, a4, full, ssem, rsem, ca, cd, cb, cl, gsc, msc):
        def local_gram():
            x = x_ref[...]
            gsc[...] = jnp.dot(x.T, x, precision=HI, preferred_element_type=jnp.float32)

        _ar_kernel(dims, gsc, None, rc, ry, rx, rzl, rzh, a1, a2, a3, a4, full, ssem, rsem, local_gram)
        _chol_inv_kernel(count, full, msc, ca, cd, cb, cl)
        for j in range(N // t):
            k = (j + 1) * t
            out_ref[:, j * t:k] = _mm_t(x_ref[:, :k], msc[j * t:k, :k])

    return pl.pallas_call(
        kernel,
        out_shape=jax.ShapeDtypeStruct(images.shape, jnp.float32),
        in_specs=[pl.BlockSpec(memory_space=vmem)],
        out_specs=pl.BlockSpec(memory_space=vmem),
        scratch_shapes=[
            vmem((S1, M), jnp.float32),
            vmem((Y, S2, M), jnp.float32),
            vmem((X, S3, M), jnp.float32),
            vmem((S4, M), jnp.float32),
            vmem((ZH, S4, M), jnp.float32),
            vmem((S1, M), jnp.float32),
            vmem((S2, M), jnp.float32),
            vmem((S3, M), jnp.float32),
            vmem((S4, M), jnp.float32),
            vmem((N, M), jnp.float32),
            pltpu.SemaphoreType.DMA((nsem,)),
            pltpu.SemaphoreType.DMA((nsem,)),
            vmem((N, N), jnp.float32),
            vmem((t, t), jnp.float32),
            vmem((t, t), jnp.float32),
            vmem((N, N), jnp.float32),
            vmem((N, N), jnp.float32),
            vmem((N, N), jnp.float32),
        ],
        compiler_params=pltpu.CompilerParams(collective_id=0, has_side_effects=True),
    )(images)


def extended(x, sides, width):
    for axis, dim in sides:
        devices, length = (lax.axis_size(axis), x.shape[dim])
        up = [(i, (i + 1) % devices) for i in range(devices - 1)]
        down = [(j, i) for i, j in up]
        last = lax.slice_in_dim(x, length - width, length, axis=dim)
        first = lax.slice_in_dim(x, 0, width, axis=dim)
        before = lax.ppermute(last, axis, up)
        after = lax.ppermute(first, axis, down)
        x = jnp.concatenate([before, x, after], axis=dim)
    return x


def _dims():
    rows, blk = lax.axis_size("rows"), lax.axis_size("blk")
    return (2, rows // 4, 2, 2, blk // 2)


def local(cov_blocks, col_index, block_count, probes):
    rows_here, slots, block, _ = cov_blocks.shape
    tile_rows = probes.shape[0]
    probe_cols = probes.shape[1]
    zone_blocks = rows_here * lax.axis_size("blk")
    zone_number = lax.axis_index("rows")
    relative = col_index - (zone_number - 1) * zone_blocks
    window_blocks = 3 * zone_blocks
    inside = (relative >= 0) & (relative < window_blocks)
    slot_ids = lax.broadcasted_iota(jnp.int32, (rows_here, slots), 1)
    live_mask = inside & (slot_ids < block_count[:, None])
    column_ids = jnp.arange(window_blocks, dtype=jnp.int32)
    hits = (relative[:, :, None] == column_ids[None, None, :]) & live_mask[:, :, None]
    selector = hits.astype(jnp.bfloat16)
    window_matrix = jnp.einsum(
        "lsp,lsac->lapc", selector, cov_blocks, preferred_element_type=jnp.float32
    )
    window_matrix = window_matrix.astype(jnp.bfloat16).reshape(
        rows_here * block, window_blocks * block
    )

    def add_columns(running, shard_rows, first_row):
        length = shard_rows.shape[0]
        columns = lax.dynamic_slice_in_dim(window_matrix, first_row, length, 1)
        return running + jnp.dot(columns, shard_rows, preferred_element_type=jnp.float32)

    zeros_out = jnp.zeros((tile_rows, probe_cols), jnp.float32)
    own_zone = zone_gather(probes, lax.axis_size("blk"))
    zone_length = own_zone.shape[0]
    images = add_columns(zeros_out, own_zone, zone_length)
    near_zones = extended(own_zone, (("rows", 0),), zone_length)
    images = add_columns(images, lax.slice_in_dim(near_zones, 0, zone_length, axis=0), 0)
    images = add_columns(
        images,
        lax.slice_in_dim(near_zones, 2 * zone_length, 3 * zone_length, axis=0),
        2 * zone_length,
    )
    point_count = tile_rows * lax.axis_size("rows") * lax.axis_size("blk")
    return orthonormal_basis(images, _dims(), float(point_count))


def solution(mesh):
    return jax.shard_map(
        local,
        mesh=mesh,
        in_specs=(
            P(("rows", "blk"), None, None, None),
            P(("rows", "blk"), None),
            P(("rows", "blk")),
            P(("rows", "blk"), None),
        ),
        out_specs=P(("rows", "blk"), None),
        check_vma=False,
    )
```

```python
import functools
import jax
import jax.numpy as jnp
from jax import lax
from jax.experimental import pallas as pl
from jax.experimental.pallas import tpu as pltpu
from jax.sharding import PartitionSpec as P

MESH_ID = pl.DeviceIdType.MESH


def _ar_kernel(dims, g_ref, out_ref, rc, ry, rx, rzl, rzh, a1, a2, a3, a4, full, ssem, rsem, prologue=None):
    XL, Z, C, XH, Y = dims
    X = XL * XH
    ZH = Z // 2
    N = g_ref.shape[0]
    S1 = N // C
    S2 = S1 // Y
    S3 = S2 // X
    S4 = S3 // 2
    r = lax.axis_index("rows")
    b = lax.axis_index("blk")
    c = r % C
    z = (r // C) % Z
    xl = r // (C * Z)
    xh = b // Y
    y = b % Y
    x = xh * XL + xl
    zl = z % 2
    zh = z // 2

    def dev(c_, y_, x_, z_):
        return ((x_ % XL) * (Z * C) + z_ * C + c_, (x_ // XL) * Y + y_)

    core_peer = dev(1 - c, y, x, z)
    y_peers = [(y + k) % Y for k in range(1, Y)]
    x_peers = [(x + k) % X for k in range(1, X)]
    zl_peer = dev(c, y, x, zh * 2 + 1 - zl)
    zh_peers = [(zh + k) % ZH for k in range(1, ZH)]
    peers = [core_peer, zl_peer]
    peers += [dev(c, p, x, z) for p in y_peers]
    peers += [dev(c, y, p, z) for p in x_peers]
    peers += [dev(c, y, x, p * 2 + zl) for p in zh_peers]

    barrier = pltpu.get_barrier_semaphore()
    for p in peers:
        pl.semaphore_signal(barrier, inc=1, device_id=p, device_id_type=MESH_ID)
    if prologue is not None:
        prologue()
    pl.semaphore_wait(barrier, len(peers))

    o_core, o_y, o_x, o_zl, o_zh = 0, 1, 1 + Y, 1 + Y + X, 2 + Y + X
    o_agzl, o_agx, o_agy, o_agc = 2 + Y + X + ZH, 3 + Y + X + ZH, 3 + Y + 2 * X + ZH, 3 + 2 * Y + 2 * X + ZH

    pending = []

    def send(src, dst, sidx, ridx, peer):
        d = pltpu.make_async_remote_copy(
            src_ref=src, dst_ref=dst, send_sem=ssem.at[sidx], recv_sem=rsem.at[ridx],
            device_id=peer, device_id_type=MESH_ID)
        d.start()
        pending.append(d)
        return d

    def wait_recv(src, dst, ridx, peer):
        pltpu.make_async_remote_copy(
            src_ref=src, dst_ref=dst, send_sem=ssem.at[0], recv_sem=rsem.at[ridx],
            device_id=peer, device_id_type=MESH_ID).wait_recv()

    def rows(start, size):
        return pl.ds(pl.multiple_of(start, 8), size)

    d = send(g_ref.at[rows((1 - c) * S1, S1)], rc, o_core, o_core, core_peer)
    wait_recv(g_ref.at[rows(c * S1, S1)], rc, o_core, core_peer)
    a1[...] = g_ref[rows(c * S1, S1), :] + rc[...]

    ds = [send(a1.at[rows(p * S2, S2)], ry.at[y], o_y + k, o_y + y, dev(c, p, x, z))
          for k, p in enumerate(y_peers)]
    for k in range(1, Y):
        s = (y - k + Y) % Y
        wait_recv(a1.at[rows(0, S2)], ry.at[s], o_y + s, dev(c, s, x, z))
    acc = a1[rows(y * S2, S2), :]
    for k in range(1, Y):
        acc = acc + ry[(y - k + Y) % Y]
    a2[...] = acc

    ds = [send(a2.at[rows(p * S3, S3)], rx.at[x], o_x + k, o_x + x, dev(c, y, p, z))
          for k, p in enumerate(x_peers)]
    for k in range(1, X):
        s = (x - k + X) % X
        wait_recv(a2.at[rows(0, S3)], rx.at[s], o_x + s, dev(c, y, s, z))
    acc = a2[rows(x * S3, S3), :]
    for k in range(1, X):
        acc = acc + rx[(x - k + X) % X]
    a3[...] = acc

    d = send(a3.at[rows((1 - zl) * S4, S4)], rzl, o_zl, o_zl, zl_peer)
    wait_recv(a3.at[rows(zl * S4, S4)], rzl, o_zl, zl_peer)
    a4[...] = a3[rows(zl * S4, S4), :] + rzl[...]

    ds = [send(a4, rzh.at[zh], o_zh + k, o_zh + zh, dev(c, y, x, p * 2 + zl))
          for k, p in enumerate(zh_peers)]
    rzh[zh] = a4[...]
    for k in range(1, ZH):
        s = (zh - k + ZH) % ZH
        wait_recv(a4, rzh.at[s], o_zh + s, dev(c, y, x, s * 2 + zl))
    acc = rzh[0]
    for j in range(1, ZH):
        acc = acc + rzh[j]
    base = c * S1 + y * S2 + x * S3
    full[rows(base + zl * S4, S4), :] = acc

    mine = rows(base + zl * S4, S4)
    d = send(full.at[mine], full.at[mine], o_agzl, o_agzl, zl_peer)
    wait_recv(full.at[mine], full.at[rows(base + (1 - zl) * S4, S4)], o_agzl, zl_peer)

    mine = rows(c * S1 + y * S2 + x * S3, S3)
    ds = [send(full.at[mine], full.at[mine], o_agx + k, o_agx + x, dev(c, y, p, z))
          for k, p in enumerate(x_peers)]
    for k in range(1, X):
        s = (x - k + X) % X
        wait_recv(full.at[mine], full.at[rows(c * S1 + y * S2 + s * S3, S3)], o_agx + s, dev(c, y, s, z))

    mine = rows(c * S1 + y * S2, S2)
    ds = [send(full.at[mine], full.at[mine], o_agy + k, o_agy + y, dev(c, p, x, z))
          for k, p in enumerate(y_peers)]
    for k in range(1, Y):
        s = (y - k + Y) % Y
        wait_recv(full.at[mine], full.at[rows(c * S1 + s * S2, S2)], o_agy + s, dev(c, s, x, z))

    mine = rows(c * S1, S1)
    d = send(full.at[mine], full.at[mine], o_agc, o_agc, core_peer)
    wait_recv(full.at[mine], full.at[rows((1 - c) * S1, S1)], o_agc, core_peer)

    for d in pending:
        d.wait_send()
    if out_ref is not None:
        out_ref[...] = full[...]


def _zone_gather_kernel(nb, p_ref, out_ref, ssem, rsem, lsem):
    T = p_ref.shape[0]
    r = lax.axis_index("rows")
    b = lax.axis_index("blk")
    barrier = pltpu.get_barrier_semaphore()
    for k in range(1, nb):
        pl.semaphore_signal(barrier, inc=1, device_id=(r, (b + k) % nb), device_id_type=MESH_ID)
    pl.semaphore_wait(barrier, nb - 1)
    here = pl.ds(pl.multiple_of(b * T, 8), T)
    ds = []
    for k in range(1, nb):
        d = pltpu.make_async_remote_copy(
            src_ref=p_ref, dst_ref=out_ref.at[here], send_sem=ssem.at[k - 1], recv_sem=rsem.at[b],
            device_id=(r, (b + k) % nb), device_id_type=MESH_ID)
        d.start()
        ds.append(d)
    own = pltpu.make_async_copy(p_ref, out_ref.at[here], lsem.at[0])
    own.start()
    for k in range(1, nb):
        s = (b - k + nb) % nb
        pltpu.make_async_remote_copy(
            src_ref=p_ref, dst_ref=out_ref.at[pl.ds(pl.multiple_of(s * T, 8), T)], send_sem=ssem.at[0],
            recv_sem=rsem.at[s], device_id=(r, s), device_id_type=MESH_ID).wait_recv()
    for d in ds:
        d.wait_send()
    own.wait()


def zone_gather(p, nb):
    T, K = p.shape
    return pl.pallas_call(
        functools.partial(_zone_gather_kernel, nb),
        out_shape=jax.ShapeDtypeStruct((nb * T, K), p.dtype),
        in_specs=[pl.BlockSpec(memory_space=pl.ANY)],
        out_specs=pl.BlockSpec(memory_space=pl.ANY),
        scratch_shapes=[
            pltpu.SemaphoreType.DMA((nb - 1,)),
            pltpu.SemaphoreType.DMA((nb,)),
            pltpu.SemaphoreType.DMA((1,)),
        ],
        compiler_params=pltpu.CompilerParams(collective_id=1, has_side_effects=True),
    )(p)


HI = lax.Precision.HIGHEST


def _mm(a, b):
    return jnp.dot(a, b, precision=HI, preferred_element_type=jnp.float32)


def _mm_t(a, b):
    return lax.dot_general(a, b, (((1,), (1,)), ((), ())), precision=HI, preferred_element_type=jnp.float32)


def _chol_inv_kernel(count, g_ref, m_ref, a_ref, d_ref, b_ref, l_ref):
    n = g_ref.shape[0]
    t = d_ref.shape[0]
    nb = n // t
    gram = g_ref[...] / count
    a_ref[...] = (gram + gram.T) / 2
    m_ref[...] = jnp.zeros_like(m_ref)
    lane = lax.broadcasted_iota(jnp.int32, (1, t), 1)
    eye = (lax.broadcasted_iota(jnp.int32, (t, t), 0) == lax.broadcasted_iota(jnp.int32, (t, t), 1)).astype(jnp.float32)

    for k in range(nb):
        lo = k * t
        d_ref[...] = a_ref[lo:lo + t, lo:lo + t]
        b_ref[...] = eye
        for r0 in range(0, t, 8):
            sub = lax.broadcasted_iota(jnp.int32, (t - r0, 1), 0) + r0
            dl = d_ref[r0:, :]
            bl = b_ref[r0:, :]
            for i in range(8):
                j = r0 + i
                inv = lax.rsqrt(dl[i:i + 1, j:j + 1])
                col = jnp.where(sub >= j, dl[:, j:j + 1] * inv, 0.0)
                lrow = jnp.where(lane >= j, dl[i:i + 1, :] * inv, 0.0)
                dl = dl - col * lrow
                brow = bl[i:i + 1, :] * inv
                bl = jnp.where(sub == j, brow, bl - jnp.where(sub > j, col, 0.0) * brow)
            d_ref[r0:, :] = dl
            b_ref[r0:, :] = bl
        m_ref[lo:lo + t, lo:lo + t] = b_ref[...]
        if k < nb - 1:
            hi = lo + t
            panel = _mm_t(a_ref[hi:, lo:lo + t], b_ref[...])
            l_ref[hi:, lo:lo + t] = panel
            a_ref[hi:, hi:] = a_ref[hi:, hi:] - _mm_t(panel, panel)
    for dist in range(1, nb):
        for i in range(dist, nb):
            j = i - dist
            acc = None
            for k in range(j, i):
                term = _mm(l_ref[i * t:(i + 1) * t, k * t:(k + 1) * t], m_ref[k * t:(k + 1) * t, j * t:(j + 1) * t])
                acc = term if acc is None else acc + term
            m_ref[i * t:(i + 1) * t, j * t:(j + 1) * t] = -_mm(m_ref[i * t:(i + 1) * t, i * t:(i + 1) * t], acc)


def orthonormal_basis(images, dims, count, t=128):
    XL, Z, C, XH, Y = dims
    X = XL * XH
    ZH = Z // 2
    N = M = images.shape[1]
    S1 = N // C
    S2 = S1 // Y
    S3 = S2 // X
    S4 = S3 // 2
    nsem = 4 + 2 * Y + 2 * X + ZH
    vmem = pltpu.VMEM

    def kernel(x_ref, out_ref, rc, ry, rx, rzl, rzh, a1, a2, a3, a4, full, ssem, rsem, ca, cd, cb, cl, gsc, msc):
        def local_gram():
            x = x_ref[...]
            gsc[...] = jnp.dot(x.T, x, precision=HI, preferred_element_type=jnp.float32)

        _ar_kernel(dims, gsc, None, rc, ry, rx, rzl, rzh, a1, a2, a3, a4, full, ssem, rsem, local_gram)
        _chol_inv_kernel(count, full, msc, ca, cd, cb, cl)
        out_ref[...] = _mm_t(x_ref[...], msc[...])

    return pl.pallas_call(
        kernel,
        out_shape=jax.ShapeDtypeStruct(images.shape, jnp.float32),
        in_specs=[pl.BlockSpec(memory_space=vmem)],
        out_specs=pl.BlockSpec(memory_space=vmem),
        scratch_shapes=[
            vmem((S1, M), jnp.float32),
            vmem((Y, S2, M), jnp.float32),
            vmem((X, S3, M), jnp.float32),
            vmem((S4, M), jnp.float32),
            vmem((ZH, S4, M), jnp.float32),
            vmem((S1, M), jnp.float32),
            vmem((S2, M), jnp.float32),
            vmem((S3, M), jnp.float32),
            vmem((S4, M), jnp.float32),
            vmem((N, M), jnp.float32),
            pltpu.SemaphoreType.DMA((nsem,)),
            pltpu.SemaphoreType.DMA((nsem,)),
            vmem((N, N), jnp.float32),
            vmem((t, t), jnp.float32),
            vmem((t, t), jnp.float32),
            vmem((N, N), jnp.float32),
            vmem((N, N), jnp.float32),
            vmem((N, N), jnp.float32),
        ],
        compiler_params=pltpu.CompilerParams(collective_id=0, has_side_effects=True),
    )(images)


def extended(x, sides, width):
    for axis, dim in sides:
        devices, length = (lax.axis_size(axis), x.shape[dim])
        up = [(i, (i + 1) % devices) for i in range(devices - 1)]
        down = [(j, i) for i, j in up]
        last = lax.slice_in_dim(x, length - width, length, axis=dim)
        first = lax.slice_in_dim(x, 0, width, axis=dim)
        before = lax.ppermute(last, axis, up)
        after = lax.ppermute(first, axis, down)
        x = jnp.concatenate([before, x, after], axis=dim)
    return x


def _dims():
    rows, blk = lax.axis_size("rows"), lax.axis_size("blk")
    return (2, rows // 4, 2, 2, blk // 2)


def local(cov_blocks, col_index, block_count, probes):
    rows_here, slots, block, _ = cov_blocks.shape
    tile_rows = probes.shape[0]
    probe_cols = probes.shape[1]
    zone_blocks = rows_here * lax.axis_size("blk")
    zone_number = lax.axis_index("rows")
    relative = col_index - (zone_number - 1) * zone_blocks
    window_blocks = 3 * zone_blocks
    inside = (relative >= 0) & (relative < window_blocks)
    slot_ids = lax.broadcasted_iota(jnp.int32, (rows_here, slots), 1)
    live_mask = inside & (slot_ids < block_count[:, None])
    column_ids = jnp.arange(window_blocks, dtype=jnp.int32)
    hits = (relative[:, :, None] == column_ids[None, None, :]) & live_mask[:, :, None]
    selector = hits.astype(jnp.bfloat16)
    window_matrix = jnp.einsum(
        "lsp,lsac->lapc", selector, cov_blocks, preferred_element_type=jnp.float32
    )
    window_matrix = window_matrix.astype(jnp.bfloat16).reshape(
        rows_here * block, window_blocks * block
    )

    def add_columns(running, shard_rows, first_row):
        length = shard_rows.shape[0]
        columns = lax.dynamic_slice_in_dim(window_matrix, first_row, length, 1)
        return running + jnp.dot(columns, shard_rows, preferred_element_type=jnp.float32)

    zeros_out = jnp.zeros((tile_rows, probe_cols), jnp.float32)
    own_zone = zone_gather(probes, lax.axis_size("blk"))
    zone_length = own_zone.shape[0]
    images = add_columns(zeros_out, own_zone, zone_length)
    near_zones = extended(own_zone, (("rows", 0),), zone_length)
    images = add_columns(images, lax.slice_in_dim(near_zones, 0, zone_length, axis=0), 0)
    images = add_columns(
        images,
        lax.slice_in_dim(near_zones, 2 * zone_length, 3 * zone_length, axis=0),
        2 * zone_length,
    )
    point_count = tile_rows * lax.axis_size("rows") * lax.axis_size("blk")
    return orthonormal_basis(images, _dims(), float(point_count))


def solution(mesh):
    return jax.shard_map(
        local,
        mesh=mesh,
        in_specs=(
            P(("rows", "blk"), None, None, None),
            P(("rows", "blk"), None),
            P(("rows", "blk")),
            P(("rows", "blk"), None),
        ),
        out_specs=P(("rows", "blk"), None),
        check_vma=False,
    )
```
